256 devices in a mesh: tm: 8 (over x, z_hi), space: 32 (over z_lo, y, core).
Axes of the slice: x: 4, y: 4, z: 8 (z_hi: 2, z_lo: 4; z = z_hi * 4 + z_lo), core: 2. Of those that a mesh axis runs over, the one named last changes fastest.
Arguments:
- orbitals: bfloat16 [13824, 320], P('space'), may hold values from -6 to 6
- gaps: float32 [320], replicated, may hold values from 0.005 to 50
- times: float32 [8], P('tm'), may hold values from 0.01 to 100, as said below
- cos_weights: float32 [8, 8], replicated, may hold values from -1 to 1
Outputs:
- polarizability: float32 [8, 864, 864], P('tm', 'space')
The draws below stay inside these ranges and needn't reach their ends.
Inputs may be any that keep to these rules, and one draw needn't show every extreme that they name: times rise with their index.
All inputs are finite; a program needn't handle non-finite values.
Results may differ from the reference program's by a relative error of at most 0.0044.
Values may be sent and summed in bfloat16 or wider, within the bound.
A program may use at most 192 MiB of HBM per device.

```python
import math
import jax
import jax.numpy as jnp
from jax import lax

SIDE = 24
NG = 864
NOCC = 64
NEMP = 256
R = 13824
NORB = 320
NT = 8
NW = 8


def draw_gaps(key, part):
    level = jax.random.uniform(key, (NORB,), jnp.float32, 0.0, 1.0)
    return 0.005 * jnp.exp(level * level * math.log(10000.0))


def draw_times(key, part):
    position = jnp.arange(NT, dtype=jnp.float32)
    jitter = jax.random.uniform(key, (NT,), jnp.float32, 0.3, 0.7)
    return 0.01 * jnp.exp((position + jitter) / NT * math.log(10000.0))


def draw_cos_weights(key, part):
    phase_key, size_key = jax.random.split(jax.random.fold_in(key, 17))
    frequency = jnp.arange(NW, dtype=jnp.float32)[:, None]
    moment_index = jnp.arange(NT, dtype=jnp.float32)[None, :]
    phase = jax.random.uniform(phase_key, (NW, 1), jnp.float32, -math.pi, math.pi)
    amplitude = jax.random.uniform(size_key, (NW, NT), jnp.float32, 0.5, 1.0)
    ramp = 0.5 + 0.5 * (moment_index + 1.0) / NT
    angle = math.pi * (frequency + 0.5) * (moment_index + 0.5) / NT + phase
    return amplitude * ramp * jnp.cos(angle)


def steps_of(own_key, dims, cuts, smallest, top_value):
    level = 1.0
    for dim, blocks in cuts:
        draws = jax.random.uniform(jax.random.fold_in(jax.random.fold_in(own_key, 6), dim), (blocks,), jnp.float32, smallest / len(cuts), top_value / len(cuts))
        level = level * jnp.repeat(jnp.exp(draws), dims[dim] // blocks).reshape((-1,) + (1,) * (len(dims) - 1 - dim))
    return level


def noise(rng, shape, width, reach, cuts=(), kind=jnp.bfloat16):
    loudness = steps_of(rng, shape, cuts, -0.22, 0.18) if cuts else 1.0
    result = jax.random.normal(rng, shape, jnp.float32) * width * loudness
    return jnp.minimum(jnp.maximum(result, -reach), reach).astype(kind)


def setup_inputs(seed: int = 0) -> dict:
    splits = jax.random.split(jax.random.key(seed), 5)
    orbitals = noise(splits[0], (R, NORB), 1.0, 6.0, ((0, 32),))
    gaps = draw_gaps(jax.random.fold_in(splits[4], 71), 0)
    times = draw_times(jax.random.fold_in(splits[4], 71), 0)
    cos_weights = draw_cos_weights(jax.random.fold_in(splits[4], 71), 0)
    return dict(orbitals=orbitals, gaps=gaps, times=times, cos_weights=cos_weights)


def plane_table(grid_side, mode_count):
    side_index = jnp.arange(grid_side, dtype=jnp.int32)
    wave_index = jnp.arange(mode_count // 2, dtype=jnp.int32)
    span_first = grid_side // 2
    span_second = grid_side // 4
    wave_first = wave_index % span_first - span_first // 2
    wave_second = wave_index // span_first % span_second - span_second // 2
    wave_third = wave_index // (span_first * span_second) + 1

    def factor(wave_vector):
        step_counts = jnp.mod(wave_vector[:, None] * side_index[None, :], grid_side)
        angles = step_counts.astype(jnp.float32) * (2.0 * math.pi / grid_side)
        return (jnp.cos(angles), jnp.sin(angles))
    cos_first, sin_first = factor(wave_first)
    cos_second, sin_second = factor(wave_second)
    cos_third, sin_third = factor(wave_third)
    cos_first = cos_first[:, :, None, None]
    sin_first = sin_first[:, :, None, None]
    cos_second = cos_second[:, None, :, None]
    sin_second = sin_second[:, None, :, None]
    cos_third = cos_third[:, None, None, :]
    sin_third = sin_third[:, None, None, :]
    inner_cos = cos_second * cos_third - sin_second * sin_third
    inner_sin = sin_second * cos_third + cos_second * sin_third
    cos_whole = cos_first * inner_cos - sin_first * inner_sin
    sin_whole = sin_first * inner_cos + cos_first * inner_sin
    half_count = mode_count // 2
    scaling = math.sqrt(2.0 / grid_side ** 3)
    joined = jnp.concatenate([cos_whole.reshape(half_count, -1), sin_whole.reshape(half_count, -1)], axis=0)
    return (joined * scaling).astype(jnp.bfloat16)

def reference(orbitals, gaps, times, cos_weights):
    block = SIDE * SIDE
    blocks = R // block
    column_scale = jnp.concatenate([jnp.full((NOCC,), NOCC ** (-0.5), jnp.float32), jnp.full((NEMP,), NEMP ** (-0.5), jnp.float32)])
    table = plane_table(SIDE, NG)

    def one_time(tau_value):
        factors = jnp.exp(-gaps * tau_value) * column_scale
        weighted = (orbitals.astype(jnp.float32) * factors[None, :]).astype(jnp.bfloat16)

        def first_pass(carry, block_index):
            row_start = (block_index * block).astype(jnp.int32)
            row_block = lax.dynamic_slice_in_dim(orbitals, row_start, block, 0)
            green_occ = jnp.dot(row_block[:, :NOCC], weighted[:, :NOCC].T, preferred_element_type=jnp.float32)
            green_emp = jnp.dot(row_block[:, NOCC:], weighted[:, NOCC:].T, preferred_element_type=jnp.float32)
            chi_block = (green_occ * green_emp).astype(jnp.bfloat16)
            table_block = lax.dynamic_slice_in_dim(table, row_start, block, 1)
            return (carry + jnp.dot(table_block, chi_block, preferred_element_type=jnp.float32), None)
        half, _ = lax.scan(first_pass, jnp.zeros((NG, R), jnp.float32), jnp.arange(blocks, dtype=jnp.int32))
        half = half.astype(jnp.bfloat16)
        return jnp.dot(half, table.T, preferred_element_type=jnp.float32)
    moments = lax.map(one_time, times)
    return jnp.einsum('wt,tgh->wgh', cos_weights, moments, precision=lax.Precision.HIGHEST)
```

```python
import math

import jax
import jax.numpy as jnp
import numpy as np
from jax import lax
from jax.experimental import pallas as pl
from jax.experimental.pallas import tpu as pltpu
from jax.sharding import PartitionSpec as P

SIDE = 24
NG = 864
NOCC = 64
NEMP = 256
MESH = pl.DeviceIdType.MESH
F32 = jnp.float32
BF16 = jnp.bfloat16


def wave_tables():
    pos = np.arange(1024)
    cls, m = pos // 256, pos % 256
    pa, pc = cls >> 1, cls & 1
    trig, ci, bi, ai = m // 108, m // 36 % 3, m // 6 % 6, m % 6
    a, b, c = 2 * ai + pa - 6, bi - 3, 1 + 2 * ci + pc
    valid = m < 216
    natural = np.where(valid, (a + 6) + 12 * (b + 3) + 72 * (c - 1) + 432 * trig, -1)

    def factor(side, wave):
        step = np.mod(side[:, None] * wave[None, :], SIDE)
        angle = step * (2.0 * math.pi / SIDE)
        return np.cos(angle), np.sin(angle)

    x_cos, x_sin = factor(np.arange(16), a)
    y_cos, y_sin = factor(np.arange(24), b)
    y_first = np.where(trig == 0, y_cos, y_sin)
    y_second = np.where(trig == 0, y_sin, -y_cos)
    z_rows = np.concatenate([np.arange(8), np.tile(np.arange(8, 12), 2)])
    z_cos, z_sin = factor(z_rows, c)
    scaling = math.sqrt(2.0 / SIDE**3) * valid
    factors = np.concatenate(
        [x_cos, x_sin, y_first, y_second, z_cos * scaling, z_sin * scaling], axis=0
    ).astype(np.float32)

    where_natural = np.full(1024, -1, np.int32)
    where_natural[natural[valid]] = pos[valid]
    lane = np.arange(1024)
    block, core, low, row = lane // 256, lane // 128 % 2, lane // 32 % 4, lane % 32
    g = 27 * (low * 8 + block * 2 + core) + row
    where_g = np.where(row < 27, where_natural[np.minimum(g, NG - 1)], -1)
    columns = np.stack([where_g, where_natural]).astype(np.int32)

    k = np.arange(256)
    tail = k - 144
    u = np.where(k < 144, k // 8, tail // 8 * 2 + tail % 8 // 4)
    z = np.where(k < 144, k % 8, 8 + tail % 4)
    inside = k < 216
    first = np.where(inside, u * 24 + z, -1)
    second = np.where(inside, u * 24 + 12 + z, -1)
    points = np.concatenate([first, second])[None, :].astype(np.int32)
    return factors, columns, points


FX, FXS, FY, FYS, FZ, FZS = 0, 16, 32, 56, 80, 96


def kernel(
    orb_ref, gaps_ref, times_ref, cw_ref, fac_ref, col_ref, pts_ref, out_ref,
    orb_p, recv, t_own, t_all, lead, quad, table, sel, acc, m_g, m_h, g_all, h_all,
    g_t, dmat, p_buf, keep, c_send, c_recv, q_buf, r_buf,
    a_recv, a_send, t_recv, t_send, g_recv, g_send, h_recv, h_send, l_sem, x_recv, x_send, r_recv, r_send,
):
    tm = lax.axis_index("tm")
    sp = lax.axis_index("space")
    x, zh = tm // 2, tm % 2
    zl, y, core = sp // 8, sp // 2 % 4, sp % 2
    z = zh * 4 + zl

    def device(xx, yy, zz, cc):
        return (xx * 2 + zz // 4, (zz % 4) * 8 + yy * 2 + cc)

    def remote(src, dst, send, recv_sem, target):
        return pltpu.make_async_remote_copy(
            src_ref=src, dst_ref=dst, send_sem=send, recv_sem=recv_sem,
            device_id=target, device_id_type=MESH,
        )

    t_own[...] = jnp.full((8, 128), times_ref[0], F32)
    pick = lax.broadcasted_iota(jnp.int32, (432, 512), 0) == pts_ref[...]
    pick = jnp.where(pick, 1.0, 0.0).astype(BF16)
    moved = jnp.dot(orb_ref[...], pick, preferred_element_type=F32).astype(BF16)
    for n in range(40):
        orb_p[n] = moved[n * 8 : (n + 1) * 8, :]

    for dz, cc in ((2, 0), (-2, 1), (1, 0), (1, 1), (-1, 0), (-1, 1), (0, 0), (0, 1)):
        zz = (z + dz + 8) % 8
        for dy in (2, 1, 3, 0):
            yy = (y + dy) % 4
            blocks = (4 * cc + x, 8 + 4 * zz + yy)
            for part, block in enumerate(blocks):
                src, dst = orb_p.at[block], recv.at[sp, part]
                copy = remote(src, dst, a_send, a_recv, device(x, yy, zz, cc))
                if dz == 0 and dy == 0:
                    local = pltpu.make_async_copy(src, dst, a_recv)
                    pl.when(core == cc)(local.start)
                    pl.when(core != cc)(copy.start)
                else:
                    copy.start()
    for step in range(1, 8):
        remote(t_own, t_all.at[tm], t_send, t_recv, ((tm + step) % 8, sp)).start()
    t_all[tm] = t_own[...]

    def lead_rows(xx, carry):
        cos = fac_ref[pl.ds(FX + xx, 1), :]
        sin = fac_ref[pl.ds(FXS + xx, 1), :]
        first, second = fac_ref[FY : FY + 24, :], fac_ref[FYS : FYS + 24, :]
        rows = pl.ds(pl.multiple_of(xx * 24, 8), 24)
        lead[rows, :] = cos * first - sin * second
        quad[rows, :] = sin * first + cos * second
        return carry

    lax.fori_loop(0, 12, lead_rows, 0)
    odd = lax.broadcasted_iota(jnp.int32, (8, 1024), 0) >= 4

    def table_rows(chunk, carry):
        base = chunk * 18

        def pair(v, inner):
            row = base + 2 * v
            a0, a1 = lead[pl.ds(row, 1), :], lead[pl.ds(row + 1, 1), :]
            b0, b1 = quad[pl.ds(row, 1), :], quad[pl.ds(row + 1, 1), :]
            cos, sin = fac_ref[FZ : FZ + 8, :], fac_ref[FZS : FZS + 8, :]
            both = jnp.concatenate([a0 * cos - b0 * sin, a1 * cos - b1 * sin], axis=0)
            table[chunk, pl.ds(pl.multiple_of(v * 16, 16), 16), :] = both.astype(BF16)
            return inner

        lax.fori_loop(0, 9, pair, 0)

        def tail(v):
            row = base + 2 * v
            a = jnp.where(odd, lead[pl.ds(row + 1, 1), :], lead[pl.ds(row, 1), :])
            b = jnp.where(odd, quad[pl.ds(row + 1, 1), :], quad[pl.ds(row, 1), :])
            return a * fac_ref[FZ + 8 : FZ + 16, :] - b * fac_ref[FZS + 8 : FZS + 16, :]

        def tails(w, inner):
            both = jnp.concatenate([tail(2 * w), tail(jnp.minimum(2 * w + 1, 8))], axis=0)
            table[chunk, pl.ds(pl.multiple_of(144 + w * 16, 16), 16), :] = both.astype(BF16)
            return inner

        lax.fori_loop(0, 5, tails, 0)
        table[chunk, 224:256, :] = jnp.zeros((32, 1024), BF16)
        return carry

    lax.fori_loop(0, 16, table_rows, 0)

    def select_rows(n, carry):
        rows = lax.broadcasted_iota(jnp.int32, (128, 1024), 0) + n * 128
        for side in range(2):
            hit = rows == col_ref[side : side + 1, :]
            sel[side, pl.ds(pl.multiple_of(n * 128, 128), 128), :] = jnp.where(hit, 1.0, 0.0).astype(BF16)
        return carry

    lax.fori_loop(0, 8, select_rows, 0)

    pltpu.make_async_copy(t_all.at[pl.ds(0, 7)], t_all.at[pl.ds(0, 7)], t_recv).wait()
    sub = lax.broadcasted_iota(jnp.int32, (8, 128), 0)
    tcol = jnp.zeros((8, 128), F32)
    for n in range(8):
        tcol = jnp.where(sub == n, t_all[n], tcol)
    tcol = tcol[:, 0:1]
    pair_index = lax.broadcasted_iota(jnp.int32, (1, 1024), 1)
    which_i = 32 * core + 8 * (pair_index // 256) + pair_index // 8 % 8
    which_a = NOCC + 32 * z + 8 * (pair_index // 64 % 4) + pair_index % 8
    orbital = lax.broadcasted_iota(jnp.int32, (320, 1024), 0)
    hot_i = jnp.where(orbital == which_i, 1.0, 0.0).astype(F32)
    hot_a = jnp.where(orbital == which_a, 1.0, 0.0).astype(F32)
    gaps = jnp.broadcast_to(gaps_ref[...], (8, 320))
    high = lax.Precision.HIGHEST
    gap_i = jnp.dot(gaps, hot_i, precision=high, preferred_element_type=F32)
    gap_a = jnp.dot(gaps, hot_a, precision=high, preferred_element_type=F32)
    decay = jnp.exp(-gap_i * tcol) * jnp.exp(-gap_a * tcol) * (NOCC**-0.5 * NEMP**-0.5)
    dmat[...] = jnp.dot(cw_ref[...], decay, precision=high, preferred_element_type=F32)

    acc[...] = jnp.zeros_like(acc)
    pltpu.make_async_copy(recv, recv, a_recv).wait()

    def chunk_step(n, carry):
        i0, e0 = recv[n, 0].astype(F32), recv[n, 1].astype(F32)
        i1, e1 = recv[n + 16, 0].astype(F32), recv[n + 16, 1].astype(F32)
        parts = ([], [], [], [])
        for i in range(8):
            p0, p1 = i0[i : i + 1, :] * e0, i1[i : i + 1, :] * e1
            s, d = p0 + p1, p0 - p1
            parts[0].append(s[:, :256] - s[:, 256:])
            parts[1].append(s[:, :256] + s[:, 256:])
            parts[2].append(d[:, :256] - d[:, 256:])
            parts[3].append(d[:, :256] + d[:, 256:])
        for cls in range(4):
            left = jnp.concatenate(parts[cls], axis=0).astype(BF16)
            lanes = slice(cls * 256, (cls + 1) * 256)
            acc[:, lanes] += jnp.dot(left, table[n, :, lanes], preferred_element_type=F32)
        return carry

    lax.fori_loop(0, 16, chunk_step, 0)
    m_all = acc[...].astype(BF16)
    for n in range(4):
        lanes = slice(n * 256, (n + 1) * 256)
        m_g[n] = jnp.dot(m_all, sel[0, :, lanes], preferred_element_type=F32).astype(BF16)
        m_h[n] = jnp.dot(m_all, sel[1, :, lanes], preferred_element_type=F32).astype(BF16)

    own = x * 4 + y
    for d in (2, 1, 3):
        xx, yy = (x + d) % 4, (y + d) % 4
        remote(m_g.at[xx], g_all.at[own], g_send.at[d], g_recv.at[own], device(xx, y, z, core)).start()
        remote(m_h.at[yy], h_all.at[own], h_send.at[d], h_recv.at[own], device(x, yy, z, core)).start()
    local_g = pltpu.make_async_copy(m_g.at[x], g_all.at[own], g_recv.at[own])
    local_h = pltpu.make_async_copy(m_h.at[y], h_all.at[own], h_recv.at[own])
    local_g.start()
    local_h.start()

    def arrived(buf, sem, slot):
        pltpu.make_async_copy(buf.at[slot], buf.at[slot], sem.at[slot]).wait()

    def pass_g(slot, dy, send):
        remote(g_all.at[slot], g_all.at[slot], g_send.at[send], g_recv.at[slot],
               device(x, (y + dy) % 4, z, core)).start()

    def pass_h(slot, dx, send):
        remote(h_all.at[slot], h_all.at[slot], h_send.at[send], h_recv.at[slot],
               device((x + dx) % 4, y, z, core)).start()

    order = (0, 1, 3, 2)
    for n, d in enumerate(order):
        slot_g, slot_h = (x + d) % 4 * 4 + y, x * 4 + (y + d) % 4
        arrived(g_all, g_recv, slot_g)
        pass_g(slot_g, 1, 4 + 2 * n)
        pass_g(slot_g, 3, 5 + 2 * n)
        arrived(h_all, h_recv, slot_h)
        pass_h(slot_h, 1, 4 + 2 * n)
        pass_h(slot_h, 3, 5 + 2 * n)
    for n, d in enumerate(order):
        up_g, up_h = (x + d) % 4 * 4 + (y + 3) % 4, (x + 3) % 4 * 4 + (y + d) % 4
        down_g, down_h = (x + d) % 4 * 4 + (y + 1) % 4, (x + 1) % 4 * 4 + (y + d) % 4
        arrived(g_all, g_recv, up_g)
        pl.when((x + d) % 4 < 2)(lambda s=up_g, k=12 + n: pass_g(s, 1, k))
        arrived(g_all, g_recv, down_g)
        pl.when((x + d) % 4 >= 2)(lambda s=down_g, k=12 + n: pass_g(s, 3, k))
        arrived(h_all, h_recv, up_h)
        pl.when((y + d) % 4 < 2)(lambda s=up_h, k=12 + n: pass_h(s, 1, k))
        arrived(h_all, h_recv, down_h)
        pl.when((y + d) % 4 >= 2)(lambda s=down_h, k=12 + n: pass_h(s, 3, k))
    for d in range(4):
        arrived(g_all, g_recv, d * 4 + (y + 2) % 4)
        arrived(h_all, h_recv, (x + 2) % 4 * 4 + d)

    for n in range(8):
        rows = slice(n * 128, (n + 1) * 128)
        block = jnp.concatenate([g_all[2 * n], g_all[2 * n + 1]], axis=0).astype(F32)
        g_t[:, rows] = block.T
    sibling = device(x, y, z, 1 - core)
    mine = pl.ds(pl.multiple_of(core * 128, 128), 128)
    other = pl.ds(pl.multiple_of((1 - core) * 128, 128), 128)

    def frequency(w, carry):
        total = jnp.zeros((256, 256), F32)
        for n in range(4):
            lanes = slice(n * 256, (n + 1) * 256)
            left = (g_t[:, lanes] * dmat[pl.ds(w, 1), lanes]).astype(BF16)
            right = h_all[4 * n : 4 * n + 4].reshape(256, 256)
            total += jnp.dot(left, right, preferred_element_type=F32)
        p_buf[...] = total
        keep[w] = p_buf[mine, :]
        c_send[w] = p_buf[other, :].astype(BF16)
        remote(c_send.at[w], c_recv.at[w], x_send.at[w], x_recv.at[w], sibling).start()
        return carry

    lax.fori_loop(0, 8, frequency, 0)

    slot = z * 4 + y

    def deliver(w, carry):
        pltpu.make_async_copy(c_recv.at[w], c_recv.at[w], x_recv.at[w]).wait()
        total = (keep[w] + c_recv[w].astype(F32)).astype(BF16)
        for low in range(4):
            q_buf[w * 4 + low] = total[low * 32 : (low + 1) * 32, :]
        for low in range(4):
            src = q_buf.at[w * 4 + low]
            target = low * 8 + x * 2 + core
            copy = remote(src, r_buf.at[slot], r_send, r_recv, (w, target))
            local = pltpu.make_async_copy(src, r_buf.at[slot], r_recv)
            here = jnp.logical_and(w == tm, target == sp)
            pl.when(here)(local.start)
            pl.when(jnp.logical_not(here))(copy.start)
        return carry

    lax.fori_loop(0, 8, deliver, 0)
    pltpu.make_async_copy(r_buf, r_buf, r_recv).wait()
    for n in range(4):
        total = r_buf[n].astype(F32)
        for m in range(1, 8):
            total += r_buf[m * 4 + n].astype(F32)
        width = 256 if n < 3 else 96
        out_ref[:, n * 256 : n * 256 + width] = total[:27, :width]

    away = jnp.where(jnp.logical_and(x == y, True), 1, 0)
    pltpu.make_async_copy(recv.at[pl.ds(0, 31)], recv.at[pl.ds(0, 31)], a_send).wait()
    pltpu.make_async_copy(t_all.at[pl.ds(0, 7)], t_all.at[pl.ds(0, 7)], t_send).wait()
    for n in range(1, 16):
        pltpu.make_async_copy(m_g.at[0], m_g.at[0], g_send.at[n]).wait()
        pltpu.make_async_copy(m_h.at[0], m_h.at[0], h_send.at[n]).wait()
    for n in range(8):
        pltpu.make_async_copy(c_send.at[n], c_send.at[n], x_send.at[n]).wait()
    short = pltpu.make_async_copy(q_buf.at[pl.ds(0, 31)], q_buf.at[pl.ds(0, 31)], r_send)
    whole = pltpu.make_async_copy(q_buf, q_buf, r_send)
    pl.when(away == 1)(short.wait)
    pl.when(away == 0)(whole.wait)


def local(orbitals, gaps, times, cos_weights):
    factors, columns, points = wave_tables()
    vmem = pl.BlockSpec(memory_space=pltpu.VMEM)
    smem = pl.BlockSpec(memory_space=pltpu.SMEM)
    dma = pltpu.SemaphoreType.DMA
    out = pl.pallas_call(
        kernel,
        out_shape=jax.ShapeDtypeStruct((27, NG), F32),
        in_specs=[vmem, vmem, smem, vmem, vmem, vmem, vmem],
        out_specs=vmem,
        scratch_shapes=[
            pltpu.VMEM((40, 8, 512), BF16),
            pltpu.VMEM((32, 2, 8, 512), BF16),
            pltpu.VMEM((8, 128), F32),
            pltpu.VMEM((8, 8, 128), F32),
            pltpu.VMEM((288, 1024), F32),
            pltpu.VMEM((288, 1024), F32),
            pltpu.VMEM((16, 256, 1024), BF16),
            pltpu.VMEM((2, 1024, 1024), BF16),
            pltpu.VMEM((64, 1024), F32),
            pltpu.VMEM((4, 64, 256), BF16),
            pltpu.VMEM((4, 64, 256), BF16),
            pltpu.VMEM((16, 64, 256), BF16),
            pltpu.VMEM((16, 64, 256), BF16),
            pltpu.VMEM((256, 1024), F32),
            pltpu.VMEM((8, 1024), F32),
            pltpu.VMEM((256, 256), F32),
            pltpu.VMEM((8, 128, 256), F32),
            pltpu.VMEM((8, 128, 256), BF16),
            pltpu.VMEM((8, 128, 256), BF16),
            pltpu.VMEM((32, 32, 256), BF16),
            pltpu.VMEM((32, 32, 256), BF16),
            dma, dma, dma, dma,
            dma((16,)), dma((16,)), dma((16,)), dma((16,)),
            dma,
            dma((8,)), dma((8,)),
            dma, dma,
        ],
        compiler_params=pltpu.CompilerParams(has_side_effects=True),
    )(
        orbitals.T, gaps[None, :], times, cos_weights,
        jnp.asarray(factors), jnp.asarray(columns), jnp.asarray(points),
    )
    return out[None]


def solution(mesh):
    return jax.shard_map(
        local,
        mesh=mesh,
        in_specs=(P("space", None), P(), P("tm"), P()),
        out_specs=P("tm", "space", None),
        check_vma=False,
    )
```

```python
import math

import jax
import jax.numpy as jnp
import numpy as np
from jax import lax
from jax.experimental import pallas as pl
from jax.experimental.pallas import tpu as pltpu
from jax.sharding import PartitionSpec as P

SIDE = 24
NG = 864
NOCC = 64
NEMP = 256
MESH = pl.DeviceIdType.MESH
F32 = jnp.float32
BF16 = jnp.bfloat16


def wave_tables():
    pos = np.arange(1024)
    cls, m = pos // 256, pos % 256
    pa, pc = cls >> 1, cls & 1
    trig, ci, bi, ai = m // 108, m // 36 % 3, m // 6 % 6, m % 6
    a, b, c = 2 * ai + pa - 6, bi - 3, 1 + 2 * ci + pc
    valid = m < 216
    natural = np.where(valid, (a + 6) + 12 * (b + 3) + 72 * (c - 1) + 432 * trig, -1)

    def factor(side, wave):
        step = np.mod(side[:, None] * wave[None, :], SIDE)
        angle = step * (2.0 * math.pi / SIDE)
        return np.cos(angle), np.sin(angle)

    x_cos, x_sin = factor(np.arange(16), a)
    y_cos, y_sin = factor(np.arange(24), b)
    y_first = np.where(trig == 0, y_cos, y_sin)
    y_second = np.where(trig == 0, y_sin, -y_cos)
    z_rows = np.concatenate([np.arange(8), np.tile(np.arange(8, 12), 2)])
    z_cos, z_sin = factor(z_rows, c)
    scaling = math.sqrt(2.0 / SIDE**3) * valid
    factors = np.concatenate(
        [x_cos, x_sin, y_first, y_second, z_cos * scaling, z_sin * scaling], axis=0
    ).astype(np.float32)

    where_natural = np.full(1024, -1, np.int32)
    where_natural[natural[valid]] = pos[valid]
    lane = np.arange(1024)
    block, core, low, row = lane // 256, lane // 128 % 2, lane // 32 % 4, lane % 32
    g = 27 * (low * 8 + block * 2 + core) + row
    where_g = np.where(row < 27, where_natural[np.minimum(g, NG - 1)], -1)
    columns = np.stack([where_g, where_natural]).astype(np.int32)

    k = np.arange(256)
    tail = k - 144
    u = np.where(k < 144, k // 8, tail // 8 * 2 + tail % 8 // 4)
    z = np.where(k < 144, k % 8, 8 + tail % 4)
    inside = k < 216
    first = np.where(inside, u * 24 + z, -1)
    second = np.where(inside, u * 24 + 12 + z, -1)
    points = np.concatenate([first, second])[None, :].astype(np.int32)
    return factors, columns, points


FX, FXS, FY, FYS, FZ, FZS = 0, 16, 32, 56, 80, 96


def kernel(
    orb_ref, gaps_ref, times_ref, cw_ref, fac_ref, col_ref, pts_ref, out_ref,
    orb_p, recv, t_own, t_all, lead, quad, table, sel, gap_i, gap_a, acc, m_g, m_h, g_all, h_all,
    g_t, dmat, p_buf, keep, c_send, c_recv, q_buf, r_buf,
    a_recv, a_send, t_recv, t_send, g_recv, g_send, h_recv, h_send, l_sem, x_recv, x_send, r_recv, r_send,
):
    tm = lax.axis_index("tm")
    sp = lax.axis_index("space")
    x, zh = tm // 2, tm % 2
    zl, y, core = sp // 8, sp // 2 % 4, sp % 2
    z = zh * 4 + zl

    def device(xx, yy, zz, cc):
        return (xx * 2 + zz // 4, (zz % 4) * 8 + yy * 2 + cc)

    def remote(src, dst, send, recv_sem, target):
        return pltpu.make_async_remote_copy(
            src_ref=src, dst_ref=dst, send_sem=send, recv_sem=recv_sem,
            device_id=target, device_id_type=MESH,
        )

    barrier = pltpu.get_barrier_semaphore()

    def greet(target):
        pl.semaphore_signal(barrier, inc=1, device_id=target, device_id_type=MESH)

    far = (z + 6 + 4 * core) % 8
    for dy in (2, 1, 3, 0):
        yy = (y + dy) % 4
        for cc in range(2):
            greet(device(x, yy, far, cc))
            greet(device(x, yy, (z + 1) % 8, cc))
            greet(device(x, yy, (z + 7) % 8, cc))
        if dy > 0:
            greet(device(x, yy, z, core))
        greet(device(x, yy, z, 1 - core))
    for dx in range(1, 4):
        greet(device((x + dx) % 4, y, z, core))
    greet(device(x, y, (z + 4) % 8, core))

    t_own[...] = jnp.full((8, 128), times_ref[0], F32)
    pick = lax.broadcasted_iota(jnp.int32, (432, 512), 0) == pts_ref[...]
    pick = jnp.where(pick, 1.0, 0.0).astype(BF16)
    moved = jnp.dot(orb_ref[...], pick, preferred_element_type=F32).astype(BF16)
    for n in range(40):
        orb_p[n] = moved[n * 8 : (n + 1) * 8, :]

    pl.semaphore_wait(barrier, 35)
    for dz, cc in ((2, 0), (-2, 1), (1, 0), (1, 1), (-1, 0), (-1, 1), (0, 0), (0, 1)):
        zz = (z + dz + 8) % 8
        for dy in (2, 1, 3, 0):
            yy = (y + dy) % 4
            blocks = (4 * cc + x, 8 + 4 * zz + yy)
            for part, block in enumerate(blocks):
                src, dst = orb_p.at[block], recv.at[sp, part]
                copy = remote(src, dst, a_send, a_recv.at[sp], device(x, yy, zz, cc))
                if dz == 0 and dy == 0:
                    local = pltpu.make_async_copy(src, dst, a_recv.at[sp])
                    pl.when(core == cc)(local.start)
                    pl.when(core != cc)(copy.start)
                else:
                    copy.start()
    t_all[tm] = t_own[...]

    def lead_rows(xx, carry):
        cos = fac_ref[pl.ds(FX + xx, 1), :]
        sin = fac_ref[pl.ds(FXS + xx, 1), :]
        first, second = fac_ref[FY : FY + 24, :], fac_ref[FYS : FYS + 24, :]
        rows = pl.ds(pl.multiple_of(xx * 24, 8), 24)
        lead[rows, :] = cos * first - sin * second
        quad[rows, :] = sin * first + cos * second
        return carry

    lax.fori_loop(0, 12, lead_rows, 0)
    odd = lax.broadcasted_iota(jnp.int32, (8, 1024), 0) >= 4

    def table_rows(chunk, carry):
        base = chunk * 18

        def pair(v, inner):
            row = base + 2 * v
            a0, a1 = lead[pl.ds(row, 1), :], lead[pl.ds(row + 1, 1), :]
            b0, b1 = quad[pl.ds(row, 1), :], quad[pl.ds(row + 1, 1), :]
            cos, sin = fac_ref[FZ : FZ + 8, :], fac_ref[FZS : FZS + 8, :]
            both = jnp.concatenate([a0 * cos - b0 * sin, a1 * cos - b1 * sin], axis=0)
            table[chunk, pl.ds(pl.multiple_of(v * 16, 16), 16), :] = both.astype(BF16)
            return inner

        lax.fori_loop(0, 9, pair, 0)

        def tail(v):
            row = base + 2 * v
            a = jnp.where(odd, lead[pl.ds(row + 1, 1), :], lead[pl.ds(row, 1), :])
            b = jnp.where(odd, quad[pl.ds(row + 1, 1), :], quad[pl.ds(row, 1), :])
            return a * fac_ref[FZ + 8 : FZ + 16, :] - b * fac_ref[FZS + 8 : FZS + 16, :]

        def tails(w, inner):
            both = jnp.concatenate([tail(2 * w), tail(jnp.minimum(2 * w + 1, 8))], axis=0)
            table[chunk, pl.ds(pl.multiple_of(144 + w * 16, 16), 16), :] = both.astype(BF16)
            return inner

        lax.fori_loop(0, 5, tails, 0)
        table[chunk, 224:256, :] = jnp.zeros((32, 1024), BF16)
        return carry

    lax.fori_loop(0, 16, table_rows, 0)

    def select_rows(n, carry):
        rows = lax.broadcasted_iota(jnp.int32, (128, 1024), 0) + n * 128
        for side in range(2):
            hit = rows == col_ref[side : side + 1, :]
            sel[side, pl.ds(pl.multiple_of(n * 128, 128), 128), :] = jnp.where(hit, 1.0, 0.0).astype(BF16)
        return carry

    lax.fori_loop(0, 8, select_rows, 0)

    pair_index = lax.broadcasted_iota(jnp.int32, (1, 1024), 1)
    which_i = 32 * core + 8 * (pair_index // 256) + pair_index // 8 % 8
    which_a = NOCC + 32 * z + 8 * (pair_index // 64 % 4) + pair_index % 8
    orbital = lax.broadcasted_iota(jnp.int32, (320, 1024), 0)
    hot_i = jnp.where(orbital == which_i, 1.0, 0.0).astype(F32)
    hot_a = jnp.where(orbital == which_a, 1.0, 0.0).astype(F32)
    gaps = jnp.broadcast_to(gaps_ref[...], (8, 320))
    high = lax.Precision.HIGHEST
    gap_i[...] = jnp.dot(gaps, hot_i, precision=high, preferred_element_type=F32)
    gap_a[...] = jnp.dot(gaps, hot_a, precision=high, preferred_element_type=F32)

    acc[...] = jnp.zeros_like(acc)

    def chunk_step(step, carry):
        low = jnp.where(step < 8, 1 - zl % 2, zl % 2)
        n = low * 8 + (step % 8 + 2 * y) % 8
        for shard in (n, n + 16):
            pltpu.make_async_copy(recv.at[shard], recv.at[shard], a_recv.at[shard]).wait()
        i0, e0 = recv[n, 0].astype(F32), recv[n, 1].astype(F32)
        i1, e1 = recv[n + 16, 0].astype(F32), recv[n + 16, 1].astype(F32)
        parts = ([], [], [], [])
        for i in range(8):
            p0, p1 = i0[i : i + 1, :] * e0, i1[i : i + 1, :] * e1
            s, d = p0 + p1, p0 - p1
            parts[0].append(s[:, :256] - s[:, 256:])
            parts[1].append(s[:, :256] + s[:, 256:])
            parts[2].append(d[:, :256] - d[:, 256:])
            parts[3].append(d[:, :256] + d[:, 256:])
        for cls in range(4):
            left = jnp.concatenate(parts[cls], axis=0).astype(BF16)
            lanes = slice(cls * 256, (cls + 1) * 256)
            acc[:, lanes] += jnp.dot(left, table[n, :, lanes], preferred_element_type=F32)
        return carry

    lax.fori_loop(0, 16, chunk_step, 0)
    m_all = acc[...].astype(BF16)
    for n in range(4):
        lanes = slice(n * 256, (n + 1) * 256)
        m_g[n] = jnp.dot(m_all, sel[0, :, lanes], preferred_element_type=F32).astype(BF16)
        m_h[n] = jnp.dot(m_all, sel[1, :, lanes], preferred_element_type=F32).astype(BF16)

    own = x * 4 + y
    for d in (2, 1, 3):
        xx, yy = (x + d) % 4, (y + d) % 4
        remote(m_g.at[xx], g_all.at[own], g_send.at[d], g_recv.at[own], device(xx, y, z, core)).start()
        remote(m_h.at[yy], h_all.at[own], h_send.at[d], h_recv.at[own], device(x, yy, z, core)).start()
    for n, d in enumerate((1, 3)):
        yy, xx = (y + d) % 4, (x + d) % 4
        remote(m_g.at[x], g_all.at[own], g_send.at[4 + n], g_recv.at[own], device(x, yy, z, core)).start()
        remote(m_h.at[y], h_all.at[own], h_send.at[4 + n], h_recv.at[own], device(xx, y, z, core)).start()
    pltpu.make_async_copy(m_g.at[x], g_all.at[own], g_recv.at[own]).start()
    pltpu.make_async_copy(m_h.at[y], h_all.at[own], h_recv.at[own]).start()

    def arrived(buf, sem, slot):
        pltpu.make_async_copy(buf.at[slot], buf.at[slot], sem.at[slot]).wait()

    def pass_g(slot, dy, send):
        remote(g_all.at[slot], g_all.at[slot], g_send.at[send], g_recv.at[slot],
               device(x, (y + dy) % 4, z, core)).start()

    def pass_h(slot, dx, send):
        remote(h_all.at[slot], h_all.at[slot], h_send.at[send], h_recv.at[slot],
               device((x + dx) % 4, y, z, core)).start()

    order = (0, 1, 3, 2)
    for n, d in enumerate(order):
        if d == 0:
            continue
        slot_g, slot_h = (x + d) % 4 * 4 + y, x * 4 + (y + d) % 4
        arrived(g_all, g_recv, slot_g)
        pass_g(slot_g, 1, 4 + 2 * n)
        pass_g(slot_g, 3, 5 + 2 * n)
        arrived(h_all, h_recv, slot_h)
        pass_h(slot_h, 1, 4 + 2 * n)
        pass_h(slot_h, 3, 5 + 2 * n)
    for step in range(1, 8):
        remote(t_own, t_all.at[tm], t_send, t_recv, ((tm + step) % 8, sp)).start()
    for n, d in enumerate(order):
        up_g, up_h = (x + d) % 4 * 4 + (y + 3) % 4, (x + 3) % 4 * 4 + (y + d) % 4
        down_g, down_h = (x + d) % 4 * 4 + (y + 1) % 4, (x + 1) % 4 * 4 + (y + d) % 4
        arrived(g_all, g_recv, up_g)
        pl.when((x + d) % 4 < 2)(lambda s=up_g, k=12 + n: pass_g(s, 1, k))
        arrived(g_all, g_recv, down_g)
        pl.when((x + d) % 4 >= 2)(lambda s=down_g, k=12 + n: pass_g(s, 3, k))
        arrived(h_all, h_recv, up_h)
        pl.when((y + d) % 4 < 2)(lambda s=up_h, k=12 + n: pass_h(s, 1, k))
        arrived(h_all, h_recv, down_h)
        pl.when((y + d) % 4 >= 2)(lambda s=down_h, k=12 + n: pass_h(s, 3, k))
    arrived(g_all, g_recv, own)
    arrived(h_all, h_recv, own)

    pltpu.make_async_copy(t_all.at[pl.ds(0, 7)], t_all.at[pl.ds(0, 7)], t_recv).wait()
    sub = lax.broadcasted_iota(jnp.int32, (8, 128), 0)
    tcol = jnp.zeros((8, 128), F32)
    for n in range(8):
        tcol = jnp.where(sub == n, t_all[n], tcol)
    tcol = tcol[:, 0:1]
    decay = jnp.exp(-gap_i[...] * tcol) * jnp.exp(-gap_a[...] * tcol) * (NOCC**-0.5 * NEMP**-0.5)
    dmat[...] = jnp.dot(cw_ref[...], decay, precision=high, preferred_element_type=F32)
    for d in range(4):
        arrived(g_all, g_recv, d * 4 + (y + 2) % 4)
        arrived(h_all, h_recv, (x + 2) % 4 * 4 + d)

    for n in range(8):
        rows = slice(n * 128, (n + 1) * 128)
        block = jnp.concatenate([g_all[2 * n], g_all[2 * n + 1]], axis=0).astype(F32)
        g_t[:, rows] = block.T
    sibling = device(x, y, z, 1 - core)
    mine = pl.ds(pl.multiple_of(core * 128, 128), 128)
    other = pl.ds(pl.multiple_of((1 - core) * 128, 128), 128)

    slot = z * 4 + y

    def deliver(w):
        pltpu.make_async_copy(c_recv.at[w], c_recv.at[w], x_recv.at[w]).wait()
        total = (keep[w] + c_recv[w].astype(F32)).astype(BF16)
        for low in range(4):
            q_buf[w * 4 + low] = total[low * 32 : (low + 1) * 32, :]
        for low in range(4):
            src = q_buf.at[w * 4 + low]
            target = low * 8 + x * 2 + core
            copy = remote(src, r_buf.at[slot], r_send, r_recv, (w, target))
            local = pltpu.make_async_copy(src, r_buf.at[slot], r_recv)
            here = jnp.logical_and(w == tm, target == sp)
            pl.when(here)(local.start)
            pl.when(jnp.logical_not(here))(copy.start)

    def frequency(w, carry):
        total = jnp.zeros((256, 256), F32)
        for n in range(4):
            lanes = slice(n * 256, (n + 1) * 256)
            left = (g_t[:, lanes] * dmat[pl.ds(w, 1), lanes]).astype(BF16)
            right = h_all[4 * n : 4 * n + 4].reshape(256, 256)
            total += jnp.dot(left, right, preferred_element_type=F32)
        p_buf[...] = total
        keep[w] = p_buf[mine, :]
        c_send[w] = p_buf[other, :].astype(BF16)
        remote(c_send.at[w], c_recv.at[w], x_send.at[w], x_recv.at[w], sibling).start()
        pl.when(w >= 4)(lambda: deliver(w - 4))
        return carry

    lax.fori_loop(0, 8, frequency, 0)
    lax.fori_loop(4, 8, lambda w, carry: (deliver(w), carry)[1], 0)
    pltpu.make_async_copy(r_buf, r_buf, r_recv).wait()
    for n in range(4):
        total = r_buf[n].astype(F32)
        for m in range(1, 8):
            total += r_buf[m * 4 + n].astype(F32)
        width = 256 if n < 3 else 96
        out_ref[:, n * 256 : n * 256 + width] = total[:27, :width]

    away = jnp.where(jnp.logical_and(x == y, True), 1, 0)
    pltpu.make_async_copy(recv.at[pl.ds(0, 31)], recv.at[pl.ds(0, 31)], a_send).wait()
    pltpu.make_async_copy(t_all.at[pl.ds(0, 7)], t_all.at[pl.ds(0, 7)], t_send).wait()
    for n in range(1, 16):
        pltpu.make_async_copy(m_g.at[0], m_g.at[0], g_send.at[n]).wait()
        pltpu.make_async_copy(m_h.at[0], m_h.at[0], h_send.at[n]).wait()
    for n in range(8):
        pltpu.make_async_copy(c_send.at[n], c_send.at[n], x_send.at[n]).wait()
    short = pltpu.make_async_copy(q_buf.at[pl.ds(0, 31)], q_buf.at[pl.ds(0, 31)], r_send)
    whole = pltpu.make_async_copy(q_buf, q_buf, r_send)
    pl.when(away == 1)(short.wait)
    pl.when(away == 0)(whole.wait)


def local(orbitals, gaps, times, cos_weights):
    factors, columns, points = wave_tables()
    vmem = pl.BlockSpec(memory_space=pltpu.VMEM)
    smem = pl.BlockSpec(memory_space=pltpu.SMEM)
    dma = pltpu.SemaphoreType.DMA
    out = pl.pallas_call(
        kernel,
        out_shape=jax.ShapeDtypeStruct((27, NG), F32),
        in_specs=[vmem, vmem, smem, vmem, vmem, vmem, vmem],
        out_specs=vmem,
        scratch_shapes=[
            pltpu.VMEM((40, 8, 512), BF16),
            pltpu.VMEM((32, 2, 8, 512), BF16),
            pltpu.VMEM((8, 128), F32),
            pltpu.VMEM((8, 8, 128), F32),
            pltpu.VMEM((288, 1024), F32),
            pltpu.VMEM((288, 1024), F32),
            pltpu.VMEM((16, 256, 1024), BF16),
            pltpu.VMEM((2, 1024, 1024), BF16),
            pltpu.VMEM((8, 1024), F32),
            pltpu.VMEM((8, 1024), F32),
            pltpu.VMEM((64, 1024), F32),
            pltpu.VMEM((4, 64, 256), BF16),
            pltpu.VMEM((4, 64, 256), BF16),
            pltpu.VMEM((16, 64, 256), BF16),
            pltpu.VMEM((16, 64, 256), BF16),
            pltpu.VMEM((256, 1024), F32),
            pltpu.VMEM((8, 1024), F32),
            pltpu.VMEM((256, 256), F32),
            pltpu.VMEM((8, 128, 256), F32),
            pltpu.VMEM((8, 128, 256), BF16),
            pltpu.VMEM((8, 128, 256), BF16),
            pltpu.VMEM((32, 32, 256), BF16),
            pltpu.VMEM((32, 32, 256), BF16),
            dma((32,)), dma, dma, dma,
            dma((16,)), dma((16,)), dma((16,)), dma((16,)),
            dma,
            dma((8,)), dma((8,)),
            dma, dma,
        ],
        compiler_params=pltpu.CompilerParams(has_side_effects=True, collective_id=0),
    )(
        orbitals.T, gaps[None, :], times, cos_weights,
        jnp.asarray(factors), jnp.asarray(columns), jnp.asarray(points),
    )
    return out[None]


def solution(mesh):
    return jax.shard_map(
        local,
        mesh=mesh,
        in_specs=(P("space", None), P(), P("tm"), P()),
        out_specs=P("tm", "space", None),
        check_vma=False,
    )
```

```python
import math

import jax
import jax.numpy as jnp
import numpy as np
from jax import lax
from jax.experimental import pallas as pl
from jax.experimental.pallas import tpu as pltpu
from jax.sharding import PartitionSpec as P

SIDE = 24
NG = 864
NOCC = 64
NEMP = 256
MESH = pl.DeviceIdType.MESH
F32 = jnp.float32
BF16 = jnp.bfloat16


def wave_tables():
    pos = np.arange(1024)
    group, m = pos // 128, pos % 128
    even = group < 4
    c_even = np.where(even, group % 2, (group - 4) // 2)
    trig = np.where(even, m // 54, group % 2)
    c = 1 + 2 * np.where(even, m // 18 % 3, m // 36) + c_even
    b = np.where(even, m // 3, m // 6) % 6 - 3
    a = np.where(even, 4 * (m % 3) - 4 - 2 * (group // 2), 2 * (m % 6) - 5)
    valid = m < 108
    natural = np.where(valid, (a + 6) + 12 * (b + 3) + 72 * (c - 1) + 432 * trig, -1)

    def factor(side, wave):
        step = np.mod(side[:, None] * wave[None, :], SIDE)
        angle = step * (2.0 * math.pi / SIDE)
        return np.cos(angle), np.sin(angle)

    x_cos, x_sin = factor(np.arange(8), a)
    y_cos, y_sin = factor(np.arange(24), b)
    y_first = np.where(trig == 0, y_cos, y_sin)
    y_second = np.where(trig == 0, y_sin, -y_cos)
    z_rows = np.concatenate([np.arange(8), np.tile(np.arange(8, 12), 2)])
    z_cos, z_sin = factor(z_rows, c)
    scaling = math.sqrt(2.0 / SIDE**3) * valid
    turn = np.where(a % 4 == 1, 1.0, -1.0) * np.ones((8, 1))
    factors = np.concatenate(
        [x_cos, x_sin, y_first, y_second, z_cos * scaling, z_sin * scaling, turn], axis=0
    ).astype(np.float32)

    where_natural = np.full(1024, -1, np.int32)
    where_natural[natural[valid]] = pos[valid]
    lane = np.arange(1024)
    block, core, low, row = lane // 256, lane // 128 % 2, lane // 32 % 4, lane % 32
    g = 27 * (low * 8 + block * 2 + core) + row
    where_g = np.where(row < 27, where_natural[np.minimum(g, NG - 1)], -1)
    offsets = np.repeat(np.array(OFFSETS), 64, axis=0).T
    columns = np.stack([where_g, where_natural, offsets[0], offsets[1]]).astype(np.int32)

    k = np.arange(256)
    tail = k - 144
    u = np.where(k < 144, k // 8, tail // 8 * 2 + tail % 8 // 4)
    z = np.where(k < 144, k % 8, 8 + tail % 4)
    inside = k < 216
    first = np.where(inside, u * 24 + z, -1)
    second = np.where(inside, u * 24 + 12 + z, -1)
    points = np.concatenate([first, second])[None, :].astype(np.int32)
    return factors, columns, points


OFFSETS = (
    (0, 0), (0, 1), (0, 3), (1, 0), (3, 0), (1, 1), (3, 3), (1, 3),
    (3, 1), (0, 2), (2, 0), (1, 2), (2, 1), (3, 2), (2, 3), (2, 2),
)
SLOT = {offset: n for n, offset in enumerate(OFFSETS)}
FX, FXS, FY, FYS, FZ, FZS, FT = 0, 8, 16, 40, 64, 80, 96


def kernel(
    orb_hbm, gaps_hbm, times_hbm, cw_hbm, fac_hbm, col_hbm, pts_hbm, out_any,
    out_ref, gaps_ref, times_ref, cw_ref, col_ref, pts_ref, orb_ref, fac_ref,
    orb_p, recv, t_own, t_all, lead, quad, table, sel, acc, acc_odd, m_g, m_h, g_all, h_all,
    g_t, dmat, both, keep, c_send, c_recv, q_buf, s_buf, f_buf, r_buf,
    a_recv, a_send, t_recv, t_send, u_recv, u_send, g_recv, g_send, h_recv, h_send, l_sem, x_recv, x_send, s_recv, s_send, r_recv, r_send,
):
    tm = lax.axis_index("tm")
    sp = lax.axis_index("space")
    x, zh = tm // 2, tm % 2
    zl, y, core = sp // 8, sp // 2 % 4, sp % 2
    z = zh * 4 + zl

    def device(xx, yy, zz, cc):
        return (xx * 2 + zz // 4, (zz % 4) * 8 + yy * 2 + cc)

    def remote(src, dst, send, recv_sem, target):
        return pltpu.make_async_remote_copy(
            src_ref=src, dst_ref=dst, send_sem=send, recv_sem=recv_sem,
            device_id=target, device_id_type=MESH,
        )

    barrier = pltpu.get_barrier_semaphore()

    def greet(target):
        pl.semaphore_signal(barrier, inc=1, device_id=target, device_id_type=MESH)

    far = (z + 6 + 4 * core) % 8
    for dy in (2, 1, 3, 0):
        yy = (y + dy) % 4
        for cc in range(2):
            greet(device(x, yy, far, cc))
            greet(device(x, yy, (z + 1) % 8, cc))
            greet(device(x, yy, (z + 7) % 8, cc))
        if dy > 0:
            greet(device(x, yy, z, core))
        greet(device(x, yy, z, 1 - core))
    for dx in range(1, 4):
        greet(device((x + dx) % 4, y, z, core))
    greet(device(x, y, (z + 4) % 8, core))

    load_orb = pltpu.make_async_copy(orb_hbm, orb_ref, l_sem.at[0])
    load_pts = pltpu.make_async_copy(pts_hbm, pts_ref, l_sem.at[1])
    load_orb.start()
    load_pts.start()
    loads = [
        pltpu.make_async_copy(src, dst, l_sem.at[2 + n])
        for n, (src, dst) in enumerate((
            (fac_hbm, fac_ref), (col_hbm, col_ref), (gaps_hbm, gaps_ref), (cw_hbm, cw_ref), (times_hbm, times_ref),
        ))
    ]
    for load in loads:
        load.start()

    load_pts.wait()
    pick = lax.broadcasted_iota(jnp.int32, (432, 512), 0) == pts_ref[...]
    pick = jnp.where(pick, 1.0, 0.0).astype(BF16)
    load_orb.wait()
    moved = jnp.dot(orb_ref[...], pick, preferred_element_type=F32).astype(BF16)
    for n in range(40):
        orb_p[n] = moved[n * 8 : (n + 1) * 8, :]

    pl.semaphore_wait(barrier, 35)
    for dy in (2, 1, 3, 0):
        yy = (y + dy) % 4
        for dz, cc in ((2, 0), (-2, 1), (1, 0), (-1, 1), (1, 1), (-1, 0), (0, 0), (0, 1)):
            zz = (z + dz + 8) % 8
            blocks = (4 * cc + x, 8 + 4 * zz + yy)
            for part, block in enumerate(blocks):
                src, dst = orb_p.at[block], recv.at[sp, part]
                copy = remote(src, dst, a_send, a_recv.at[sp], device(x, yy, zz, cc))
                if dz == 0 and dy == 0:
                    local = pltpu.make_async_copy(src, dst, a_recv.at[sp])
                    pl.when(core == cc)(local.start)
                    pl.when(core != cc)(copy.start)
                else:
                    copy.start()
    for load in loads:
        load.wait()
    t_own[...] = jnp.full((8, 128), times_ref[0], F32)
    for dx in range(1, 4):
        remote(t_own, t_all.at[zh * 4 + x], t_send, t_recv, device((x + dx) % 4, y, z, core)).start()
    t_all[zh * 4 + x] = t_own[...]

    def lead_rows(xx, carry):
        cos = fac_ref[pl.ds(FX + xx, 1), :]
        sin = fac_ref[pl.ds(FXS + xx, 1), :]
        first, second = fac_ref[FY : FY + 24, :], fac_ref[FYS : FYS + 24, :]
        rows = pl.ds(pl.multiple_of(xx * 24, 8), 24)
        lead[rows, :] = cos * first - sin * second
        quad[rows, :] = sin * first + cos * second
        return carry

    lax.fori_loop(0, 6, lead_rows, 0)
    odd = lax.broadcasted_iota(jnp.int32, (8, 1024), 0) >= 4

    def table_rows(chunk, carry):
        base = chunk * 18

        def pair(v, inner):
            row = base + 2 * v
            a0, a1 = lead[pl.ds(row, 1), :], lead[pl.ds(row + 1, 1), :]
            b0, b1 = quad[pl.ds(row, 1), :], quad[pl.ds(row + 1, 1), :]
            cos, sin = fac_ref[FZ : FZ + 8, :], fac_ref[FZS : FZS + 8, :]
            both = jnp.concatenate([a0 * cos - b0 * sin, a1 * cos - b1 * sin], axis=0)
            table[chunk, pl.ds(pl.multiple_of(v * 16, 16), 16), :] = both.astype(BF16)
            return inner

        lax.fori_loop(0, 9, pair, 0)

        def tail(v):
            row = base + 2 * v
            a = jnp.where(odd, lead[pl.ds(row + 1, 1), :], lead[pl.ds(row, 1), :])
            b = jnp.where(odd, quad[pl.ds(row + 1, 1), :], quad[pl.ds(row, 1), :])
            return a * fac_ref[FZ + 8 : FZ + 16, :] - b * fac_ref[FZS + 8 : FZS + 16, :]

        def tails(w, inner):
            both = jnp.concatenate([tail(2 * w), tail(jnp.minimum(2 * w + 1, 8))], axis=0)
            table[chunk, pl.ds(pl.multiple_of(144 + w * 16, 16), 16), :] = both.astype(BF16)
            return inner

        lax.fori_loop(0, 5, tails, 0)
        table[chunk, 224:256, :] = jnp.zeros((32, 1024), BF16)
        return carry

    lax.fori_loop(0, 8, table_rows, 0)

    def select_rows(n, carry):
        rows = lax.broadcasted_iota(jnp.int32, (128, 1024), 0) + n * 128
        for side in range(2):
            hit = rows == col_ref[side : side + 1, :]
            sel[side, pl.ds(pl.multiple_of(n * 128, 128), 128), :] = jnp.where(hit, 1.0, 0.0).astype(BF16)
        return carry

    lax.fori_loop(0, 8, select_rows, 0)

    pltpu.make_async_copy(t_all.at[pl.ds(0, 3)], t_all.at[pl.ds(0, 3)], t_recv).wait()
    half_times = t_all.at[pl.ds(zh * 4, 4)]
    remote(half_times, half_times, u_send, u_recv, device(x, y, (z + 4) % 8, core)).start()

    acc[...] = jnp.zeros_like(acc)
    acc_odd[...] = jnp.zeros_like(acc_odd)

    def chunk_step(step, carry):
        turn = step // 2
        away = jnp.where(turn == 0, 2, 2 * turn - 1)
        away = jnp.where(turn == 3, 0, away)
        n = (y + away) % 4 * 2 + step % 2
        for quarter in range(4):
            shard = n + 8 * quarter
            pltpu.make_async_copy(recv.at[shard], recv.at[shard], a_recv.at[shard]).wait()
        occupied = [recv[n + 8 * quarter, 0].astype(F32) for quarter in range(4)]
        empty = [recv[n + 8 * quarter, 1].astype(F32) for quarter in range(4)]
        minus, plus = ([], [], [], []), ([], [], [], [])
        for i in range(8):
            p = [o[i : i + 1, :] * e for o, e in zip(occupied, empty)]
            s0, s1, d0, d1 = p[0] + p[2], p[1] + p[3], p[0] - p[2], p[1] - p[3]
            for kind, value in enumerate((s0 + s1, s0 - s1, d0, d1)):
                minus[kind].append(value[:, :256] - value[:, 256:])
                plus[kind].append(value[:, :256] + value[:, 256:])

        def product(rows, start, width):
            left = jnp.concatenate(rows, axis=0).astype(BF16)
            return jnp.dot(left, table[n, :, start : start + width], preferred_element_type=F32)

        acc[:, 0:128] += product(minus[0], 0, 128)
        acc[:, 128:256] += product(plus[0], 128, 128)
        acc[:, 256:384] += product(minus[1], 256, 128)
        acc[:, 384:512] += product(plus[1], 384, 128)
        acc_odd[:, 0:256] += product(minus[2] + minus[3], 512, 256)
        acc_odd[:, 256:512] += product(plus[2] + plus[3], 768, 256)
        return carry

    lax.fori_loop(0, 8, chunk_step, 0)
    columns = [acc[...]]
    for part in range(2):
        at = part * 256
        sign = fac_ref[FT : FT + 1, 512 + at : 640 + at]
        u_cos, u_sin = acc_odd[0:64, at : at + 128], acc_odd[0:64, at + 128 : at + 256]
        v_cos, v_sin = acc_odd[64:128, at : at + 128], acc_odd[64:128, at + 128 : at + 256]
        columns += [u_cos - sign * v_sin, u_sin + sign * v_cos]
    m_all = jnp.concatenate(columns, axis=1).astype(BF16)
    for n in range(4):
        lanes = slice(n * 256, (n + 1) * 256)
        m_g[n] = jnp.dot(m_all, sel[0, :, lanes], preferred_element_type=F32).astype(BF16)
        m_h[n] = jnp.dot(m_all, sel[1, :, lanes], preferred_element_type=F32).astype(BF16)

    def send_g(src, to, dx, dy, send):
        target = device((x + dx) % 4, (y + dy) % 4, z, core)
        remote(src, g_all.at[to], g_send.at[send], g_recv.at[to], target).start()

    def send_h(src, to, dx, dy, send):
        target = device((x + dx) % 4, (y + dy) % 4, z, core)
        remote(src, h_all.at[to], h_send.at[send], h_recv.at[to], target).start()

    for d in (2, 1, 3):
        send_g(m_g.at[(y + d) % 4], SLOT[0, 4 - d], 0, d, d)
        send_h(m_h.at[(x + d) % 4], SLOT[4 - d, 0], d, 0, d)
    for n, d in enumerate((1, 3)):
        send_g(m_g.at[y], SLOT[4 - d, 0], d, 0, 4 + n)
        send_h(m_h.at[x], SLOT[0, 4 - d], 0, d, 4 + n)
    pltpu.make_async_copy(m_g.at[y], g_all.at[0], g_recv.at[0]).start()
    pltpu.make_async_copy(m_h.at[x], h_all.at[0], h_recv.at[0]).start()

    pltpu.make_async_copy(half_times, half_times, u_recv).wait()
    pair_index = lax.broadcasted_iota(jnp.int32, (1, 1024), 1)
    which_i = 32 * core + 8 * ((col_ref[2:3, :] + x) % 4) + pair_index // 8 % 8
    which_a = NOCC + 32 * z + 8 * ((col_ref[3:4, :] + y) % 4) + pair_index % 8
    orbital = lax.broadcasted_iota(jnp.int32, (320, 1024), 0)
    hot_i = jnp.where(orbital == which_i, 1.0, 0.0).astype(F32)
    hot_a = jnp.where(orbital == which_a, 1.0, 0.0).astype(F32)
    gaps = jnp.broadcast_to(gaps_ref[...].reshape(1, 320), (8, 320))
    high = lax.Precision.HIGHEST
    gap_i = jnp.dot(gaps, hot_i, precision=high, preferred_element_type=F32)
    gap_a = jnp.dot(gaps, hot_a, precision=high, preferred_element_type=F32)
    sub = lax.broadcasted_iota(jnp.int32, (8, 128), 0)
    tcol = jnp.zeros((8, 128), F32)
    for n in range(8):
        tcol = jnp.where(sub == n, t_all[n % 2 * 4 + n // 2], tcol)
    tcol = tcol[:, 0:1]
    decay = jnp.exp(-gap_i * tcol) * jnp.exp(-gap_a * tcol) * (NOCC**-0.5 * NEMP**-0.5)
    dmat[...] = jnp.dot(cw_ref[...], decay, precision=high, preferred_element_type=F32)

    def arrived(buf, sem, slot):
        pltpu.make_async_copy(buf.at[slot], buf.at[slot], sem.at[slot]).wait()

    def got_g(dx, dy):
        arrived(g_all, g_recv, SLOT[dx, dy])

    def got_h(dx, dy):
        arrived(h_all, h_recv, SLOT[dx, dy])

    def relay(d, n):
        got_g(3, d)
        up = (y + d) % 4 < 2
        pl.when(up)(lambda: send_g(g_all.at[SLOT[3, d]], SLOT[2, d], 1, 0, 12 + n))
        got_g(1, d)
        pl.when(jnp.logical_not(up))(lambda: send_g(g_all.at[SLOT[1, d]], SLOT[2, d], 3, 0, 12 + n))
        got_h(d, 3)
        up = (x + d) % 4 < 2
        pl.when(up)(lambda: send_h(h_all.at[SLOT[d, 3]], SLOT[d, 2], 0, 1, 12 + n))
        got_h(d, 1)
        pl.when(jnp.logical_not(up))(lambda: send_h(h_all.at[SLOT[d, 1]], SLOT[d, 2], 0, 3, 12 + n))

    relay(0, 0)
    for n, d in enumerate((1, 3, 2)):
        got_g(0, d)
        send_g(g_all.at[SLOT[0, d]], SLOT[3, d], 1, 0, 6 + 2 * n)
        send_g(g_all.at[SLOT[0, d]], SLOT[1, d], 3, 0, 7 + 2 * n)
        got_h(d, 0)
        send_h(h_all.at[SLOT[d, 0]], SLOT[d, 3], 0, 1, 6 + 2 * n)
        send_h(h_all.at[SLOT[d, 0]], SLOT[d, 1], 0, 3, 7 + 2 * n)
    for n, d in enumerate((1, 3, 2)):
        relay(d, 1 + n)
    got_g(0, 0)
    got_h(0, 0)

    def turn_g(start):
        for n in range(start, start + 4):
            block = jnp.concatenate([g_all[2 * n], g_all[2 * n + 1]], axis=0).astype(F32)
            g_t[:, n * 128 : (n + 1) * 128] = block.T

    turn_g(0)
    h_early = h_all[0:8].reshape(512, 256)

    def early(w, carry):
        left = (g_t[:, 0:512] * dmat[pl.ds(w, 1), 0:512]).astype(BF16)
        keep[w] = jnp.dot(left, h_early, preferred_element_type=F32)
        return carry

    lax.fori_loop(0, 8, early, 0)
    for d in range(4):
        got_g(2, d)
        got_h(d, 2)
    turn_g(4)
    sibling = device(x, y, z, 1 - core)
    mine = pl.ds(pl.multiple_of(core * 128, 128), 128)
    other = pl.ds(pl.multiple_of((1 - core) * 128, 128), 128)

    side = 2 * ((z + core) % 2) - 1
    partner = device(x, y, (z - side + 8) % 8, core)

    h_late = h_all[8:16].reshape(512, 256)

    def late(w, rows):
        left = [g_t[rows, 512:1024] * dmat[pl.ds(w + n, 1), 512:1024] for n in range(2)]
        left = jnp.concatenate(left, axis=0).astype(BF16)
        return jnp.dot(left, h_late, preferred_element_type=F32)

    def for_sibling(n, carry):
        total = late(2 * n, other)
        for m in range(2):
            w = 2 * n + m
            c_send[w] = (keep[w, other, :] + total[m * 128 : (m + 1) * 128, :]).astype(BF16)
            remote(c_send.at[w], c_recv.at[w], x_send.at[w], x_recv.at[w], sibling).start()
        return carry

    def both_cores(n, carry):
        rest = late(2 * n, mine)
        for m in range(2):
            w = 2 * n + m
            pltpu.make_async_copy(c_recv.at[w], c_recv.at[w], x_recv.at[w]).wait()
            total = keep[w, mine, :] + rest[m * 128 : (m + 1) * 128, :] + c_recv[w].astype(F32)
            both[w] = total
            for low in range(4):
                q_buf[w * 4 + low] = total[low * 32 : (low + 1) * 32, :].astype(BF16)
            for low in range(4):
                owner = m * 4 + low
                step = ((owner - z) * side + 8) % 8
                there = n * 4 + 7 - step
                copy = remote(q_buf.at[w * 4 + low], s_buf.at[there], s_send, s_recv.at[there], partner)
                pl.when(step >= 4)(copy.start)
        return carry

    lax.fori_loop(0, 4, for_sibling, 0)
    lax.fori_loop(0, 4, both_cores, 0)
    slot = (z + core) // 2 % 4 * 4 + x

    def deliver(n, carry):
        step = 3 - n % 4
        owner = (z + side * step + 8) % 8
        w, low = n // 4 * 2 + owner // 4, owner % 4
        here = n // 4 * 4 + step
        pltpu.make_async_copy(s_buf.at[here], s_buf.at[here], s_recv.at[here]).wait()
        rows = pl.ds(pl.multiple_of(low * 32, 32), 32)
        f_buf[here] = (both[w, rows, :] + s_buf[here].astype(F32)).astype(BF16)
        target = low * 8 + y * 2 + core
        copy = remote(f_buf.at[here], r_buf.at[slot], r_send, r_recv, (w, target))
        local = pltpu.make_async_copy(f_buf.at[here], r_buf.at[slot], r_recv)
        own_block = jnp.logical_and(w == tm, target == sp)
        pl.when(own_block)(local.start)
        pl.when(jnp.logical_not(own_block))(copy.start)
        return carry

    lax.fori_loop(0, 16, deliver, 0)
    pltpu.make_async_copy(r_buf, r_buf, r_recv).wait()
    for n in range(4):
        total = r_buf[n].astype(F32)
        for m in range(1, 4):
            total += r_buf[m * 4 + n].astype(F32)
        width = 256 if n < 3 else 96
        out_ref[:, 0, n * 256 : n * 256 + width] = total[:27, :width]

    final = pltpu.make_async_copy(out_ref, out_any, l_sem.at[0])
    final.start()

    pltpu.make_async_copy(recv.at[pl.ds(0, 31)], recv.at[pl.ds(0, 31)], a_send).wait()
    pltpu.make_async_copy(t_all.at[pl.ds(0, 3)], t_all.at[pl.ds(0, 3)], t_send).wait()
    pltpu.make_async_copy(half_times, half_times, u_send).wait()
    for n in range(1, 16):
        pltpu.make_async_copy(m_g.at[0], m_g.at[0], g_send.at[n]).wait()
        pltpu.make_async_copy(m_h.at[0], m_h.at[0], h_send.at[n]).wait()
    for n in range(8):
        pltpu.make_async_copy(c_send.at[n], c_send.at[n], x_send.at[n]).wait()
    pltpu.make_async_copy(s_buf, s_buf, s_send).wait()
    final.wait()
    pltpu.make_async_copy(f_buf.at[pl.ds(0, 15)], f_buf.at[pl.ds(0, 15)], r_send).wait()


def local(orbitals, gaps, times, cos_weights):
    factors, columns, points = wave_tables()
    stay = lambda value: pltpu.with_memory_space_constraint(value, pltpu.HBM)
    dma = pltpu.SemaphoreType.DMA
    out = pl.pallas_call(
        kernel,
        out_shape=jax.ShapeDtypeStruct((27, 1, NG), F32),
        in_specs=[pl.BlockSpec(memory_space=pltpu.HBM)] * 7,
        out_specs=pl.BlockSpec(memory_space=pl.ANY),
        scratch_shapes=[
            pltpu.VMEM((27, 1, NG), F32),
            pltpu.VMEM((NOCC + NEMP,), F32),
            pltpu.SMEM((1,), F32),
            pltpu.VMEM((8, 8), F32),
            pltpu.VMEM((4, 1024), jnp.int32),
            pltpu.VMEM((1, 512), jnp.int32),
            pltpu.VMEM((320, 432), BF16),
            pltpu.VMEM((104, 1024), F32),
            pltpu.VMEM((40, 8, 512), BF16),
            pltpu.VMEM((32, 2, 8, 512), BF16),
            pltpu.VMEM((8, 128), F32),
            pltpu.VMEM((8, 8, 128), F32),
            pltpu.VMEM((144, 1024), F32),
            pltpu.VMEM((144, 1024), F32),
            pltpu.VMEM((8, 256, 1024), BF16),
            pltpu.VMEM((2, 1024, 1024), BF16),
            pltpu.VMEM((64, 512), F32),
            pltpu.VMEM((128, 512), F32),
            pltpu.VMEM((4, 64, 256), BF16),
            pltpu.VMEM((4, 64, 256), BF16),
            pltpu.VMEM((16, 64, 256), BF16),
            pltpu.VMEM((16, 64, 256), BF16),
            pltpu.VMEM((256, 1024), F32),
            pltpu.VMEM((8, 1024), F32),
            pltpu.VMEM((8, 128, 256), F32),
            pltpu.VMEM((8, 256, 256), F32),
            pltpu.VMEM((8, 128, 256), BF16),
            pltpu.VMEM((8, 128, 256), BF16),
            pltpu.VMEM((32, 32, 256), BF16),
            pltpu.VMEM((16, 32, 256), BF16),
            pltpu.VMEM((16, 32, 256), BF16),
            pltpu.VMEM((16, 32, 256), BF16),
            dma((32,)), dma, dma, dma, dma, dma,
            dma((16,)), dma((16,)), dma((16,)), dma((16,)),
            dma((7,)),
            dma((8,)), dma((8,)),
            dma((16,)), dma,
            dma, dma,
        ],
        compiler_params=pltpu.CompilerParams(has_side_effects=True, collective_id=0, vmem_limit_bytes=34 * 2**20),
    )(
        stay(orbitals.T), stay(gaps), times, stay(cos_weights),
        stay(jnp.asarray(factors)), stay(jnp.asarray(columns)), stay(jnp.asarray(points)),
    )
    return out.transpose(1, 0, 2)


def solution(mesh):
    return jax.shard_map(
        local,
        mesh=mesh,
        in_specs=(P("space", None), P(), P("tm"), P()),
        out_specs=P("tm", "space", None),
        check_vma=False,
    )
```

```python
import math

import jax
import jax.numpy as jnp
import numpy as np
from jax import lax
from jax.experimental import pallas as pl
from jax.experimental.pallas import tpu as pltpu
from jax.sharding import PartitionSpec as P

SIDE = 24
NG = 864
NOCC = 64
NEMP = 256
MESH = pl.DeviceIdType.MESH
F32 = jnp.float32
BF16 = jnp.bfloat16


def wave_tables():
    pos = np.arange(1024)
    group, m = pos // 128, pos % 128
    even = group < 4
    c_even = np.where(even, group % 2, (group - 4) // 2)
    trig = np.where(even, m // 54, group % 2)
    c = 1 + 2 * np.where(even, m // 18 % 3, m // 36) + c_even
    b = np.where(even, m // 3, m // 6) % 6 - 3
    a = np.where(even, 4 * (m % 3) - 4 - 2 * (group // 2), 2 * (m % 6) - 5)
    valid = m < 108
    natural = np.where(valid, (a + 6) + 12 * (b + 3) + 72 * (c - 1) + 432 * trig, -1)

    def factor(side, wave):
        step = np.mod(side[:, None] * wave[None, :], SIDE)
        angle = step * (2.0 * math.pi / SIDE)
        return np.cos(angle), np.sin(angle)

    x_cos, x_sin = factor(np.arange(8), a)
    y_cos, y_sin = factor(np.arange(24), b)
    y_first = np.where(trig == 0, y_cos, y_sin)
    y_second = np.where(trig == 0, y_sin, -y_cos)
    z_rows = np.concatenate([np.arange(8), np.tile(np.arange(8, 12), 2)])
    z_cos, z_sin = factor(z_rows, c)
    scaling = math.sqrt(2.0 / SIDE**3) * valid
    turn = np.where(a % 4 == 1, 1.0, -1.0) * np.ones((8, 1))
    factors = np.concatenate(
        [x_cos, x_sin, y_first, y_second, z_cos * scaling, z_sin * scaling, turn], axis=0
    ).astype(np.float32)

    where_natural = np.full(1024, -1, np.int32)
    where_natural[natural[valid]] = pos[valid]
    lane = np.arange(1024)
    block, core, low, row = lane // 256, lane // 128 % 2, lane // 32 % 4, lane % 32
    g = 27 * (low * 8 + block * 2 + core) + row
    where_g = np.where(row < 27, where_natural[np.minimum(g, NG - 1)], -1)
    offsets = np.repeat(np.array(OFFSETS), 64, axis=0).T
    columns = np.stack([where_g, where_natural, offsets[0], offsets[1]]).astype(np.int32)

    k = np.arange(256)
    tail = k - 144
    u = np.where(k < 144, k // 8, tail // 8 * 2 + tail % 8 // 4)
    z = np.where(k < 144, k % 8, 8 + tail % 4)
    inside = k < 216
    first = np.where(inside, u * 24 + z, -1)
    second = np.where(inside, u * 24 + 12 + z, -1)
    points = np.concatenate([first, second])[None, :].astype(np.int32)
    return factors, columns, points


OFFSETS = (
    (0, 0), (0, 1), (0, 3), (1, 0), (3, 0), (1, 1), (3, 3), (1, 3),
    (3, 1), (0, 2), (2, 0), (1, 2), (2, 1), (3, 2), (2, 3), (2, 2),
)
SLOT = {offset: n for n, offset in enumerate(OFFSETS)}
FX, FXS, FY, FYS, FZ, FZS, FT = 0, 8, 16, 40, 64, 80, 96


def kernel(
    orb_hbm, gaps_hbm, times_hbm, cw_hbm, fac_hbm, col_hbm, pts_hbm, out_any,
    out_ref, gaps_ref, times_ref, cw_ref, col_ref, pts_ref, orb_ref, fac_ref,
    orb_p, recv, t_own, t_all, lead, quad, table, sel, acc, acc_odd, m_g, m_h, g_all, h_all,
    g_t, dmat, both, keep, c_send, c_recv, q_buf, s_buf, f_buf, r_buf,
    a_recv, a_send, t_recv, t_send, u_recv, u_send, g_recv, g_send, h_recv, h_send, l_sem, x_recv, x_send, s_recv, s_send, r_recv, r_send,
):
    tm = lax.axis_index("tm")
    sp = lax.axis_index("space")
    x, zh = tm // 2, tm % 2
    zl, y, core = sp // 8, sp // 2 % 4, sp % 2
    z = zh * 4 + zl

    def device(xx, yy, zz, cc):
        return (xx * 2 + zz // 4, (zz % 4) * 8 + yy * 2 + cc)

    def remote(src, dst, send, recv_sem, target):
        return pltpu.make_async_remote_copy(
            src_ref=src, dst_ref=dst, send_sem=send, recv_sem=recv_sem,
            device_id=target, device_id_type=MESH,
        )

    load_orb = pltpu.make_async_copy(orb_hbm, orb_ref, l_sem.at[0])
    load_pts = pltpu.make_async_copy(pts_hbm, pts_ref, l_sem.at[1])
    load_orb.start()
    load_pts.start()
    loads = [
        pltpu.make_async_copy(src, dst, l_sem.at[2])
        for n, (src, dst) in enumerate((
            (fac_hbm, fac_ref), (col_hbm, col_ref), (gaps_hbm, gaps_ref), (cw_hbm, cw_ref), (times_hbm, times_ref),
        ))
    ]
    for load in loads:
        load.start()

    barrier = pltpu.get_barrier_semaphore()

    def greet(target):
        pl.semaphore_signal(barrier, inc=1, device_id=target, device_id_type=MESH)

    far = (z + 6 + 4 * core) % 8
    for dy in (2, 1, 3, 0):
        yy = (y + dy) % 4
        for cc in range(2):
            greet(device(x, yy, far, cc))
            greet(device(x, yy, (z + 1) % 8, cc))
            greet(device(x, yy, (z + 7) % 8, cc))
        if dy > 0:
            greet(device(x, yy, z, core))
        greet(device(x, yy, z, 1 - core))
    for dx in range(1, 4):
        greet(device((x + dx) % 4, y, z, core))
    greet(device(x, y, (z + 4) % 8, core))

    load_pts.wait()
    pick = lax.broadcasted_iota(jnp.int32, (432, 512), 0) == pts_ref[...]
    pick = jnp.where(pick, 1.0, 0.0).astype(BF16)
    load_orb.wait()
    moved = jnp.dot(orb_ref[...], pick, preferred_element_type=F32).astype(BF16)
    for n in range(40):
        orb_p[n] = moved[n * 8 : (n + 1) * 8, :]

    pl.semaphore_wait(barrier, 35)
    links = ((2, 0), (-2, 1), (1, 0), (-1, 1), (1, 1), (-1, 0), (0, 0), (0, 1))
    for dy, (dz, cc) in [(dy, link) for pair in ((1, 3), (2, 0)) for link in links for dy in pair]:
        yy, zz = (y + dy) % 4, (z + dz + 8) % 8
        blocks = (4 * cc + x, 8 + 4 * zz + yy)
        for part, block in enumerate(blocks):
            src, dst = orb_p.at[block], recv.at[sp, part]
            copy = remote(src, dst, a_send, a_recv.at[sp % 8], device(x, yy, zz, cc))
            if dz == 0 and dy == 0:
                local = pltpu.make_async_copy(src, dst, a_recv.at[sp % 8])
                pl.when(core == cc)(local.start)
                pl.when(core != cc)(copy.start)
            else:
                copy.start()
    for load in loads:
        load.wait()
    t_own[...] = jnp.full((8, 128), times_ref[0], F32)
    for dx in range(1, 4):
        remote(t_own, t_all.at[zh * 4 + x], t_send, t_recv, device((x + dx) % 4, y, z, core)).start()
    t_all[zh * 4 + x] = t_own[...]

    def lead_rows(xx, carry):
        cos = fac_ref[pl.ds(FX + xx, 1), :]
        sin = fac_ref[pl.ds(FXS + xx, 1), :]
        first, second = fac_ref[FY : FY + 24, :], fac_ref[FYS : FYS + 24, :]
        rows = pl.ds(pl.multiple_of(xx * 24, 8), 24)
        lead[rows, :] = cos * first - sin * second
        quad[rows, :] = sin * first + cos * second
        return carry

    lax.fori_loop(0, 6, lead_rows, 0)
    odd = lax.broadcasted_iota(jnp.int32, (8, 1024), 0) >= 4

    def table_rows(chunk, carry):
        base = chunk * 18

        def pair(v, inner):
            row = base + 2 * v
            a0, a1 = lead[pl.ds(row, 1), :], lead[pl.ds(row + 1, 1), :]
            b0, b1 = quad[pl.ds(row, 1), :], quad[pl.ds(row + 1, 1), :]
            cos, sin = fac_ref[FZ : FZ + 8, :], fac_ref[FZS : FZS + 8, :]
            both = jnp.concatenate([a0 * cos - b0 * sin, a1 * cos - b1 * sin], axis=0)
            table[chunk, pl.ds(pl.multiple_of(v * 16, 16), 16), :] = both.astype(BF16)
            return inner

        lax.fori_loop(0, 9, pair, 0)

        def tail(v):
            row = base + 2 * v
            a = jnp.where(odd, lead[pl.ds(row + 1, 1), :], lead[pl.ds(row, 1), :])
            b = jnp.where(odd, quad[pl.ds(row + 1, 1), :], quad[pl.ds(row, 1), :])
            return a * fac_ref[FZ + 8 : FZ + 16, :] - b * fac_ref[FZS + 8 : FZS + 16, :]

        def tails(w, inner):
            both = jnp.concatenate([tail(2 * w), tail(jnp.minimum(2 * w + 1, 8))], axis=0)
            table[chunk, pl.ds(pl.multiple_of(144 + w * 16, 16), 16), :] = both.astype(BF16)
            return inner

        lax.fori_loop(0, 5, tails, 0)
        table[chunk, 224:256, :] = jnp.zeros((32, 1024), BF16)
        return carry

    lax.fori_loop(0, 8, table_rows, 0)

    def select_rows(n, carry):
        rows = lax.broadcasted_iota(jnp.int32, (128, 1024), 0) + n * 128
        for side in range(2):
            hit = rows == col_ref[side : side + 1, :]
            sel[side, pl.ds(pl.multiple_of(n * 128, 128), 128), :] = jnp.where(hit, 1.0, 0.0).astype(BF16)
        return carry

    lax.fori_loop(0, 8, select_rows, 0)

    pltpu.make_async_copy(t_all.at[pl.ds(0, 3)], t_all.at[pl.ds(0, 3)], t_recv).wait()
    half_times = t_all.at[pl.ds(zh * 4, 4)]
    remote(half_times, half_times, u_send, u_recv, device(x, y, (z + 4) % 8, core)).start()

    acc[...] = jnp.zeros_like(acc)
    acc_odd[...] = jnp.zeros_like(acc_odd)

    def chunk_step(step, carry):
        turn = step // 2
        away = jnp.where(turn < 2, 2 * turn + 1, 6 - 2 * turn)
        n = (y + away) % 4 * 2 + step % 2
        pltpu.make_async_copy(recv.at[pl.ds(0, 4)], recv.at[pl.ds(0, 4)], a_recv.at[n]).wait()
        occupied = [recv[n + 8 * quarter, 0].astype(F32) for quarter in range(4)]
        empty = [recv[n + 8 * quarter, 1].astype(F32) for quarter in range(4)]
        minus, plus = ([], [], [], []), ([], [], [], [])
        for i in range(8):
            p = [o[i : i + 1, :] * e for o, e in zip(occupied, empty)]
            s0, s1, d0, d1 = p[0] + p[2], p[1] + p[3], p[0] - p[2], p[1] - p[3]
            for kind, value in enumerate((s0 + s1, s0 - s1, d0, d1)):
                minus[kind].append(value[:, :256] - value[:, 256:])
                plus[kind].append(value[:, :256] + value[:, 256:])

        def product(rows, start, width):
            left = jnp.concatenate(rows, axis=0).astype(BF16)
            return jnp.dot(left, table[n, :, start : start + width], preferred_element_type=F32)

        acc[:, 0:128] += product(minus[0], 0, 128)
        acc[:, 128:256] += product(plus[0], 128, 128)
        acc[:, 256:384] += product(minus[1], 256, 128)
        acc[:, 384:512] += product(plus[1], 384, 128)
        acc_odd[:, 0:256] += product(minus[2] + minus[3], 512, 256)
        acc_odd[:, 256:512] += product(plus[2] + plus[3], 768, 256)
        return carry

    lax.fori_loop(0, 8, chunk_step, 0)
    columns = [acc[...]]
    for part in range(2):
        at = part * 256
        sign = fac_ref[FT : FT + 1, 512 + at : 640 + at]
        u_cos, u_sin = acc_odd[0:64, at : at + 128], acc_odd[0:64, at + 128 : at + 256]
        v_cos, v_sin = acc_odd[64:128, at : at + 128], acc_odd[64:128, at + 128 : at + 256]
        columns += [u_cos - sign * v_sin, u_sin + sign * v_cos]
    m_all = jnp.concatenate(columns, axis=1).astype(BF16)
    for n in range(4):
        lanes = slice(n * 256, (n + 1) * 256)
        m_g[n] = jnp.dot(m_all, sel[0, :, lanes], preferred_element_type=F32).astype(BF16)
        m_h[n] = jnp.dot(m_all, sel[1, :, lanes], preferred_element_type=F32).astype(BF16)

    def send_g(src, to, dx, dy):
        target = device((x + dx) % 4, (y + dy) % 4, z, core)
        remote(src, g_all.at[to], g_send, g_recv.at[to], target).start()

    def send_h(src, to, dx, dy):
        target = device((x + dx) % 4, (y + dy) % 4, z, core)
        remote(src, h_all.at[to], h_send, h_recv.at[to], target).start()

    for d in (2, 1, 3):
        send_g(m_g.at[(y + d) % 4], SLOT[0, 4 - d], 0, d)
        send_h(m_h.at[(x + d) % 4], SLOT[4 - d, 0], d, 0)
    for d in (1, 3):
        send_g(m_g.at[y], SLOT[4 - d, 0], d, 0)
        send_h(m_h.at[x], SLOT[0, 4 - d], 0, d)
    pltpu.make_async_copy(m_g.at[y], g_all.at[0], g_recv.at[0]).start()
    pltpu.make_async_copy(m_h.at[x], h_all.at[0], h_recv.at[0]).start()

    pltpu.make_async_copy(half_times, half_times, u_recv).wait()
    pair_index = lax.broadcasted_iota(jnp.int32, (1, 1024), 1)
    which_i = 32 * core + 8 * ((col_ref[2:3, :] + x) % 4) + pair_index // 8 % 8
    which_a = NOCC + 32 * z + 8 * ((col_ref[3:4, :] + y) % 4) + pair_index % 8
    orbital = lax.broadcasted_iota(jnp.int32, (320, 1024), 0)
    hot_i = jnp.where(orbital == which_i, 1.0, 0.0).astype(F32)
    hot_a = jnp.where(orbital == which_a, 1.0, 0.0).astype(F32)
    gaps = jnp.broadcast_to(gaps_ref[...].reshape(1, 320), (8, 320))
    high = lax.Precision.HIGHEST
    gap_i = jnp.dot(gaps, hot_i, precision=high, preferred_element_type=F32)
    gap_a = jnp.dot(gaps, hot_a, precision=high, preferred_element_type=F32)
    sub = lax.broadcasted_iota(jnp.int32, (8, 128), 0)
    tcol = jnp.zeros((8, 128), F32)
    for n in range(8):
        tcol = jnp.where(sub == n, t_all[n % 2 * 4 + n // 2], tcol)
    tcol = tcol[:, 0:1]
    decay = jnp.exp(-gap_i * tcol) * jnp.exp(-gap_a * tcol) * (NOCC**-0.5 * NEMP**-0.5)
    dmat[...] = jnp.dot(cw_ref[...], decay, precision=high, preferred_element_type=F32)

    def arrived(buf, sem, slot):
        pltpu.make_async_copy(buf.at[slot], buf.at[slot], sem.at[slot]).wait()

    def got_g(dx, dy):
        arrived(g_all, g_recv, SLOT[dx, dy])

    def got_h(dx, dy):
        arrived(h_all, h_recv, SLOT[dx, dy])

    def relay(d):
        got_g(3, d)
        up = (y + d) % 4 < 2
        pl.when(up)(lambda: send_g(g_all.at[SLOT[3, d]], SLOT[2, d], 1, 0))
        got_g(1, d)
        pl.when(jnp.logical_not(up))(lambda: send_g(g_all.at[SLOT[1, d]], SLOT[2, d], 3, 0))
        got_h(d, 3)
        up = (x + d) % 4 < 2
        pl.when(up)(lambda: send_h(h_all.at[SLOT[d, 3]], SLOT[d, 2], 0, 1))
        got_h(d, 1)
        pl.when(jnp.logical_not(up))(lambda: send_h(h_all.at[SLOT[d, 1]], SLOT[d, 2], 0, 3))

    relay(0)
    for d in (1, 3, 2):
        got_g(0, d)
        send_g(g_all.at[SLOT[0, d]], SLOT[3, d], 1, 0)
        send_g(g_all.at[SLOT[0, d]], SLOT[1, d], 3, 0)
        got_h(d, 0)
        send_h(h_all.at[SLOT[d, 0]], SLOT[d, 3], 0, 1)
        send_h(h_all.at[SLOT[d, 0]], SLOT[d, 1], 0, 3)
    relay(1)
    relay(3)
    relay(2)
    got_g(0, 0)
    got_h(0, 0)

    def turn_g(start):
        for n in range(start, start + 4):
            block = jnp.concatenate([g_all[2 * n], g_all[2 * n + 1]], axis=0).astype(F32)
            g_t[:, n * 128 : (n + 1) * 128] = block.T

    turn_g(0)
    h_early = h_all[0:8].reshape(512, 256)

    def early(w, carry):
        left = (g_t[:, 0:512] * dmat[pl.ds(w, 1), 0:512]).astype(BF16)
        keep[w] = jnp.dot(left, h_early, preferred_element_type=F32)
        return carry

    lax.fori_loop(0, 8, early, 0)
    for d in range(4):
        got_g(2, d)
        got_h(d, 2)
    turn_g(4)
    sibling = device(x, y, z, 1 - core)
    mine = pl.ds(pl.multiple_of(core * 128, 128), 128)
    other = pl.ds(pl.multiple_of((1 - core) * 128, 128), 128)

    side = 2 * ((z + core) % 2) - 1
    partner = device(x, y, (z - side + 8) % 8, core)

    h_late = h_all[8:16].reshape(512, 256)

    def late(w, rows):
        left = [g_t[rows, 512:1024] * dmat[pl.ds(w + n, 1), 512:1024] for n in range(2)]
        left = jnp.concatenate(left, axis=0).astype(BF16)
        return jnp.dot(left, h_late, preferred_element_type=F32)

    def for_sibling(n, carry):
        first = 2 * n
        total = late(first, other)
        for m in range(2):
            w = first + m
            c_send[w] = (keep[w, other, :] + total[m * 128 : (m + 1) * 128, :]).astype(BF16)
            remote(c_send.at[w], c_recv.at[w], x_send, x_recv.at[w], sibling).start()
        return carry

    def both_cores(n, carry):
        first = 2 * n
        rest = late(first, mine)
        for m in range(2):
            w = first + m
            pltpu.make_async_copy(c_recv.at[w], c_recv.at[w], x_recv.at[w]).wait()
            total = keep[w, mine, :] + rest[m * 128 : (m + 1) * 128, :] + c_recv[w].astype(F32)
            both[w] = total
            for low in range(4):
                q_buf[w * 4 + low] = total[low * 32 : (low + 1) * 32, :].astype(BF16)
            for low in range(4):
                owner = m * 4 + low
                step = ((owner - z) * side + 8) % 8
                there = first * 2 + 7 - step
                copy = remote(q_buf.at[w * 4 + low], s_buf.at[there], s_send, s_recv.at[there], partner)
                pl.when(step >= 4)(copy.start)
        return carry

    lax.fori_loop(0, 4, for_sibling, 0)
    lax.fori_loop(0, 4, both_cores, 0)
    slot = (z + core) // 2 % 4 * 4 + x

    def deliver(n, carry):
        step = 3 - n % 4
        owner = (z + side * step + 8) % 8
        pair = n // 4
        w, low = pair * 2 + owner // 4, owner % 4
        here = pair * 4 + step
        pltpu.make_async_copy(s_buf.at[here], s_buf.at[here], s_recv.at[here]).wait()
        rows = pl.ds(pl.multiple_of(low * 32, 32), 32)
        f_buf[here] = (both[w, rows, :] + s_buf[here].astype(F32)).astype(BF16)
        target = low * 8 + y * 2 + core
        copy = remote(f_buf.at[here], r_buf.at[slot], r_send, r_recv, (w, target))
        local = pltpu.make_async_copy(f_buf.at[here], r_buf.at[slot], r_recv)
        own_block = jnp.logical_and(w == tm, target == sp)
        pl.when(own_block)(local.start)
        pl.when(jnp.logical_not(own_block))(copy.start)
        return carry

    lax.fori_loop(0, 16, deliver, 0)
    pltpu.make_async_copy(r_buf, r_buf, r_recv).wait()
    for n in range(4):
        total = r_buf[n].astype(F32)
        for m in range(1, 4):
            total += r_buf[m * 4 + n].astype(F32)
        width = 256 if n < 3 else 96
        out_ref[:, 0, n * 256 : n * 256 + width] = total[:27, :width]

    final = pltpu.make_async_copy(out_ref, out_any, l_sem.at[0])
    final.start()

    pltpu.make_async_copy(recv.at[pl.ds(0, 31)], recv.at[pl.ds(0, 31)], a_send).wait()
    pltpu.make_async_copy(t_all.at[pl.ds(0, 3)], t_all.at[pl.ds(0, 3)], t_send).wait()
    pltpu.make_async_copy(half_times, half_times, u_send).wait()
    pltpu.make_async_copy(g_all.at[pl.ds(0, 15)], g_all.at[pl.ds(0, 15)], g_send).wait()
    pltpu.make_async_copy(h_all.at[pl.ds(0, 15)], h_all.at[pl.ds(0, 15)], h_send).wait()
    pltpu.make_async_copy(c_send, c_send, x_send).wait()
    pltpu.make_async_copy(s_buf, s_buf, s_send).wait()
    final.wait()
    pltpu.make_async_copy(f_buf.at[pl.ds(0, 15)], f_buf.at[pl.ds(0, 15)], r_send).wait()


def local(orbitals, gaps, times, cos_weights):
    factors, columns, points = wave_tables()
    stay = lambda value: pltpu.with_memory_space_constraint(value, pltpu.HBM)
    dma = pltpu.SemaphoreType.DMA
    out = pl.pallas_call(
        kernel,
        out_shape=jax.ShapeDtypeStruct((27, 1, NG), F32),
        in_specs=[pl.BlockSpec(memory_space=pltpu.HBM)] * 7,
        out_specs=pl.BlockSpec(memory_space=pl.ANY),
        scratch_shapes=[
            pltpu.VMEM((27, 1, NG), F32),
            pltpu.VMEM((NOCC + NEMP,), F32),
            pltpu.SMEM((1,), F32),
            pltpu.VMEM((8, 8), F32),
            pltpu.VMEM((4, 1024), jnp.int32),
            pltpu.VMEM((1, 512), jnp.int32),
            pltpu.VMEM((320, 432), BF16),
            pltpu.VMEM((104, 1024), F32),
            pltpu.VMEM((40, 8, 512), BF16),
            pltpu.VMEM((32, 2, 8, 512), BF16),
            pltpu.VMEM((8, 128), F32),
            pltpu.VMEM((8, 8, 128), F32),
            pltpu.VMEM((144, 1024), F32),
            pltpu.VMEM((144, 1024), F32),
            pltpu.VMEM((8, 256, 1024), BF16),
            pltpu.VMEM((2, 1024, 1024), BF16),
            pltpu.VMEM((64, 512), F32),
            pltpu.VMEM((128, 512), F32),
            pltpu.VMEM((4, 64, 256), BF16),
            pltpu.VMEM((4, 64, 256), BF16),
            pltpu.VMEM((16, 64, 256), BF16),
            pltpu.VMEM((16, 64, 256), BF16),
            pltpu.VMEM((256, 1024), F32),
            pltpu.VMEM((8, 1024), F32),
            pltpu.VMEM((8, 128, 256), F32),
            pltpu.VMEM((8, 256, 256), F32),
            pltpu.VMEM((8, 128, 256), BF16),
            pltpu.VMEM((8, 128, 256), BF16),
            pltpu.VMEM((32, 32, 256), BF16),
            pltpu.VMEM((16, 32, 256), BF16),
            pltpu.VMEM((16, 32, 256), BF16),
            pltpu.VMEM((16, 32, 256), BF16),
            dma((8,)), dma, dma, dma, dma, dma,
            dma((16,)), dma, dma((16,)), dma,
            dma((3,)),
            dma((8,)), dma,
            dma((16,)), dma,
            dma, dma,
        ],
        compiler_params=pltpu.CompilerParams(has_side_effects=True, collective_id=0, vmem_limit_bytes=34 * 2**20),
    )(
        stay(orbitals.T), stay(gaps), times, stay(cos_weights),
        stay(jnp.asarray(factors)), stay(jnp.asarray(columns)), stay(jnp.asarray(points)),
    )
    return out.transpose(1, 0, 2)


def solution(mesh):
    return jax.shard_map(
        local,
        mesh=mesh,
        in_specs=(P("space", None), P(), P("tm"), P()),
        out_specs=P("tm", "space", None),
        check_vma=False,
    )
```

```python
import math

import jax
import jax.numpy as jnp
import numpy as np
from jax import lax
from jax.experimental import pallas as pl
from jax.experimental.pallas import tpu as pltpu
from jax.sharding import PartitionSpec as P

SIDE = 24
NG = 864
NOCC = 64
NEMP = 256
MESH = pl.DeviceIdType.MESH
F32 = jnp.float32
BF16 = jnp.bfloat16


def wave_tables():
    pos = np.arange(1024)
    group, m = pos // 128, pos % 128
    even = group < 4
    c_even = np.where(even, group % 2, (group - 4) // 2)
    trig = np.where(even, m // 54, group % 2)
    c = 1 + 2 * np.where(even, m // 18 % 3, m // 36) + c_even
    b = np.where(even, m // 3, m // 6) % 6 - 3
    a = np.where(even, 4 * (m % 3) - 4 - 2 * (group // 2), 2 * (m % 6) - 5)
    valid = m < 108
    natural = np.where(valid, (a + 6) + 12 * (b + 3) + 72 * (c - 1) + 432 * trig, -1)

    def factor(side, wave):
        step = np.mod(side[:, None] * wave[None, :], SIDE)
        angle = step * (2.0 * math.pi / SIDE)
        return np.cos(angle), np.sin(angle)

    x_cos, x_sin = factor(np.arange(8), a)
    y_cos, y_sin = factor(np.arange(24), b)
    y_first = np.where(trig == 0, y_cos, y_sin)
    y_second = np.where(trig == 0, y_sin, -y_cos)
    z_rows = np.concatenate([np.arange(8), np.tile(np.arange(8, 12), 2)])
    z_cos, z_sin = factor(z_rows, c)
    scaling = math.sqrt(2.0 / SIDE**3) * valid
    turn = np.where(a % 4 == 1, 1.0, -1.0) * np.ones((8, 1))
    factors = np.concatenate(
        [x_cos, x_sin, y_first, y_second, z_cos * scaling, z_sin * scaling, turn], axis=0
    ).astype(np.float32)

    where_natural = np.full(1024, -1, np.int32)
    where_natural[natural[valid]] = pos[valid]
    lane = np.arange(1024)
    block, core, low, row = lane // 256, lane // 128 % 2, lane // 32 % 4, lane % 32
    g = 27 * (low * 8 + block * 2 + core) + row
    where_g = np.where(row < 27, where_natural[np.minimum(g, NG - 1)], -1)
    offsets = np.repeat(np.array(OFFSETS), 64, axis=0).T
    columns = np.stack([where_g, where_natural, offsets[0], offsets[1]]).astype(np.int32)

    k = np.arange(256)
    tail = k - 144
    u = np.where(k < 144, k // 8, tail // 8 * 2 + tail % 8 // 4)
    z = np.where(k < 144, k % 8, 8 + tail % 4)
    inside = k < 216
    first = np.where(inside, u * 24 + z, -1)
    second = np.where(inside, u * 24 + 12 + z, -1)
    points = np.concatenate([first, second])[None, :].astype(np.int32)
    return factors, columns, points


OFFSETS = (
    (0, 0), (0, 1), (0, 3), (1, 0), (3, 0), (1, 1), (3, 3), (1, 3),
    (3, 1), (0, 2), (2, 0), (1, 2), (2, 1), (3, 2), (2, 3), (2, 2),
)
SLOT = {offset: n for n, offset in enumerate(OFFSETS)}
MIRROR = [SLOT[dy, dx] for dx, dy in OFFSETS]
FX, FXS, FY, FYS, FZ, FZS, FT = 0, 8, 16, 40, 64, 80, 96


def kernel(
    orb_hbm, gaps_hbm, times_hbm, cw_hbm, fac_hbm, col_hbm, pts_hbm, out_any,
    out_ref, gaps_ref, times_ref, cw_ref, col_ref, pts_ref, orb_ref, fac_ref,
    orb_p, recv, t_own, t_all, lead, quad, table, sel, acc, acc_odd, m_g, m_h, g_all, h_all,
    g_t, dmat, both, keep, c_send, c_recv, q_buf, s_buf, f_buf, r_buf,
    a_recv, a_send, e_send, t_recv, t_send, u_recv, u_send, b_recv, g_send, h_send, l_sem, x_recv, x_send, s_recv, s_send, r_recv, r_send,
):
    tm = lax.axis_index("tm")
    sp = lax.axis_index("space")
    x, zh = tm // 2, tm % 2
    zl, y, core = sp // 8, sp // 2 % 4, sp % 2
    z = zh * 4 + zl

    def device(xx, yy, zz, cc):
        return (xx * 2 + zz // 4, (zz % 4) * 8 + yy * 2 + cc)

    def remote(src, dst, send, recv_sem, target):
        return pltpu.make_async_remote_copy(
            src_ref=src, dst_ref=dst, send_sem=send, recv_sem=recv_sem,
            device_id=target, device_id_type=MESH,
        )

    load_orb = pltpu.make_async_copy(orb_hbm, orb_ref, l_sem.at[0])
    load_pts = pltpu.make_async_copy(pts_hbm, pts_ref, l_sem.at[1])
    load_orb.start()
    load_pts.start()
    loads = [
        pltpu.make_async_copy(src, dst, l_sem.at[2])
        for n, (src, dst) in enumerate((
            (fac_hbm, fac_ref), (col_hbm, col_ref), (gaps_hbm, gaps_ref), (cw_hbm, cw_ref), (times_hbm, times_ref),
        ))
    ]
    for load in loads:
        load.start()

    barrier = pltpu.get_barrier_semaphore()

    def greet(target):
        pl.semaphore_signal(barrier, inc=1, device_id=target, device_id_type=MESH)

    far = (z + 6 + 4 * core) % 8
    for dy in (2, 1, 3, 0):
        yy = (y + dy) % 4
        for cc in range(2):
            greet(device(x, yy, far, cc))
            greet(device(x, yy, (z + 1) % 8, cc))
            greet(device(x, yy, (z + 7) % 8, cc))
        if dy > 0:
            greet(device(x, yy, z, core))
        greet(device(x, yy, z, 1 - core))
    for dx in range(1, 4):
        greet(device((x + dx) % 4, y, z, core))
    greet(device(x, y, (z + 4) % 8, core))

    load_pts.wait()
    pick = lax.broadcasted_iota(jnp.int32, (432, 512), 0) == pts_ref[...]
    pick = jnp.where(pick, 1.0, 0.0).astype(BF16)
    load_orb.wait()
    moved = jnp.dot(orb_ref[...], pick, preferred_element_type=F32).astype(BF16)
    for n in range(40):
        orb_p[n] = moved[n * 8 : (n + 1) * 8, :]

    pl.semaphore_wait(barrier, 35)
    links = ((2, 0), (-2, 1), (1, 0), (-1, 1), (1, 1), (-1, 0), (0, 0), (0, 1))
    for dy, (dz, cc) in [(dy, link) for pair in ((1, 3), (2, 0)) for link in links for dy in pair]:
        yy, zz = (y + dy) % 4, (z + dz + 8) % 8
        blocks = (4 * cc + x, 8 + 4 * zz + yy)
        for part, block in enumerate(blocks):
            src, dst = orb_p.at[block], recv.at[sp, part]
            copy = remote(src, dst, a_send, a_recv.at[sp % 8], device(x, yy, zz, cc))
            local = pltpu.make_async_copy(src, dst, a_recv.at[sp % 8])
            if dz == 0 and dy == 0:
                pl.when(core == cc)(local.start)
                if part == 0:
                    pl.when(core != cc)(copy.start)
            elif part == 0:
                copy.start()
            else:
                pl.when(core == cc)(copy.start)
    for load in loads:
        load.wait()
    t_own[...] = jnp.full((8, 128), times_ref[0], F32)
    for dx in range(1, 4):
        remote(t_own, t_all.at[zh * 4 + x], t_send, t_recv, device((x + dx) % 4, y, z, core)).start()
    t_all[zh * 4 + x] = t_own[...]

    def lead_rows(xx, carry):
        cos = fac_ref[pl.ds(FX + xx, 1), :]
        sin = fac_ref[pl.ds(FXS + xx, 1), :]
        first, second = fac_ref[FY : FY + 24, :], fac_ref[FYS : FYS + 24, :]
        rows = pl.ds(pl.multiple_of(xx * 24, 8), 24)
        lead[rows, :] = cos * first - sin * second
        quad[rows, :] = sin * first + cos * second
        return carry

    lax.fori_loop(0, 6, lead_rows, 0)
    odd = lax.broadcasted_iota(jnp.int32, (8, 1024), 0) >= 4

    def table_rows(chunk, carry):
        base = chunk * 18

        def pair(v, inner):
            row = base + 2 * v
            a0, a1 = lead[pl.ds(row, 1), :], lead[pl.ds(row + 1, 1), :]
            b0, b1 = quad[pl.ds(row, 1), :], quad[pl.ds(row + 1, 1), :]
            cos, sin = fac_ref[FZ : FZ + 8, :], fac_ref[FZS : FZS + 8, :]
            both = jnp.concatenate([a0 * cos - b0 * sin, a1 * cos - b1 * sin], axis=0)
            table[chunk, pl.ds(pl.multiple_of(v * 16, 16), 16), :] = both.astype(BF16)
            return inner

        lax.fori_loop(0, 9, pair, 0)

        def tail(v):
            row = base + 2 * v
            a = jnp.where(odd, lead[pl.ds(row + 1, 1), :], lead[pl.ds(row, 1), :])
            b = jnp.where(odd, quad[pl.ds(row + 1, 1), :], quad[pl.ds(row, 1), :])
            return a * fac_ref[FZ + 8 : FZ + 16, :] - b * fac_ref[FZS + 8 : FZS + 16, :]

        def tails(w, inner):
            both = jnp.concatenate([tail(2 * w), tail(jnp.minimum(2 * w + 1, 8))], axis=0)
            table[chunk, pl.ds(pl.multiple_of(144 + w * 16, 16), 16), :] = both.astype(BF16)
            return inner

        lax.fori_loop(0, 5, tails, 0)
        table[chunk, 224:256, :] = jnp.zeros((32, 1024), BF16)
        return carry

    lax.fori_loop(0, 8, table_rows, 0)

    def select_rows(n, carry):
        rows = lax.broadcasted_iota(jnp.int32, (128, 1024), 0) + n * 128
        for side in range(2):
            hit = rows == col_ref[side : side + 1, :]
            sel[side, pl.ds(pl.multiple_of(n * 128, 128), 128), :] = jnp.where(hit, 1.0, 0.0).astype(BF16)
        return carry

    lax.fori_loop(0, 8, select_rows, 0)

    pltpu.make_async_copy(t_all.at[pl.ds(0, 3)], t_all.at[pl.ds(0, 3)], t_recv).wait()
    half_times = t_all.at[pl.ds(zh * 4, 4)]
    remote(half_times, half_times, u_send, u_recv, device(x, y, (z + 4) % 8, core)).start()

    acc[...] = jnp.zeros_like(acc)
    acc_odd[...] = jnp.zeros_like(acc_odd)

    def chunk_step(step, carry):
        turn = step // 4 * 2 + step % 2
        away = jnp.where(turn < 2, 2 * turn + 1, 6 - 2 * turn)
        passed = step // 2 % 2
        n = (y + away) % 4 * 2 + (core + passed) % 2
        pltpu.make_async_copy(recv.at[pl.ds(0, 4)], recv.at[pl.ds(0, 4)], a_recv.at[n]).wait()
        for quarter in range(4):
            block = recv.at[n + 8 * quarter, 1]
            pl.when(passed == 0)(remote(block, block, e_send, a_recv.at[n], device(x, y, z, 1 - core)).start)
        occupied = [recv[n + 8 * quarter, 0].astype(F32) for quarter in range(4)]
        empty = [recv[n + 8 * quarter, 1].astype(F32) for quarter in range(4)]
        minus, plus = ([], [], [], []), ([], [], [], [])
        for i in range(8):
            p = [o[i : i + 1, :] * e for o, e in zip(occupied, empty)]
            s0, s1, d0, d1 = p[0] + p[2], p[1] + p[3], p[0] - p[2], p[1] - p[3]
            for kind, value in enumerate((s0 + s1, s0 - s1, d0, d1)):
                minus[kind].append(value[:, :256] - value[:, 256:])
                plus[kind].append(value[:, :256] + value[:, 256:])

        def product(rows, start, width):
            left = jnp.concatenate(rows, axis=0).astype(BF16)
            return jnp.dot(left, table[n, :, start : start + width], preferred_element_type=F32)

        acc[:, 0:128] += product(minus[0], 0, 128)
        acc[:, 128:256] += product(plus[0], 128, 128)
        acc[:, 256:384] += product(minus[1], 256, 128)
        acc[:, 384:512] += product(plus[1], 384, 128)
        acc_odd[:, 0:256] += product(minus[2] + minus[3], 512, 256)
        acc_odd[:, 256:512] += product(plus[2] + plus[3], 768, 256)
        return carry

    lax.fori_loop(0, 8, chunk_step, 0)
    columns = [acc[...]]
    for part in range(2):
        at = part * 256
        sign = fac_ref[FT : FT + 1, 512 + at : 640 + at]
        u_cos, u_sin = acc_odd[0:64, at : at + 128], acc_odd[0:64, at + 128 : at + 256]
        v_cos, v_sin = acc_odd[64:128, at : at + 128], acc_odd[64:128, at + 128 : at + 256]
        columns += [u_cos - sign * v_sin, u_sin + sign * v_cos]
    m_all = jnp.concatenate(columns, axis=1).astype(BF16)
    for n in range(4):
        lanes = slice(n * 256, (n + 1) * 256)
        m_g[n] = jnp.dot(m_all, sel[0, :, lanes], preferred_element_type=F32).astype(BF16)
        m_h[n] = jnp.dot(m_all, sel[1, :, lanes], preferred_element_type=F32).astype(BF16)

    def send_g(src, to, dx, dy):
        target = device((x + dx) % 4, (y + dy) % 4, z, core)
        remote(src, g_all.at[to], g_send, b_recv.at[to], target).start()

    def send_h(src, to, dx, dy):
        target = device((x + dx) % 4, (y + dy) % 4, z, core)
        remote(src, h_all.at[to], h_send, b_recv.at[MIRROR[to]], target).start()

    for d in (2, 1, 3):
        send_g(m_g.at[(y + d) % 4], SLOT[0, 4 - d], 0, d)
        send_h(m_h.at[(x + d) % 4], SLOT[4 - d, 0], d, 0)
    for d in (2, 1, 3):
        send_g(m_g.at[y], SLOT[4 - d, 0], d, 0)
        send_h(m_h.at[x], SLOT[0, 4 - d], 0, d)
    pltpu.make_async_copy(m_g.at[y], g_all.at[0], b_recv.at[0]).start()
    pltpu.make_async_copy(m_h.at[x], h_all.at[0], b_recv.at[0]).start()

    pltpu.make_async_copy(half_times, half_times, u_recv).wait()
    pair_index = lax.broadcasted_iota(jnp.int32, (1, 1024), 1)
    which_i = 32 * core + 8 * ((col_ref[2:3, :] + x) % 4) + pair_index // 8 % 8
    which_a = NOCC + 32 * z + 8 * ((col_ref[3:4, :] + y) % 4) + pair_index % 8
    orbital = lax.broadcasted_iota(jnp.int32, (320, 1024), 0)
    hot_i = jnp.where(orbital == which_i, 1.0, 0.0).astype(F32)
    hot_a = jnp.where(orbital == which_a, 1.0, 0.0).astype(F32)
    gaps = jnp.broadcast_to(gaps_ref[...].reshape(1, 320), (8, 320))
    high = lax.Precision.HIGHEST
    gap_i = jnp.dot(gaps, hot_i, precision=high, preferred_element_type=F32)
    gap_a = jnp.dot(gaps, hot_a, precision=high, preferred_element_type=F32)
    sub = lax.broadcasted_iota(jnp.int32, (8, 128), 0)
    tcol = jnp.zeros((8, 128), F32)
    for n in range(8):
        tcol = jnp.where(sub == n, t_all[n % 2 * 4 + n // 2], tcol)
    tcol = tcol[:, 0:1]
    decay = jnp.exp(-gap_i * tcol) * jnp.exp(-gap_a * tcol) * (NOCC**-0.5 * NEMP**-0.5)
    dmat[...] = jnp.dot(cw_ref[...], decay, precision=high, preferred_element_type=F32)

    def got(dx, dy):
        pltpu.make_async_copy(g_all.at[pl.ds(0, 2)], g_all.at[pl.ds(0, 2)], b_recv.at[SLOT[dx, dy]]).wait()

    def relay(d):
        up_g, up_h = (y + d) % 4 < 2, (x + d) % 4 < 2
        got(3, d)
        pl.when(up_g)(lambda: send_g(g_all.at[SLOT[3, d]], SLOT[2, d], 1, 0))
        pl.when(up_h)(lambda: send_h(h_all.at[SLOT[d, 3]], SLOT[d, 2], 0, 1))
        got(1, d)
        pl.when(jnp.logical_not(up_g))(lambda: send_g(g_all.at[SLOT[1, d]], SLOT[2, d], 3, 0))
        pl.when(jnp.logical_not(up_h))(lambda: send_h(h_all.at[SLOT[d, 1]], SLOT[d, 2], 0, 3))

    for d in (1, 3, 2):
        got(0, d)
        send_g(g_all.at[SLOT[0, d]], SLOT[3, d], 1, 0)
        send_g(g_all.at[SLOT[0, d]], SLOT[1, d], 3, 0)
        send_h(h_all.at[SLOT[d, 0]], SLOT[d, 3], 0, 1)
        send_h(h_all.at[SLOT[d, 0]], SLOT[d, 1], 0, 3)
    relay(1)
    relay(3)
    relay(2)
    for d in (0, 1, 3):
        got(d, 0)

    def turn_g(start):
        for n in range(start, start + 4):
            block = jnp.concatenate([g_all[2 * n], g_all[2 * n + 1]], axis=0).astype(F32)
            g_t[:, n * 128 : (n + 1) * 128] = block.T

    turn_g(0)
    h_early = h_all[0:8].reshape(512, 256)

    def early(w, carry):
        left = (g_t[:, 0:512] * dmat[pl.ds(w, 1), 0:512]).astype(BF16)
        keep[w] = jnp.dot(left, h_early, preferred_element_type=F32)
        return carry

    lax.fori_loop(0, 8, early, 0)
    for d in range(4):
        got(2, d)
    turn_g(4)
    sibling = device(x, y, z, 1 - core)
    mine = pl.ds(pl.multiple_of(core * 128, 128), 128)
    other = pl.ds(pl.multiple_of((1 - core) * 128, 128), 128)

    side = 2 * ((z + core) % 2) - 1
    partner = device(x, y, (z - side + 8) % 8, core)

    h_late = h_all[8:16].reshape(512, 256)

    def late(w, rows):
        left = [g_t[rows, 512:1024] * dmat[pl.ds(w + n, 1), 512:1024] for n in range(2)]
        left = jnp.concatenate(left, axis=0).astype(BF16)
        return jnp.dot(left, h_late, preferred_element_type=F32)

    def for_sibling(n, carry):
        first = 2 * n
        total = late(first, other)
        for m in range(2):
            w = first + m
            c_send[w] = (keep[w, other, :] + total[m * 128 : (m + 1) * 128, :]).astype(BF16)
            remote(c_send.at[w], c_recv.at[w], x_send, x_recv.at[n], sibling).start()
        return carry

    def both_cores(n, carry):
        first = 2 * n
        rest = late(first, mine)
        for m in range(2):
            w = first + m
            if m == 0:
                two = c_recv.at[pl.ds(0, 2)]
                pltpu.make_async_copy(two, two, x_recv.at[n]).wait()
            total = keep[w, mine, :] + rest[m * 128 : (m + 1) * 128, :] + c_recv[w].astype(F32)
            both[w] = total
            for low in range(4):
                q_buf[w * 4 + low] = total[low * 32 : (low + 1) * 32, :].astype(BF16)
            for low in range(4):
                owner = m * 4 + low
                step = ((owner - z) * side + 8) % 8
                there = first * 2 + 7 - step
                copy = remote(q_buf.at[w * 4 + low], s_buf.at[there], s_send, s_recv.at[there], partner)
                pl.when(step >= 4)(copy.start)
        return carry

    lax.fori_loop(0, 4, for_sibling, 0)
    lax.fori_loop(0, 4, both_cores, 0)
    slot = (z + core) // 2 % 4 * 4 + x

    def deliver(n, carry):
        step = 3 - n % 4
        owner = (z + side * step + 8) % 8
        pair = n // 4
        w, low = pair * 2 + owner // 4, owner % 4
        here = pair * 4 + step
        pltpu.make_async_copy(s_buf.at[here], s_buf.at[here], s_recv.at[here]).wait()
        rows = pl.ds(pl.multiple_of(low * 32, 32), 32)
        f_buf[here] = (both[w, rows, :] + s_buf[here].astype(F32)).astype(BF16)
        target = low * 8 + y * 2 + core
        copy = remote(f_buf.at[here], r_buf.at[slot], r_send, r_recv, (w, target))
        local = pltpu.make_async_copy(f_buf.at[here], r_buf.at[slot], r_recv)
        own_block = jnp.logical_and(w == tm, target == sp)
        pl.when(own_block)(local.start)
        pl.when(jnp.logical_not(own_block))(copy.start)
        return carry

    lax.fori_loop(0, 16, deliver, 0)
    pltpu.make_async_copy(r_buf, r_buf, r_recv).wait()
    for n in range(4):
        total = r_buf[n].astype(F32)
        for m in range(1, 4):
            total += r_buf[m * 4 + n].astype(F32)
        width = 256 if n < 3 else 96
        out_ref[:, 0, n * 256 : n * 256 + width] = total[:27, :width]

    final = pltpu.make_async_copy(out_ref, out_any, l_sem.at[0])
    final.start()

    pltpu.make_async_copy(recv.at[pl.ds(0, 23)], recv.at[pl.ds(0, 23)], a_send).wait()
    pltpu.make_async_copy(recv.at[pl.ds(0, 8)], recv.at[pl.ds(0, 8)], e_send).wait()
    pltpu.make_async_copy(t_all.at[pl.ds(0, 3)], t_all.at[pl.ds(0, 3)], t_send).wait()
    pltpu.make_async_copy(half_times, half_times, u_send).wait()
    pltpu.make_async_copy(g_all.at[pl.ds(0, 15)], g_all.at[pl.ds(0, 15)], g_send).wait()
    pltpu.make_async_copy(h_all.at[pl.ds(0, 15)], h_all.at[pl.ds(0, 15)], h_send).wait()
    pltpu.make_async_copy(c_send, c_send, x_send).wait()
    pltpu.make_async_copy(s_buf, s_buf, s_send).wait()
    final.wait()
    pltpu.make_async_copy(f_buf.at[pl.ds(0, 15)], f_buf.at[pl.ds(0, 15)], r_send).wait()


def local(orbitals, gaps, times, cos_weights):
    factors, columns, points = wave_tables()
    stay = lambda value: pltpu.with_memory_space_constraint(value, pltpu.HBM)
    dma = pltpu.SemaphoreType.DMA
    out = pl.pallas_call(
        kernel,
        out_shape=jax.ShapeDtypeStruct((27, 1, NG), F32),
        in_specs=[pl.BlockSpec(memory_space=pltpu.HBM)] * 7,
        out_specs=pl.BlockSpec(memory_space=pl.ANY),
        scratch_shapes=[
            pltpu.VMEM((27, 1, NG), F32),
            pltpu.VMEM((NOCC + NEMP,), F32),
            pltpu.SMEM((1,), F32),
            pltpu.VMEM((8, 8), F32),
            pltpu.VMEM((4, 1024), jnp.int32),
            pltpu.VMEM((1, 512), jnp.int32),
            pltpu.VMEM((320, 432), BF16),
            pltpu.VMEM((104, 1024), F32),
            pltpu.VMEM((40, 8, 512), BF16),
            pltpu.VMEM((32, 2, 8, 512), BF16),
            pltpu.VMEM((8, 128), F32),
            pltpu.VMEM((8, 8, 128), F32),
            pltpu.VMEM((144, 1024), F32),
            pltpu.VMEM((144, 1024), F32),
            pltpu.VMEM((8, 256, 1024), BF16),
            pltpu.VMEM((2, 1024, 1024), BF16),
            pltpu.VMEM((64, 512), F32),
            pltpu.VMEM((128, 512), F32),
            pltpu.VMEM((4, 64, 256), BF16),
            pltpu.VMEM((4, 64, 256), BF16),
            pltpu.VMEM((16, 64, 256), BF16),
            pltpu.VMEM((16, 64, 256), BF16),
            pltpu.VMEM((256, 1024), F32),
            pltpu.VMEM((8, 1024), F32),
            pltpu.VMEM((8, 128, 256), F32),
            pltpu.VMEM((8, 256, 256), F32),
            pltpu.VMEM((8, 128, 256), BF16),
            pltpu.VMEM((8, 128, 256), BF16),
            pltpu.VMEM((32, 32, 256), BF16),
            pltpu.VMEM((16, 32, 256), BF16),
            pltpu.VMEM((16, 32, 256), BF16),
            pltpu.VMEM((16, 32, 256), BF16),
            dma((8,)), dma, dma, dma, dma, dma, dma,
            dma((16,)), dma, dma,
            dma((3,)),
            dma((4,)), dma,
            dma((16,)), dma,
            dma, dma,
        ],
        compiler_params=pltpu.CompilerParams(has_side_effects=True, collective_id=0, vmem_limit_bytes=34 * 2**20),
    )(
        stay(orbitals.T), stay(gaps), times, stay(cos_weights),
        stay(jnp.asarray(factors)), stay(jnp.asarray(columns)), stay(jnp.asarray(points)),
    )
    return out.transpose(1, 0, 2)


def solution(mesh):
    return jax.shard_map(
        local,
        mesh=mesh,
        in_specs=(P("space", None), P(), P("tm"), P()),
        out_specs=P("tm", "space", None),
        check_vma=False,
    )
```

```python
import math

import jax
import jax.numpy as jnp
import numpy as np
from jax import lax
from jax.experimental import pallas as pl
from jax.experimental.pallas import tpu as pltpu
from jax.sharding import PartitionSpec as P

SIDE = 24
NG = 864
NOCC = 64
NEMP = 256
MESH = pl.DeviceIdType.MESH
F32 = jnp.float32
BF16 = jnp.bfloat16


def wave_tables():
    pos = np.arange(1024)
    group, m = pos // 128, pos % 128
    even = group < 4
    c_even = np.where(even, group % 2, (group - 4) // 2)
    trig = np.where(even, m // 54, group % 2)
    c = 1 + 2 * np.where(even, m // 18 % 3, m // 36) + c_even
    b = np.where(even, m // 3, m // 6) % 6 - 3
    a = np.where(even, 4 * (m % 3) - 4 - 2 * (group // 2), 2 * (m % 6) - 5)
    valid = m < 108
    natural = np.where(valid, (a + 6) + 12 * (b + 3) + 72 * (c - 1) + 432 * trig, -1)

    def factor(side, wave):
        step = np.mod(side[:, None] * wave[None, :], SIDE)
        angle = step * (2.0 * math.pi / SIDE)
        return np.cos(angle), np.sin(angle)

    x_cos, x_sin = factor(np.arange(8), a)
    y_cos, y_sin = factor(np.arange(24), b)
    y_first = np.where(trig == 0, y_cos, y_sin)
    y_second = np.where(trig == 0, y_sin, -y_cos)
    z_rows = np.concatenate([np.arange(8), np.tile(np.arange(8, 12), 2)])
    z_cos, z_sin = factor(z_rows, c)
    scaling = math.sqrt(2.0 / SIDE**3) * valid
    turn = np.where(a % 4 == 1, 1.0, -1.0) * np.ones((8, 1))
    factors = np.concatenate(
        [x_cos, x_sin, y_first, y_second, z_cos * scaling, z_sin * scaling, turn], axis=0
    ).astype(np.float32)

    where_natural = np.full(1024, -1, np.int32)
    where_natural[natural[valid]] = pos[valid]
    lane = np.arange(1024)
    block, core, low, row = lane // 256, lane // 128 % 2, lane // 32 % 4, lane % 32
    g = 27 * (low * 8 + block * 2 + core) + row
    where_g = np.where(row < 27, where_natural[np.minimum(g, NG - 1)], -1)
    offsets = np.repeat(np.array(OFFSETS), 64, axis=0).T
    columns = np.stack([where_g, where_natural, offsets[0], offsets[1]]).astype(np.int32)

    k = np.arange(256)
    tail = k - 144
    u = np.where(k < 144, k // 8, tail // 8 * 2 + tail % 8 // 4)
    z = np.where(k < 144, k % 8, 8 + tail % 4)
    inside = k < 216
    first = np.where(inside, u * 24 + z, -1)
    second = np.where(inside, u * 24 + 12 + z, -1)
    points = np.concatenate([first, second])[None, :].astype(np.int32)
    return factors, columns, points


OFFSETS = (
    (0, 0), (0, 1), (0, 3), (1, 0), (3, 0), (1, 1), (3, 3), (1, 3),
    (3, 1), (0, 2), (2, 0), (1, 2), (2, 1), (3, 2), (2, 3), (2, 2),
)
SLOT = {offset: n for n, offset in enumerate(OFFSETS)}
MIRROR = [SLOT[dy, dx] for dx, dy in OFFSETS]
FX, FXS, FY, FYS, FZ, FZS, FT = 0, 8, 16, 40, 64, 80, 96


def kernel(
    orb_hbm, gaps_hbm, times_hbm, cw_hbm, fac_hbm, col_hbm, pts_hbm, out_any,
    out_ref, gaps_ref, times_ref, cw_ref, col_ref, pts_ref, orb_ref, fac_ref,
    orb_p, recv, t_own, t_all, lead, quad, table, sel, acc, acc_odd, m_g, m_h, g_all, h_all,
    g_t, dmat, both, keep, c_send, c_recv, q_buf, s_buf, f_buf, r_buf,
    a_recv, a_send, e_send, t_recv, t_send, u_recv, u_send, b_recv, g_send, h_send, l_sem, x_recv, x_send, s_recv, s_send, r_recv, r_send,
):
    tm = lax.axis_index("tm")
    sp = lax.axis_index("space")
    x, zh = tm // 2, tm % 2
    zl, y, core = sp // 8, sp // 2 % 4, sp % 2
    z = zh * 4 + zl

    def device(xx, yy, zz, cc):
        return (xx * 2 + zz // 4, (zz % 4) * 8 + yy * 2 + cc)

    def remote(src, dst, send, recv_sem, target):
        return pltpu.make_async_remote_copy(
            src_ref=src, dst_ref=dst, send_sem=send, recv_sem=recv_sem,
            device_id=target, device_id_type=MESH,
        )

    load_orb = pltpu.make_async_copy(orb_hbm, orb_ref, l_sem.at[0])
    load_pts = pltpu.make_async_copy(pts_hbm, pts_ref, l_sem.at[1])
    load_orb.start()
    load_pts.start()
    loads = [
        pltpu.make_async_copy(src, dst, l_sem.at[2])
        for n, (src, dst) in enumerate((
            (fac_hbm, fac_ref), (col_hbm, col_ref), (gaps_hbm, gaps_ref), (cw_hbm, cw_ref), (times_hbm, times_ref),
        ))
    ]
    for load in loads:
        load.start()

    barrier = pltpu.get_barrier_semaphore()

    def greet(target):
        pl.semaphore_signal(barrier, inc=1, device_id=target, device_id_type=MESH)

    far = (z + 6 + 4 * core) % 8
    greet(device(x, y, (z + 4) % 8, core))
    for dy in (2, 1, 3, 0):
        yy = (y + dy) % 4
        for cc in range(2):
            greet(device(x, yy, far, cc))
            greet(device(x, yy, (z + 1) % 8, cc))
            greet(device(x, yy, (z + 7) % 8, cc))
        if dy > 0:
            greet(device(x, yy, z, core))
        greet(device(x, yy, z, 1 - core))
    for dx in range(1, 4):
        greet(device((x + dx) % 4, y, z, core))

    load_pts.wait()
    pick = lax.broadcasted_iota(jnp.int32, (432, 512), 0) == pts_ref[...]
    pick = jnp.where(pick, 1.0, 0.0).astype(BF16)
    load_orb.wait()
    moved = jnp.dot(orb_ref[...], pick, preferred_element_type=F32).astype(BF16)
    for n in range(40):
        orb_p[n] = moved[n * 8 : (n + 1) * 8, :]

    pl.semaphore_wait(barrier, 35)
    links = ((2, 0), (-2, 1), (1, 0), (-1, 1), (1, 1), (-1, 0), (0, 0), (0, 1))
    for dy, (dz, cc) in [(dy, link) for pair in ((1, 3), (2, 0)) for link in links for dy in pair]:
        yy, zz = (y + dy) % 4, (z + dz + 8) % 8
        blocks = (4 * cc + x, 8 + 4 * zz + yy)
        for part, block in enumerate(blocks):
            src, dst = orb_p.at[block], recv.at[sp, part]
            copy = remote(src, dst, a_send, a_recv.at[sp % 8], device(x, yy, zz, cc))
            local = pltpu.make_async_copy(src, dst, a_recv.at[sp % 8])
            if dz == 0 and dy == 0:
                pl.when(core == cc)(local.start)
                if part == 0:
                    pl.when(core != cc)(copy.start)
            elif part == 0:
                copy.start()
            else:
                pl.when(core == cc)(copy.start)
    for load in loads:
        load.wait()
    t_own[...] = jnp.full((8, 128), times_ref[0], F32)
    for dx in range(1, 4):
        remote(t_own, t_all.at[zh * 4 + x], t_send, t_recv, device((x + dx) % 4, y, z, core)).start()
    t_all[zh * 4 + x] = t_own[...]

    def lead_rows(xx, carry):
        cos = fac_ref[pl.ds(FX + xx, 1), :]
        sin = fac_ref[pl.ds(FXS + xx, 1), :]
        first, second = fac_ref[FY : FY + 24, :], fac_ref[FYS : FYS + 24, :]
        rows = pl.ds(pl.multiple_of(xx * 24, 8), 24)
        lead[rows, :] = cos * first - sin * second
        quad[rows, :] = sin * first + cos * second
        return carry

    lax.fori_loop(0, 6, lead_rows, 0)
    odd = lax.broadcasted_iota(jnp.int32, (8, 1024), 0) >= 4

    def table_rows(chunk, carry):
        base = chunk * 18

        def pair(v, inner):
            row = base + 2 * v
            a0, a1 = lead[pl.ds(row, 1), :], lead[pl.ds(row + 1, 1), :]
            b0, b1 = quad[pl.ds(row, 1), :], quad[pl.ds(row + 1, 1), :]
            cos, sin = fac_ref[FZ : FZ + 8, :], fac_ref[FZS : FZS + 8, :]
            both = jnp.concatenate([a0 * cos - b0 * sin, a1 * cos - b1 * sin], axis=0)
            table[chunk, pl.ds(pl.multiple_of(v * 16, 16), 16), :] = both.astype(BF16)
            return inner

        lax.fori_loop(0, 9, pair, 0)

        def tail(v):
            row = base + 2 * v
            a = jnp.where(odd, lead[pl.ds(row + 1, 1), :], lead[pl.ds(row, 1), :])
            b = jnp.where(odd, quad[pl.ds(row + 1, 1), :], quad[pl.ds(row, 1), :])
            return a * fac_ref[FZ + 8 : FZ + 16, :] - b * fac_ref[FZS + 8 : FZS + 16, :]

        def tails(w, inner):
            both = jnp.concatenate([tail(2 * w), tail(jnp.minimum(2 * w + 1, 8))], axis=0)
            table[chunk, pl.ds(pl.multiple_of(144 + w * 16, 16), 16), :] = both.astype(BF16)
            return inner

        lax.fori_loop(0, 5, tails, 0)
        table[chunk, 224:256, :] = jnp.zeros((32, 1024), BF16)
        return carry

    lax.fori_loop(0, 8, table_rows, 0)

    def select_rows(n, carry):
        rows = lax.broadcasted_iota(jnp.int32, (128, 1024), 0) + n * 128
        for side in range(2):
            hit = rows == col_ref[side : side + 1, :]
            sel[side, pl.ds(pl.multiple_of(n * 128, 128), 128), :] = jnp.where(hit, 1.0, 0.0).astype(BF16)
        return carry

    lax.fori_loop(0, 8, select_rows, 0)

    pltpu.make_async_copy(t_all.at[pl.ds(0, 3)], t_all.at[pl.ds(0, 3)], t_recv).wait()
    half_times = t_all.at[pl.ds(zh * 4, 4)]
    remote(half_times, half_times, u_send, u_recv, device(x, y, (z + 4) % 8, core)).start()

    acc[...] = jnp.zeros_like(acc)
    acc_odd[...] = jnp.zeros_like(acc_odd)

    def chunk_step(step, carry):
        turn = step // 4 * 2 + step % 2
        away = jnp.where(turn < 2, 2 * turn + 1, 6 - 2 * turn)
        passed = step // 2 % 2
        n = (y + away) % 4 * 2 + (core + passed) % 2
        pltpu.make_async_copy(recv.at[pl.ds(0, 4)], recv.at[pl.ds(0, 4)], a_recv.at[n]).wait()
        for quarter in range(4):
            block = recv.at[n + 8 * quarter, 1]
            pl.when(passed == 0)(remote(block, block, e_send, a_recv.at[n], device(x, y, z, 1 - core)).start)
        occupied = [recv[n + 8 * quarter, 0].astype(F32) for quarter in range(4)]
        empty = [recv[n + 8 * quarter, 1].astype(F32) for quarter in range(4)]
        minus, plus = ([], [], [], []), ([], [], [], [])
        for i in range(8):
            p = [o[i : i + 1, :] * e for o, e in zip(occupied, empty)]
            s0, s1, d0, d1 = p[0] + p[2], p[1] + p[3], p[0] - p[2], p[1] - p[3]
            for kind, value in enumerate((s0 + s1, s0 - s1, d0, d1)):
                minus[kind].append(value[:, :256] - value[:, 256:])
                plus[kind].append(value[:, :256] + value[:, 256:])

        def product(rows, start, width):
            left = jnp.concatenate(rows, axis=0).astype(BF16)
            return jnp.dot(left, table[n, :, start : start + width], preferred_element_type=F32)

        acc[:, 0:128] += product(minus[0], 0, 128)
        acc[:, 128:256] += product(plus[0], 128, 128)
        acc[:, 256:384] += product(minus[1], 256, 128)
        acc[:, 384:512] += product(plus[1], 384, 128)
        acc_odd[:, 0:256] += product(minus[2] + minus[3], 512, 256)
        acc_odd[:, 256:512] += product(plus[2] + plus[3], 768, 256)
        return carry

    lax.fori_loop(0, 8, chunk_step, 0)
    columns = [acc[...]]
    for part in range(2):
        at = part * 256
        sign = fac_ref[FT : FT + 1, 512 + at : 640 + at]
        u_cos, u_sin = acc_odd[0:64, at : at + 128], acc_odd[0:64, at + 128 : at + 256]
        v_cos, v_sin = acc_odd[64:128, at : at + 128], acc_odd[64:128, at + 128 : at + 256]
        columns += [u_cos - sign * v_sin, u_sin + sign * v_cos]
    m_all = jnp.concatenate(columns, axis=1).astype(BF16)
    for n in range(4):
        lanes = slice(n * 256, (n + 1) * 256)
        m_g[n] = jnp.dot(m_all, sel[0, :, lanes], preferred_element_type=F32).astype(BF16).reshape(2, 32, 256)
        m_h[n] = jnp.dot(m_all, sel[1, :, lanes], preferred_element_type=F32).astype(BF16).reshape(2, 32, 256)

    def send_g(src, to, dx, dy, half):
        target = device((x + dx) % 4, (y + dy) % 4, z, core)
        remote(src.at[half], g_all.at[to, half], g_send, b_recv.at[to, half], target).start()

    def send_h(src, to, dx, dy, half):
        target = device((x + dx) % 4, (y + dy) % 4, z, core)
        remote(src.at[half], h_all.at[to, half], h_send, b_recv.at[MIRROR[to], half], target).start()

    for half in range(2):
        for d in (2, 1, 3):
            send_g(m_g.at[(y + d) % 4], SLOT[0, 4 - d], 0, d, half)
            send_h(m_h.at[(x + d) % 4], SLOT[4 - d, 0], d, 0, half)
    for half in range(2):
        for d in (1, 3, 2):
            send_g(m_g.at[y], SLOT[4 - d, 0], d, 0, half)
            send_h(m_h.at[x], SLOT[0, 4 - d], 0, d, half)
    for half in range(2):
        pltpu.make_async_copy(m_g.at[y, half], g_all.at[0, half], b_recv.at[0, half]).start()
        pltpu.make_async_copy(m_h.at[x, half], h_all.at[0, half], b_recv.at[0, half]).start()

    pltpu.make_async_copy(half_times, half_times, u_recv).wait()
    pair_index = lax.broadcasted_iota(jnp.int32, (1, 1024), 1)
    which_i = 32 * core + 8 * ((col_ref[2:3, :] + x) % 4) + pair_index // 8 % 8
    which_a = NOCC + 32 * z + 8 * ((col_ref[3:4, :] + y) % 4) + pair_index % 8
    orbital = lax.broadcasted_iota(jnp.int32, (320, 1024), 0)
    hot_i = jnp.where(orbital == which_i, 1.0, 0.0).astype(F32)
    hot_a = jnp.where(orbital == which_a, 1.0, 0.0).astype(F32)
    gaps = jnp.broadcast_to(gaps_ref[...].reshape(1, 320), (8, 320))
    high = lax.Precision.HIGHEST
    gap_i = jnp.dot(gaps, hot_i, precision=high, preferred_element_type=F32)
    gap_a = jnp.dot(gaps, hot_a, precision=high, preferred_element_type=F32)
    sub = lax.broadcasted_iota(jnp.int32, (8, 128), 0)
    tcol = jnp.zeros((8, 128), F32)
    for n in range(8):
        tcol = jnp.where(sub == n, t_all[n % 2 * 4 + n // 2], tcol)
    tcol = tcol[:, 0:1]
    decay = jnp.exp(-gap_i * tcol) * jnp.exp(-gap_a * tcol) * (NOCC**-0.5 * NEMP**-0.5)
    dmat[...] = jnp.dot(cw_ref[...], decay, precision=high, preferred_element_type=F32)

    def got(dx, dy, half):
        pltpu.make_async_copy(g_all.at[0], g_all.at[0], b_recv.at[SLOT[dx, dy], half]).wait()

    def relay(d, half):
        up_g, up_h = (y + d) % 4 < 2, (x + d) % 4 < 2
        got(3, d, half)
        pl.when(up_g)(lambda: send_g(g_all.at[SLOT[3, d]], SLOT[2, d], 1, 0, half))
        pl.when(up_h)(lambda: send_h(h_all.at[SLOT[d, 3]], SLOT[d, 2], 0, 1, half))
        got(1, d, half)
        pl.when(jnp.logical_not(up_g))(lambda: send_g(g_all.at[SLOT[1, d]], SLOT[2, d], 3, 0, half))
        pl.when(jnp.logical_not(up_h))(lambda: send_h(h_all.at[SLOT[d, 1]], SLOT[d, 2], 0, 3, half))

    for d, half in ((1, 0), (3, 0), (2, 0), (1, 1), (3, 1), (2, 1)):
        got(0, d, half)
        send_g(g_all.at[SLOT[0, d]], SLOT[3, d], 1, 0, half)
        send_g(g_all.at[SLOT[0, d]], SLOT[1, d], 3, 0, half)
        send_h(h_all.at[SLOT[d, 0]], SLOT[d, 3], 0, 1, half)
        send_h(h_all.at[SLOT[d, 0]], SLOT[d, 1], 0, 3, half)
    for d in (1, 3, 2):
        for half in range(2):
            relay(d, half)
    for d in (0, 1, 3):
        for half in range(2):
            got(d, 0, half)

    def turn_g(start):
        for n in range(start, start + 4):
            block = g_all[2 * n : 2 * n + 2].reshape(128, 256).astype(F32)
            g_t[:, n * 128 : (n + 1) * 128] = block.T

    turn_g(0)
    h_early = h_all[0:8].reshape(512, 256)

    def early(w, carry):
        left = (g_t[:, 0:512] * dmat[pl.ds(w, 1), 0:512]).astype(BF16)
        keep[w] = jnp.dot(left, h_early, preferred_element_type=F32)
        return carry

    lax.fori_loop(0, 8, early, 0)
    for d in range(4):
        for half in range(2):
            got(2, d, half)
    turn_g(4)
    sibling = device(x, y, z, 1 - core)
    mine = pl.ds(pl.multiple_of(core * 128, 128), 128)
    other = pl.ds(pl.multiple_of((1 - core) * 128, 128), 128)

    side = 2 * ((z + core) % 2) - 1
    partner = device(x, y, (z - side + 8) % 8, core)

    h_late = h_all[8:16].reshape(512, 256)

    def late(w, rows):
        left = [g_t[rows, 512:1024] * dmat[pl.ds(w + n, 1), 512:1024] for n in range(2)]
        left = jnp.concatenate(left, axis=0).astype(BF16)
        return jnp.dot(left, h_late, preferred_element_type=F32)

    def pair_of(n):
        return (x + jnp.where(n == 0, 1, jnp.where(n == 1, 3, jnp.where(n == 2, 2, 0)))) % 4

    def for_sibling(n, carry):
        first = 2 * pair_of(n)
        total = late(first, other)
        for m in range(2):
            w = first + m
            c_send[w] = (keep[w, other, :] + total[m * 128 : (m + 1) * 128, :]).astype(BF16)
            remote(c_send.at[w], c_recv.at[w], x_send, x_recv.at[n], sibling).start()
        return carry

    def both_cores(n, carry):
        first = 2 * pair_of(n)
        rest = late(first, mine)
        for m in range(2):
            w = first + m
            if m == 0:
                two = c_recv.at[pl.ds(0, 2)]
                pltpu.make_async_copy(two, two, x_recv.at[n]).wait()
            total = keep[w, mine, :] + rest[m * 128 : (m + 1) * 128, :] + c_recv[w].astype(F32)
            both[w] = total
            for low in range(4):
                q_buf[w * 4 + low] = total[low * 32 : (low + 1) * 32, :].astype(BF16)
            for low in range(4):
                owner = m * 4 + low
                step = ((owner - z) * side + 8) % 8
                there = first * 2 + 7 - step
                copy = remote(q_buf.at[w * 4 + low], s_buf.at[there], s_send, s_recv.at[there], partner)
                pl.when(step >= 4)(copy.start)
        return carry

    lax.fori_loop(0, 4, for_sibling, 0)
    lax.fori_loop(0, 4, both_cores, 0)
    slot = (z + core) // 2 % 4 * 4 + x

    def deliver(n, carry):
        step = 3 - n % 4
        owner = (z + side * step + 8) % 8
        pair = pair_of(n // 4)
        w, low = pair * 2 + owner // 4, owner % 4
        here = pair * 4 + step
        pltpu.make_async_copy(s_buf.at[here], s_buf.at[here], s_recv.at[here]).wait()
        rows = pl.ds(pl.multiple_of(low * 32, 32), 32)
        f_buf[here] = (both[w, rows, :] + s_buf[here].astype(F32)).astype(BF16)
        target = low * 8 + y * 2 + core
        copy = remote(f_buf.at[here], r_buf.at[slot], r_send, r_recv, (w, target))
        local = pltpu.make_async_copy(f_buf.at[here], r_buf.at[slot], r_recv)
        own_block = jnp.logical_and(w == tm, target == sp)
        pl.when(own_block)(local.start)
        pl.when(jnp.logical_not(own_block))(copy.start)
        return carry

    lax.fori_loop(0, 16, deliver, 0)
    pltpu.make_async_copy(r_buf, r_buf, r_recv).wait()
    for n in range(4):
        total = r_buf[n].astype(F32)
        for m in range(1, 4):
            total += r_buf[m * 4 + n].astype(F32)
        width = 256 if n < 3 else 96
        out_ref[:, 0, n * 256 : n * 256 + width] = total[:27, :width]

    final = pltpu.make_async_copy(out_ref, out_any, l_sem.at[0])
    final.start()

    pltpu.make_async_copy(recv.at[pl.ds(0, 23)], recv.at[pl.ds(0, 23)], a_send).wait()
    pltpu.make_async_copy(recv.at[pl.ds(0, 8)], recv.at[pl.ds(0, 8)], e_send).wait()
    pltpu.make_async_copy(t_all.at[pl.ds(0, 3)], t_all.at[pl.ds(0, 3)], t_send).wait()
    pltpu.make_async_copy(half_times, half_times, u_send).wait()
    pltpu.make_async_copy(g_all.at[pl.ds(0, 15)], g_all.at[pl.ds(0, 15)], g_send).wait()
    pltpu.make_async_copy(h_all.at[pl.ds(0, 15)], h_all.at[pl.ds(0, 15)], h_send).wait()
    pltpu.make_async_copy(c_send, c_send, x_send).wait()
    pltpu.make_async_copy(s_buf, s_buf, s_send).wait()
    final.wait()
    pltpu.make_async_copy(f_buf.at[pl.ds(0, 15)], f_buf.at[pl.ds(0, 15)], r_send).wait()


def local(orbitals, gaps, times, cos_weights):
    factors, columns, points = wave_tables()
    stay = lambda value: pltpu.with_memory_space_constraint(value, pltpu.HBM)
    dma = pltpu.SemaphoreType.DMA
    out = pl.pallas_call(
        kernel,
        out_shape=jax.ShapeDtypeStruct((27, 1, NG), F32),
        in_specs=[pl.BlockSpec(memory_space=pltpu.HBM)] * 7,
        out_specs=pl.BlockSpec(memory_space=pl.ANY),
        scratch_shapes=[
            pltpu.VMEM((27, 1, NG), F32),
            pltpu.VMEM((NOCC + NEMP,), F32),
            pltpu.SMEM((1,), F32),
            pltpu.VMEM((8, 8), F32),
            pltpu.VMEM((4, 1024), jnp.int32),
            pltpu.VMEM((1, 512), jnp.int32),
            pltpu.VMEM((320, 432), BF16),
            pltpu.VMEM((104, 1024), F32),
            pltpu.VMEM((40, 8, 512), BF16),
            pltpu.VMEM((32, 2, 8, 512), BF16),
            pltpu.VMEM((8, 128), F32),
            pltpu.VMEM((8, 8, 128), F32),
            pltpu.VMEM((144, 1024), F32),
            pltpu.VMEM((144, 1024), F32),
            pltpu.VMEM((8, 256, 1024), BF16),
            pltpu.VMEM((2, 1024, 1024), BF16),
            pltpu.VMEM((64, 512), F32),
            pltpu.VMEM((128, 512), F32),
            pltpu.VMEM((4, 2, 32, 256), BF16),
            pltpu.VMEM((4, 2, 32, 256), BF16),
            pltpu.VMEM((16, 2, 32, 256), BF16),
            pltpu.VMEM((16, 2, 32, 256), BF16),
            pltpu.VMEM((256, 1024), F32),
            pltpu.VMEM((8, 1024), F32),
            pltpu.VMEM((8, 128, 256), F32),
            pltpu.VMEM((8, 256, 256), F32),
            pltpu.VMEM((8, 128, 256), BF16),
            pltpu.VMEM((8, 128, 256), BF16),
            pltpu.VMEM((32, 32, 256), BF16),
            pltpu.VMEM((16, 32, 256), BF16),
            pltpu.VMEM((16, 32, 256), BF16),
            pltpu.VMEM((16, 32, 256), BF16),
            dma((8,)), dma, dma, dma, dma, dma, dma,
            dma((16, 2)), dma, dma,
            dma((3,)),
            dma((4,)), dma,
            dma((16,)), dma,
            dma, dma,
        ],
        compiler_params=pltpu.CompilerParams(has_side_effects=True, collective_id=0, vmem_limit_bytes=34 * 2**20),
    )(
        stay(orbitals.T), stay(gaps), times, stay(cos_weights),
        stay(jnp.asarray(factors)), stay(jnp.asarray(columns)), stay(jnp.asarray(points)),
    )
    return out.transpose(1, 0, 2)


def solution(mesh):
    return jax.shard_map(
        local,
        mesh=mesh,
        in_specs=(P("space", None), P(), P("tm"), P()),
        out_specs=P("tm", "space", None),
        check_vma=False,
    )
```

```python
import math

import jax
import jax.numpy as jnp
import numpy as np
from jax import lax
from jax.experimental import pallas as pl
from jax.experimental.pallas import tpu as pltpu
from jax.sharding import PartitionSpec as P

SIDE = 24
NG = 864
NOCC = 64
NEMP = 256
MESH = pl.DeviceIdType.MESH
F32 = jnp.float32
BF16 = jnp.bfloat16


def wave_tables():
    pos = np.arange(1024)
    group, m = pos // 128, pos % 128
    even = group < 4
    c_even = np.where(even, group % 2, (group - 4) // 2)
    trig = np.where(even, m // 54, group % 2)
    c = 1 + 2 * np.where(even, m // 18 % 3, m // 36) + c_even
    b = np.where(even, m // 3, m // 6) % 6 - 3
    a = np.where(even, 4 * (m % 3) - 4 - 2 * (group // 2), 2 * (m % 6) - 5)
    valid = m < 108
    natural = np.where(valid, (a + 6) + 12 * (b + 3) + 72 * (c - 1) + 432 * trig, -1)

    def factor(side, wave):
        step = np.mod(side[:, None] * wave[None, :], SIDE)
        angle = step * (2.0 * math.pi / SIDE)
        return np.cos(angle), np.sin(angle)

    x_cos, x_sin = factor(np.arange(8), a)
    y_cos, y_sin = factor(np.arange(24), b)
    y_first = np.where(trig == 0, y_cos, y_sin)
    y_second = np.where(trig == 0, y_sin, -y_cos)
    z_rows = np.concatenate([np.arange(8), np.tile(np.arange(8, 12), 2)])
    z_cos, z_sin = factor(z_rows, c)
    scaling = math.sqrt(2.0 / SIDE**3) * valid
    turn = np.where(a % 4 == 1, 1.0, -1.0) * np.ones((8, 1))
    factors = np.concatenate(
        [x_cos, x_sin, y_first, y_second, z_cos * scaling, z_sin * scaling, turn], axis=0
    ).astype(np.float32)

    where_natural = np.full(1024, -1, np.int32)
    where_natural[natural[valid]] = pos[valid]
    lane = np.arange(1024)
    block, core, low, row = lane // 256, lane // 128 % 2, lane // 32 % 4, lane % 32
    g = 27 * (low * 8 + block * 2 + core) + row
    where_g = np.where(row < 27, where_natural[np.minimum(g, NG - 1)], -1)
    offsets = np.repeat(np.array(OFFSETS), 64, axis=0).T
    columns = np.stack([where_g, where_natural, offsets[0], offsets[1]]).astype(np.int32)

    k = np.arange(256)
    tail = k - 144
    u = np.where(k < 144, k // 8, tail // 8 * 2 + tail % 8 // 4)
    z = np.where(k < 144, k % 8, 8 + tail % 4)
    inside = k < 216
    first = np.where(inside, u * 24 + z, -1)
    second = np.where(inside, u * 24 + 12 + z, -1)
    points = np.concatenate([first, second])[None, :].astype(np.int32)
    return factors, columns, points


OFFSETS = (
    (0, 0), (0, 1), (0, 3), (1, 0), (3, 0), (1, 1), (3, 3), (1, 3),
    (3, 1), (0, 2), (2, 0), (1, 2), (2, 1), (3, 2), (2, 3), (2, 2),
)
SLOT = {offset: n for n, offset in enumerate(OFFSETS)}
MIRROR = [SLOT[dy, dx] for dx, dy in OFFSETS]
FX, FXS, FY, FYS, FZ, FZS, FT = 0, 8, 16, 40, 64, 80, 96


def kernel(
    orb_hbm, gaps_hbm, times_hbm, cw_hbm, fac_hbm, col_hbm, pts_hbm, out_any,
    out_ref, gaps_ref, times_ref, cw_ref, col_ref, pts_ref, orb_ref, fac_ref,
    orb_p, recv, t_own, t_all, lead, quad, table, sel, acc, acc_odd, m_g, m_h, g_all, h_all,
    g_t, dmat, both, keep, c_send, c_recv, q_buf, s_buf, f_buf, r_buf,
    a_recv, a_send, e_send, t_recv, t_send, u_recv, u_send, b_recv, g_send, h_send, l_sem, x_recv, x_send, s_recv, s_send, r_recv, r_send,
):
    tm = lax.axis_index("tm")
    sp = lax.axis_index("space")
    x, zh = tm // 2, tm % 2
    zl, y, core = sp // 8, sp // 2 % 4, sp % 2
    z = zh * 4 + zl

    def device(xx, yy, zz, cc):
        return (xx * 2 + zz // 4, (zz % 4) * 8 + yy * 2 + cc)

    def remote(src, dst, send, recv_sem, target):
        return pltpu.make_async_remote_copy(
            src_ref=src, dst_ref=dst, send_sem=send, recv_sem=recv_sem,
            device_id=target, device_id_type=MESH,
        )

    load_orb = pltpu.make_async_copy(orb_hbm, orb_ref, l_sem.at[0])
    load_pts = pltpu.make_async_copy(pts_hbm, pts_ref, l_sem.at[1])
    load_orb.start()
    load_pts.start()
    loads = [
        pltpu.make_async_copy(src, dst, l_sem.at[2])
        for n, (src, dst) in enumerate((
            (fac_hbm, fac_ref), (col_hbm, col_ref), (gaps_hbm, gaps_ref), (cw_hbm, cw_ref), (times_hbm, times_ref),
        ))
    ]
    for load in loads:
        load.start()

    barrier = pltpu.get_barrier_semaphore()

    def greet(target):
        pl.semaphore_signal(barrier, inc=1, device_id=target, device_id_type=MESH)

    far = (z + 6 + 4 * core) % 8
    greet(device(x, y, (z + 4) % 8, core))
    for dy in (2, 1, 3, 0):
        for cc in range(2):
            greet(device(x, (y + dy) % 4, far, cc))
    for dy in (2, 1, 3, 0):
        for cc in range(2):
            greet(device(x, (y + dy) % 4, (z + 1) % 8, cc))
            greet(device(x, (y + dy) % 4, (z + 7) % 8, cc))
    for dy in (2, 1, 3, 0):
        if dy > 0:
            greet(device(x, (y + dy) % 4, z, core))
        greet(device(x, (y + dy) % 4, z, 1 - core))
    for dx in range(1, 4):
        greet(device((x + dx) % 4, y, z, core))

    load_pts.wait()
    pick = lax.broadcasted_iota(jnp.int32, (432, 512), 0) == pts_ref[...]
    pick = jnp.where(pick, 1.0, 0.0).astype(BF16)
    load_orb.wait()
    moved = jnp.dot(orb_ref[...], pick, preferred_element_type=F32).astype(BF16)
    for n in range(40):
        orb_p[n] = moved[n * 8 : (n + 1) * 8, :]

    pl.semaphore_wait(barrier, 35)
    links = ((2, 0), (-2, 1), (1, 0), (-1, 1), (1, 1), (-1, 0), (0, 0), (0, 1))
    for dy, (dz, cc) in [(dy, link) for pair in ((1, 3), (2, 0)) for link in links for dy in pair]:
        yy, zz = (y + dy) % 4, (z + dz + 8) % 8
        blocks = (4 * cc + x, 8 + 4 * zz + yy)
        for part, block in enumerate(blocks):
            src, dst = orb_p.at[block], recv.at[sp, part]
            copy = remote(src, dst, a_send, a_recv.at[sp % 8], device(x, yy, zz, cc))
            local = pltpu.make_async_copy(src, dst, a_recv.at[sp % 8])
            if dz == 0 and dy == 0:
                pl.when(core == cc)(local.start)
                if part == 0:
                    pl.when(core != cc)(copy.start)
            elif part == 0:
                copy.start()
            else:
                pl.when(core == cc)(copy.start)
    for load in loads:
        load.wait()
    t_own[...] = jnp.full((8, 128), times_ref[0], F32)
    for dx in range(1, 4):
        remote(t_own, t_all.at[zh * 4 + x], t_send, t_recv, device((x + dx) % 4, y, z, core)).start()
    t_all[zh * 4 + x] = t_own[...]

    def lead_rows(xx, carry):
        cos = fac_ref[pl.ds(FX + xx, 1), :]
        sin = fac_ref[pl.ds(FXS + xx, 1), :]
        first, second = fac_ref[FY : FY + 24, :], fac_ref[FYS : FYS + 24, :]
        rows = pl.ds(pl.multiple_of(xx * 24, 8), 24)
        lead[rows, :] = cos * first - sin * second
        quad[rows, :] = sin * first + cos * second
        return carry

    lax.fori_loop(0, 6, lead_rows, 0)
    odd = lax.broadcasted_iota(jnp.int32, (8, 1024), 0) >= 4

    def table_rows(chunk, carry):
        base = chunk * 18

        def pair(v, inner):
            row = base + 2 * v
            a0, a1 = lead[pl.ds(row, 1), :], lead[pl.ds(row + 1, 1), :]
            b0, b1 = quad[pl.ds(row, 1), :], quad[pl.ds(row + 1, 1), :]
            cos, sin = fac_ref[FZ : FZ + 8, :], fac_ref[FZS : FZS + 8, :]
            both = jnp.concatenate([a0 * cos - b0 * sin, a1 * cos - b1 * sin], axis=0)
            table[chunk, pl.ds(pl.multiple_of(v * 16, 16), 16), :] = both.astype(BF16)
            return inner

        lax.fori_loop(0, 9, pair, 0)

        def tail(v):
            row = base + 2 * v
            a = jnp.where(odd, lead[pl.ds(row + 1, 1), :], lead[pl.ds(row, 1), :])
            b = jnp.where(odd, quad[pl.ds(row + 1, 1), :], quad[pl.ds(row, 1), :])
            return a * fac_ref[FZ + 8 : FZ + 16, :] - b * fac_ref[FZS + 8 : FZS + 16, :]

        def tails(w, inner):
            both = jnp.concatenate([tail(2 * w), tail(jnp.minimum(2 * w + 1, 8))], axis=0)
            table[chunk, pl.ds(pl.multiple_of(144 + w * 16, 16), 16), :] = both.astype(BF16)
            return inner

        lax.fori_loop(0, 5, tails, 0)
        table[chunk, 224:256, :] = jnp.zeros((32, 1024), BF16)
        return carry

    lax.fori_loop(0, 8, table_rows, 0)

    def select_rows(n, carry):
        rows = lax.broadcasted_iota(jnp.int32, (128, 1024), 0) + n * 128
        for side in range(2):
            hit = rows == col_ref[side : side + 1, :]
            sel[side, pl.ds(pl.multiple_of(n * 128, 128), 128), :] = jnp.where(hit, 1.0, 0.0).astype(BF16)
        return carry

    lax.fori_loop(0, 8, select_rows, 0)

    pltpu.make_async_copy(t_all.at[pl.ds(0, 3)], t_all.at[pl.ds(0, 3)], t_recv).wait()
    half_times = t_all.at[pl.ds(zh * 4, 4)]
    remote(half_times, half_times, u_send, u_recv, device(x, y, (z + 4) % 8, core)).start()

    acc[...] = jnp.zeros_like(acc)
    acc_odd[...] = jnp.zeros_like(acc_odd)

    def chunk_step(step, carry):
        turn = step // 4 * 2 + step % 2
        away = jnp.where(turn < 2, 2 * turn + 1, 6 - 2 * turn)
        passed = step // 2 % 2
        n = (y + away) % 4 * 2 + (core + passed) % 2
        pltpu.make_async_copy(recv.at[pl.ds(0, 4)], recv.at[pl.ds(0, 4)], a_recv.at[n]).wait()
        for quarter in range(4):
            block = recv.at[n + 8 * quarter, 1]
            pl.when(passed == 0)(remote(block, block, e_send, a_recv.at[n], device(x, y, z, 1 - core)).start)
        occupied = [recv[n + 8 * quarter, 0].astype(F32) for quarter in range(4)]
        empty = [recv[n + 8 * quarter, 1].astype(F32) for quarter in range(4)]
        minus, plus = ([], [], [], []), ([], [], [], [])
        for i in range(8):
            p = [o[i : i + 1, :] * e for o, e in zip(occupied, empty)]
            s0, s1, d0, d1 = p[0] + p[2], p[1] + p[3], p[0] - p[2], p[1] - p[3]
            for kind, value in enumerate((s0 + s1, s0 - s1, d0, d1)):
                minus[kind].append(value[:, :256] - value[:, 256:])
                plus[kind].append(value[:, :256] + value[:, 256:])

        def product(rows, start, width):
            left = jnp.concatenate(rows, axis=0).astype(BF16)
            return jnp.dot(left, table[n, :, start : start + width], preferred_element_type=F32)

        acc[:, 0:128] += product(minus[0], 0, 128)
        acc[:, 128:256] += product(plus[0], 128, 128)
        acc[:, 256:384] += product(minus[1], 256, 128)
        acc[:, 384:512] += product(plus[1], 384, 128)
        acc_odd[:, 0:256] += product(minus[2] + minus[3], 512, 256)
        acc_odd[:, 256:512] += product(plus[2] + plus[3], 768, 256)
        return carry

    lax.fori_loop(0, 8, chunk_step, 0)
    columns = [acc[...]]
    for part in range(2):
        at = part * 256
        sign = fac_ref[FT : FT + 1, 512 + at : 640 + at]
        u_cos, u_sin = acc_odd[0:64, at : at + 128], acc_odd[0:64, at + 128 : at + 256]
        v_cos, v_sin = acc_odd[64:128, at : at + 128], acc_odd[64:128, at + 128 : at + 256]
        columns += [u_cos - sign * v_sin, u_sin + sign * v_cos]
    m_all = jnp.concatenate(columns, axis=1).astype(BF16)
    for n in range(4):
        lanes = slice(n * 256, (n + 1) * 256)
        m_g[n] = jnp.dot(m_all, sel[0, :, lanes], preferred_element_type=F32).astype(BF16).reshape(2, 32, 256)
        m_h[n] = jnp.dot(m_all, sel[1, :, lanes], preferred_element_type=F32).astype(BF16).reshape(2, 32, 256)

    def send_g(src, to, dx, dy, half):
        target = device((x + dx) % 4, (y + dy) % 4, z, core)
        remote(src.at[half], g_all.at[to, half], g_send, b_recv.at[to, half], target).start()

    def send_h(src, to, dx, dy, half):
        target = device((x + dx) % 4, (y + dy) % 4, z, core)
        remote(src.at[half], h_all.at[to, half], h_send, b_recv.at[MIRROR[to], half], target).start()

    for half in range(2):
        for d in (2, 1, 3):
            send_g(m_g.at[(y + d) % 4], SLOT[0, 4 - d], 0, d, half)
            send_h(m_h.at[(x + d) % 4], SLOT[4 - d, 0], d, 0, half)
    for half in range(2):
        for d in (1, 3, 2):
            send_g(m_g.at[y], SLOT[4 - d, 0], d, 0, half)
            send_h(m_h.at[x], SLOT[0, 4 - d], 0, d, half)
    for half in range(2):
        pltpu.make_async_copy(m_g.at[y, half], g_all.at[0, half], b_recv.at[0, half]).start()
        pltpu.make_async_copy(m_h.at[x, half], h_all.at[0, half], b_recv.at[0, half]).start()

    pltpu.make_async_copy(half_times, half_times, u_recv).wait()
    pair_index = lax.broadcasted_iota(jnp.int32, (1, 1024), 1)
    which_i = 32 * core + 8 * ((col_ref[2:3, :] + x) % 4) + pair_index // 8 % 8
    which_a = NOCC + 32 * z + 8 * ((col_ref[3:4, :] + y) % 4) + pair_index % 8
    orbital = lax.broadcasted_iota(jnp.int32, (320, 1024), 0)
    hot_i = jnp.where(orbital == which_i, 1.0, 0.0).astype(F32)
    hot_a = jnp.where(orbital == which_a, 1.0, 0.0).astype(F32)
    gaps = jnp.broadcast_to(gaps_ref[...].reshape(1, 320), (8, 320))
    high = lax.Precision.HIGHEST
    gap_i = jnp.dot(gaps, hot_i, precision=high, preferred_element_type=F32)
    gap_a = jnp.dot(gaps, hot_a, precision=high, preferred_element_type=F32)
    sub = lax.broadcasted_iota(jnp.int32, (8, 128), 0)
    tcol = jnp.zeros((8, 128), F32)
    for n in range(8):
        tcol = jnp.where(sub == n, t_all[n % 2 * 4 + n // 2], tcol)
    tcol = tcol[:, 0:1]
    decay = jnp.exp(-gap_i * tcol) * jnp.exp(-gap_a * tcol) * (NOCC**-0.5 * NEMP**-0.5)
    dmat[...] = jnp.dot(cw_ref[...], decay, precision=high, preferred_element_type=F32)

    def got(dx, dy, half):
        pltpu.make_async_copy(g_all.at[0], g_all.at[0], b_recv.at[SLOT[dx, dy], half]).wait()

    def relay(d, half):
        up_g, up_h = (y + d) % 4 < 2, (x + d) % 4 < 2
        got(3, d, half)
        pl.when(up_g)(lambda: send_g(g_all.at[SLOT[3, d]], SLOT[2, d], 1, 0, half))
        pl.when(up_h)(lambda: send_h(h_all.at[SLOT[d, 3]], SLOT[d, 2], 0, 1, half))
        got(1, d, half)
        pl.when(jnp.logical_not(up_g))(lambda: send_g(g_all.at[SLOT[1, d]], SLOT[2, d], 3, 0, half))
        pl.when(jnp.logical_not(up_h))(lambda: send_h(h_all.at[SLOT[d, 1]], SLOT[d, 2], 0, 3, half))

    for d, half in ((1, 0), (3, 0), (2, 0), (1, 1), (3, 1), (2, 1)):
        got(0, d, half)
        send_g(g_all.at[SLOT[0, d]], SLOT[3, d], 1, 0, half)
        send_g(g_all.at[SLOT[0, d]], SLOT[1, d], 3, 0, half)
        send_h(h_all.at[SLOT[d, 0]], SLOT[d, 3], 0, 1, half)
        send_h(h_all.at[SLOT[d, 0]], SLOT[d, 1], 0, 3, half)
    for d in (1, 3, 2):
        for half in range(2):
            relay(d, half)
    for d in (0, 1, 3):
        for half in range(2):
            got(d, 0, half)

    def turn_g(start):
        for n in range(start, start + 4):
            block = g_all[2 * n : 2 * n + 2].reshape(128, 256).astype(F32)
            g_t[:, n * 128 : (n + 1) * 128] = block.T

    turn_g(0)
    h_early = h_all[0:8].reshape(512, 256)

    def early(w, carry):
        left = (g_t[:, 0:512] * dmat[pl.ds(w, 1), 0:512]).astype(BF16)
        keep[w] = jnp.dot(left, h_early, preferred_element_type=F32)
        return carry

    lax.fori_loop(0, 8, early, 0)
    for d in range(4):
        for half in range(2):
            got(2, d, half)
    turn_g(4)
    sibling = device(x, y, z, 1 - core)
    mine = pl.ds(pl.multiple_of(core * 128, 128), 128)
    other = pl.ds(pl.multiple_of((1 - core) * 128, 128), 128)

    side = 2 * ((z + core) % 2) - 1
    partner = device(x, y, (z - side + 8) % 8, core)

    h_late = h_all[8:16].reshape(512, 256)

    def late(w, rows):
        left = [g_t[rows, 512:1024] * dmat[pl.ds(w + n, 1), 512:1024] for n in range(2)]
        left = jnp.concatenate(left, axis=0).astype(BF16)
        return jnp.dot(left, h_late, preferred_element_type=F32)

    def pair_of(n):
        return (x + jnp.where(n == 0, 1, jnp.where(n == 1, 3, jnp.where(n == 2, 2, 0)))) % 4

    def for_sibling(n, carry):
        first = 2 * pair_of(n)
        total = late(first, other)
        for m in range(2):
            w = first + m
            c_send[w] = (keep[w, other, :] + total[m * 128 : (m + 1) * 128, :]).astype(BF16)
            remote(c_send.at[w], c_recv.at[w], x_send, x_recv.at[n], sibling).start()
        return carry

    def either(action):
        pl.when(x < 3)(lambda: action(slice(0, 256)))
        pl.when(x == 3)(lambda: action(slice(0, 128)))

    def both_cores(n, carry):
        first = 2 * pair_of(n)
        rest = late(first, mine)
        for m in range(2):
            w = first + m
            if m == 0:
                two = c_recv.at[pl.ds(0, 2)]
                pltpu.make_async_copy(two, two, x_recv.at[n]).wait()
            total = keep[w, mine, :] + rest[m * 128 : (m + 1) * 128, :] + c_recv[w].astype(F32)
            both[w] = total
            for low in range(4):
                q_buf[w * 4 + low] = total[low * 32 : (low + 1) * 32, :].astype(BF16)
            for step in range(4, 8):
                owner = (z + side * step + 8) % 8
                there = w // 2 * 4 + 7 - step
                src, dst = q_buf.at[w * 4 + owner % 4], s_buf.at[there]

                def exchange():
                    either(lambda lanes: remote(
                        src.at[:, lanes], dst.at[:, lanes], s_send, s_recv.at[there], partner
                    ).start())

                pl.when(owner // 4 == m)(exchange)
        return carry

    lax.fori_loop(0, 4, for_sibling, 0)
    lax.fori_loop(0, 4, both_cores, 0)
    slot = (z + core) // 2 % 4 * 4 + x

    def deliver(n, carry):
        w = 2 * pair_of(n // 2) + n % 2
        for step in (3, 2, 1, 0):
            owner = (z + side * step + 8) % 8
            low, here = owner % 4, w // 2 * 4 + step

            def send():
                held = s_buf.at[here]
                either(lambda lanes: pltpu.make_async_copy(held.at[:, lanes], held.at[:, lanes], s_recv.at[here]).wait())
                rows = pl.ds(pl.multiple_of(low * 32, 32), 32)
                f_buf[here] = (both[w, rows, :] + s_buf[here].astype(F32)).astype(BF16)
                own_block = jnp.logical_and(w == tm, step == 0)
                src, dst = f_buf.at[here], r_buf.at[slot]

                def pass_on():
                    either(lambda lanes: remote(
                        src.at[:, lanes], dst.at[:, lanes], r_send, r_recv, (w, low * 8 + y * 2 + core)
                    ).start())

                def take():
                    either(lambda lanes: pltpu.make_async_copy(src.at[:, lanes], dst.at[:, lanes], r_recv).start())

                pl.when(own_block)(take)
                pl.when(jnp.logical_not(own_block))(pass_on)

            pl.when(owner // 4 == n % 2)(send)
        return carry

    lax.fori_loop(0, 8, deliver, 0)
    pltpu.make_async_copy(r_buf.at[pl.ds(0, 14)], r_buf.at[pl.ds(0, 14)], r_recv).wait()
    for n in range(4):
        total = r_buf[n].astype(F32)
        for m in range(1, 4):
            total += r_buf[m * 4 + n].astype(F32)
        width = 256 if n < 3 else 96
        out_ref[:, 0, n * 256 : n * 256 + width] = total[:27, :width]

    final = pltpu.make_async_copy(out_ref, out_any, l_sem.at[0])
    final.start()

    pltpu.make_async_copy(recv.at[pl.ds(0, 23)], recv.at[pl.ds(0, 23)], a_send).wait()
    pltpu.make_async_copy(recv.at[pl.ds(0, 8)], recv.at[pl.ds(0, 8)], e_send).wait()
    pltpu.make_async_copy(t_all.at[pl.ds(0, 3)], t_all.at[pl.ds(0, 3)], t_send).wait()
    pltpu.make_async_copy(half_times, half_times, u_send).wait()
    pltpu.make_async_copy(g_all.at[pl.ds(0, 15)], g_all.at[pl.ds(0, 15)], g_send).wait()
    pltpu.make_async_copy(h_all.at[pl.ds(0, 15)], h_all.at[pl.ds(0, 15)], h_send).wait()
    pltpu.make_async_copy(c_send, c_send, x_send).wait()
    either(lambda lanes: pltpu.make_async_copy(s_buf.at[:, :, lanes], s_buf.at[:, :, lanes], s_send).wait())
    final.wait()
    sent = f_buf.at[pl.ds(0, 15)]
    either(lambda lanes: pltpu.make_async_copy(sent.at[:, :, lanes], sent.at[:, :, lanes], r_send).wait())


def local(orbitals, gaps, times, cos_weights):
    factors, columns, points = wave_tables()
    stay = lambda value: pltpu.with_memory_space_constraint(value, pltpu.HBM)
    dma = pltpu.SemaphoreType.DMA
    out = pl.pallas_call(
        kernel,
        out_shape=jax.ShapeDtypeStruct((27, 1, NG), F32),
        in_specs=[pl.BlockSpec(memory_space=pltpu.HBM)] * 7,
        out_specs=pl.BlockSpec(memory_space=pl.ANY),
        scratch_shapes=[
            pltpu.VMEM((27, 1, NG), F32),
            pltpu.VMEM((NOCC + NEMP,), F32),
            pltpu.SMEM((1,), F32),
            pltpu.VMEM((8, 8), F32),
            pltpu.VMEM((4, 1024), jnp.int32),
            pltpu.VMEM((1, 512), jnp.int32),
            pltpu.VMEM((320, 432), BF16),
            pltpu.VMEM((104, 1024), F32),
            pltpu.VMEM((40, 8, 512), BF16),
            pltpu.VMEM((32, 2, 8, 512), BF16),
            pltpu.VMEM((8, 128), F32),
            pltpu.VMEM((8, 8, 128), F32),
            pltpu.VMEM((144, 1024), F32),
            pltpu.VMEM((144, 1024), F32),
            pltpu.VMEM((8, 256, 1024), BF16),
            pltpu.VMEM((2, 1024, 1024), BF16),
            pltpu.VMEM((64, 512), F32),
            pltpu.VMEM((128, 512), F32),
            pltpu.VMEM((4, 2, 32, 256), BF16),
            pltpu.VMEM((4, 2, 32, 256), BF16),
            pltpu.VMEM((16, 2, 32, 256), BF16),
            pltpu.VMEM((16, 2, 32, 256), BF16),
            pltpu.VMEM((256, 1024), F32),
            pltpu.VMEM((8, 1024), F32),
            pltpu.VMEM((8, 128, 256), F32),
            pltpu.VMEM((8, 256, 256), F32),
            pltpu.VMEM((8, 128, 256), BF16),
            pltpu.VMEM((8, 128, 256), BF16),
            pltpu.VMEM((32, 32, 256), BF16),
            pltpu.VMEM((16, 32, 256), BF16),
            pltpu.VMEM((16, 32, 256), BF16),
            pltpu.VMEM((16, 32, 256), BF16),
            dma((8,)), dma, dma, dma, dma, dma, dma,
            dma((16, 2)), dma, dma,
            dma((3,)),
            dma((4,)), dma,
            dma((16,)), dma,
            dma, dma,
        ],
        compiler_params=pltpu.CompilerParams(has_side_effects=True, collective_id=0, vmem_limit_bytes=34 * 2**20),
    )(
        stay(orbitals.T), stay(gaps), times, stay(cos_weights),
        stay(jnp.asarray(factors)), stay(jnp.asarray(columns)), stay(jnp.asarray(points)),
    )
    return out.transpose(1, 0, 2)


def solution(mesh):
    return jax.shard_map(
        local,
        mesh=mesh,
        in_specs=(P("space", None), P(), P("tm"), P()),
        out_specs=P("tm", "space", None),
        check_vma=False,
    )
```

```python
import math

import jax
import jax.numpy as jnp
import numpy as np
from jax import lax
from jax.experimental import pallas as pl
from jax.experimental.pallas import tpu as pltpu
from jax.sharding import PartitionSpec as P

SIDE = 24
NG = 864
NOCC = 64
NEMP = 256
MESH = pl.DeviceIdType.MESH
F32 = jnp.float32
BF16 = jnp.bfloat16


def wave_tables():
    pos = np.arange(1024)
    group, m = pos // 128, pos % 128
    even = group < 4
    c_even = np.where(even, group % 2, (group - 4) // 2)
    trig = np.where(even, m // 54, group % 2)
    c = 1 + 2 * np.where(even, m // 18 % 3, m // 36) + c_even
    b = np.where(even, m // 3, m // 6) % 6 - 3
    a = np.where(even, 4 * (m % 3) - 4 - 2 * (group // 2), 2 * (m % 6) - 5)
    valid = m < 108
    natural = np.where(valid, (a + 6) + 12 * (b + 3) + 72 * (c - 1) + 432 * trig, -1)

    def factor(side, wave):
        step = np.mod(side[:, None] * wave[None, :], SIDE)
        angle = step * (2.0 * math.pi / SIDE)
        return np.cos(angle), np.sin(angle)

    x_cos, x_sin = factor(np.arange(8), a)
    y_cos, y_sin = factor(np.arange(24), b)
    y_first = np.where(trig == 0, y_cos, y_sin)
    y_second = np.where(trig == 0, y_sin, -y_cos)
    z_rows = np.concatenate([np.arange(8), np.tile(np.arange(8, 12), 2)])
    z_cos, z_sin = factor(z_rows, c)
    scaling = math.sqrt(2.0 / SIDE**3) * valid
    turn = np.where(a % 4 == 1, 1.0, -1.0) * np.ones((8, 1))
    factors = np.concatenate(
        [x_cos, x_sin, y_first, y_second, z_cos * scaling, z_sin * scaling, turn], axis=0
    ).astype(np.float32)

    where_natural = np.full(1024, -1, np.int32)
    where_natural[natural[valid]] = pos[valid]
    lane = np.arange(1024)
    block, core, low, row = lane // 256, lane // 128 % 2, lane // 32 % 4, lane % 32
    g = 27 * (low * 8 + block * 2 + core) + row
    where_g = np.where(row < 27, where_natural[np.minimum(g, NG - 1)], -1)
    offsets = np.repeat(np.array(OFFSETS), 64, axis=0).T
    columns = np.stack([where_g, where_natural, offsets[0], offsets[1]]).astype(np.int32)

    k = np.arange(256)
    tail = k - 144
    u = np.where(k < 144, k // 8, tail // 8 * 2 + tail % 8 // 4)
    z = np.where(k < 144, k % 8, 8 + tail % 4)
    inside = k < 216
    first = np.where(inside, u * 24 + z, -1)
    second = np.where(inside, u * 24 + 12 + z, -1)
    points = np.concatenate([first, second])[None, :].astype(np.int32)
    return factors, columns, points


OFFSETS = (
    (0, 0), (0, 1), (0, 3), (1, 0), (3, 0), (1, 1), (3, 3), (1, 3),
    (3, 1), (0, 2), (2, 0), (1, 2), (2, 1), (3, 2), (2, 3), (2, 2),
)
SLOT = {offset: n for n, offset in enumerate(OFFSETS)}
MIRROR = [SLOT[dy, dx] for dx, dy in OFFSETS]
FX, FXS, FY, FYS, FZ, FZS, FT = 0, 8, 16, 40, 64, 80, 96


def kernel(
    orb_hbm, gaps_hbm, times_hbm, cw_hbm, fac_hbm, col_hbm, pts_hbm, out_ref,
    gaps_ref, times_ref, cw_ref, col_ref, pts_ref, orb_ref, fac_ref,
    orb_p, recv, t_own, t_all, lead, quad, table, sel, acc, acc_odd, m_g, m_h, g_all, h_all,
    g_t, dmat, both, keep, c_send, c_recv, q_buf, s_buf, f_buf, r_buf,
    a_recv, a_send, e_send, t_recv, t_send, u_recv, u_send, b_recv, g_send, h_send, l_sem, x_recv, x_send, s_recv, s_send, r_recv, r_send,
):
    tm = lax.axis_index("tm")
    sp = lax.axis_index("space")
    x, zh = tm // 2, tm % 2
    zl, y, core = sp // 8, sp // 2 % 4, sp % 2
    z = zh * 4 + zl

    def device(xx, yy, zz, cc):
        return (xx * 2 + zz // 4, (zz % 4) * 8 + yy * 2 + cc)

    def remote(src, dst, send, recv_sem, target):
        return pltpu.make_async_remote_copy(
            src_ref=src, dst_ref=dst, send_sem=send, recv_sem=recv_sem,
            device_id=target, device_id_type=MESH,
        )

    load_orb = pltpu.make_async_copy(orb_hbm, orb_ref, l_sem.at[0])
    load_pts = pltpu.make_async_copy(pts_hbm, pts_ref, l_sem.at[1])
    load_orb.start()
    load_pts.start()
    loads = [
        pltpu.make_async_copy(src, dst, l_sem.at[2])
        for n, (src, dst) in enumerate((
            (fac_hbm, fac_ref), (col_hbm, col_ref), (gaps_hbm, gaps_ref), (cw_hbm, cw_ref), (times_hbm, times_ref),
        ))
    ]
    for load in loads:
        load.start()

    barrier = pltpu.get_barrier_semaphore()

    def greet(target):
        pl.semaphore_signal(barrier, inc=1, device_id=target, device_id_type=MESH)

    far = (z + 6 + 4 * core) % 8
    greet(device(x, y, (z + 4) % 8, core))
    for dy in (2, 1, 3, 0):
        for cc in range(2):
            greet(device(x, (y + dy) % 4, far, cc))
    for dy in (2, 1, 3, 0):
        for cc in range(2):
            greet(device(x, (y + dy) % 4, (z + 1) % 8, cc))
            greet(device(x, (y + dy) % 4, (z + 7) % 8, cc))
    for dy in (2, 1, 3, 0):
        if dy > 0:
            greet(device(x, (y + dy) % 4, z, core))
        greet(device(x, (y + dy) % 4, z, 1 - core))
    for dx in range(1, 4):
        greet(device((x + dx) % 4, y, z, core))

    load_pts.wait()
    pick = lax.broadcasted_iota(jnp.int32, (432, 512), 0) == pts_ref[...]
    pick = jnp.where(pick, 1.0, 0.0).astype(BF16)
    load_orb.wait()
    moved = jnp.dot(orb_ref[...], pick, preferred_element_type=F32).astype(BF16)
    for n in range(40):
        orb_p[n] = moved[n * 8 : (n + 1) * 8, :]

    pl.semaphore_wait(barrier, 35)
    links = ((2, 0), (-2, 1), (1, 0), (-1, 1), (1, 1), (-1, 0), (0, 0), (0, 1))
    for dy, (dz, cc) in [(dy, link) for pair in ((1, 3), (2, 0)) for link in links for dy in pair]:
        yy, zz = (y + dy) % 4, (z + dz + 8) % 8
        blocks = (4 * cc + x, 8 + 4 * zz + yy)
        for part, block in enumerate(blocks):
            src, dst = orb_p.at[block], recv.at[sp, part]
            copy = remote(src, dst, a_send, a_recv.at[sp % 8], device(x, yy, zz, cc))
            local = pltpu.make_async_copy(src, dst, a_recv.at[sp % 8])
            if dz == 0 and dy == 0:
                pl.when(core == cc)(local.start)
                if part == 0:
                    pl.when(core != cc)(copy.start)
            elif part == 0:
                copy.start()
            else:
                pl.when(core == cc)(copy.start)
    for load in loads:
        load.wait()
    t_own[...] = jnp.full((8, 128), times_ref[0], F32)
    for dx in range(1, 4):
        remote(t_own, t_all.at[zh * 4 + x], t_send, t_recv, device((x + dx) % 4, y, z, core)).start()
    t_all[zh * 4 + x] = t_own[...]

    def lead_rows(xx, carry):
        cos = fac_ref[pl.ds(FX + xx, 1), :]
        sin = fac_ref[pl.ds(FXS + xx, 1), :]
        first, second = fac_ref[FY : FY + 24, :], fac_ref[FYS : FYS + 24, :]
        rows = pl.ds(pl.multiple_of(xx * 24, 8), 24)
        lead[rows, :] = cos * first - sin * second
        quad[rows, :] = sin * first + cos * second
        return carry

    lax.fori_loop(0, 6, lead_rows, 0)
    odd = lax.broadcasted_iota(jnp.int32, (8, 1024), 0) >= 4

    def table_rows(chunk, carry):
        base = chunk * 18

        def pair(v, inner):
            row = base + 2 * v
            a0, a1 = lead[pl.ds(row, 1), :], lead[pl.ds(row + 1, 1), :]
            b0, b1 = quad[pl.ds(row, 1), :], quad[pl.ds(row + 1, 1), :]
            cos, sin = fac_ref[FZ : FZ + 8, :], fac_ref[FZS : FZS + 8, :]
            both = jnp.concatenate([a0 * cos - b0 * sin, a1 * cos - b1 * sin], axis=0)
            table[chunk, pl.ds(pl.multiple_of(v * 16, 16), 16), :] = both.astype(BF16)
            return inner

        lax.fori_loop(0, 9, pair, 0)

        def tail(v):
            row = base + 2 * v
            a = jnp.where(odd, lead[pl.ds(row + 1, 1), :], lead[pl.ds(row, 1), :])
            b = jnp.where(odd, quad[pl.ds(row + 1, 1), :], quad[pl.ds(row, 1), :])
            return a * fac_ref[FZ + 8 : FZ + 16, :] - b * fac_ref[FZS + 8 : FZS + 16, :]

        def tails(w, inner):
            both = jnp.concatenate([tail(2 * w), tail(jnp.minimum(2 * w + 1, 8))], axis=0)
            table[chunk, pl.ds(pl.multiple_of(144 + w * 16, 16), 16), :] = both.astype(BF16)
            return inner

        lax.fori_loop(0, 5, tails, 0)
        table[chunk, 224:256, :] = jnp.zeros((32, 1024), BF16)
        return carry

    lax.fori_loop(0, 8, table_rows, 0)

    def select_rows(n, carry):
        rows = lax.broadcasted_iota(jnp.int32, (128, 1024), 0) + n * 128
        for side in range(2):
            hit = rows == col_ref[side : side + 1, :]
            sel[side, pl.ds(pl.multiple_of(n * 128, 128), 128), :] = jnp.where(hit, 1.0, 0.0).astype(BF16)
        return carry

    lax.fori_loop(0, 8, select_rows, 0)

    pltpu.make_async_copy(t_all.at[pl.ds(0, 3)], t_all.at[pl.ds(0, 3)], t_recv).wait()
    half_times = t_all.at[pl.ds(zh * 4, 4)]
    remote(half_times, half_times, u_send, u_recv, device(x, y, (z + 4) % 8, core)).start()

    acc[...] = jnp.zeros_like(acc)
    acc_odd[...] = jnp.zeros_like(acc_odd)

    def chunk_step(step, carry):
        turn = step // 4 * 2 + step % 2
        away = jnp.where(turn < 2, 2 * turn + 1, 6 - 2 * turn)
        passed = step // 2 % 2
        n = (y + away) % 4 * 2 + (core + passed) % 2
        pltpu.make_async_copy(recv.at[pl.ds(0, 4)], recv.at[pl.ds(0, 4)], a_recv.at[n]).wait()
        for quarter in range(4):
            block = recv.at[n + 8 * quarter, 1]
            pl.when(passed == 0)(remote(block, block, e_send, a_recv.at[n], device(x, y, z, 1 - core)).start)
        occupied = [recv[n + 8 * quarter, 0].astype(F32) for quarter in range(4)]
        empty = [recv[n + 8 * quarter, 1].astype(F32) for quarter in range(4)]
        minus, plus = ([], [], [], []), ([], [], [], [])
        for i in range(8):
            p = [o[i : i + 1, :] * e for o, e in zip(occupied, empty)]
            s0, s1, d0, d1 = p[0] + p[2], p[1] + p[3], p[0] - p[2], p[1] - p[3]
            for kind, value in enumerate((s0 + s1, s0 - s1, d0, d1)):
                minus[kind].append(value[:, :256] - value[:, 256:])
                plus[kind].append(value[:, :256] + value[:, 256:])

        def product(rows, start, width):
            left = jnp.concatenate(rows, axis=0).astype(BF16)
            return jnp.dot(left, table[n, :, start : start + width], preferred_element_type=F32)

        acc[:, 0:128] += product(minus[0], 0, 128)
        acc[:, 128:256] += product(plus[0], 128, 128)
        acc[:, 256:384] += product(minus[1], 256, 128)
        acc[:, 384:512] += product(plus[1], 384, 128)
        acc_odd[:, 0:256] += product(minus[2] + minus[3], 512, 256)
        acc_odd[:, 256:512] += product(plus[2] + plus[3], 768, 256)
        return carry

    lax.fori_loop(0, 8, chunk_step, 0)
    columns = [acc[...]]
    for part in range(2):
        at = part * 256
        sign = fac_ref[FT : FT + 1, 512 + at : 640 + at]
        u_cos, u_sin = acc_odd[0:64, at : at + 128], acc_odd[0:64, at + 128 : at + 256]
        v_cos, v_sin = acc_odd[64:128, at : at + 128], acc_odd[64:128, at + 128 : at + 256]
        columns += [u_cos - sign * v_sin, u_sin + sign * v_cos]
    m_all = jnp.concatenate(columns, axis=1).astype(BF16)
    for n in range(4):
        lanes = slice(n * 256, (n + 1) * 256)
        m_g[n] = jnp.dot(m_all, sel[0, :, lanes], preferred_element_type=F32).astype(BF16).reshape(2, 32, 256)
        m_h[n] = jnp.dot(m_all, sel[1, :, lanes], preferred_element_type=F32).astype(BF16).reshape(2, 32, 256)

    def send_g(src, to, dx, dy, half):
        target = device((x + dx) % 4, (y + dy) % 4, z, core)
        remote(src.at[half], g_all.at[to, half], g_send, b_recv.at[to, half], target).start()

    def send_h(src, to, dx, dy, half):
        target = device((x + dx) % 4, (y + dy) % 4, z, core)
        remote(src.at[half], h_all.at[to, half], h_send, b_recv.at[MIRROR[to], half], target).start()

    for half in range(2):
        for d in (2, 1, 3):
            send_g(m_g.at[(y + d) % 4], SLOT[0, 4 - d], 0, d, half)
            send_h(m_h.at[(x + d) % 4], SLOT[4 - d, 0], d, 0, half)
    for half in range(2):
        for d in (1, 3, 2):
            send_g(m_g.at[y], SLOT[4 - d, 0], d, 0, half)
            send_h(m_h.at[x], SLOT[0, 4 - d], 0, d, half)
    for half in range(2):
        pltpu.make_async_copy(m_g.at[y, half], g_all.at[0, half], b_recv.at[0, half]).start()
        pltpu.make_async_copy(m_h.at[x, half], h_all.at[0, half], b_recv.at[0, half]).start()

    pltpu.make_async_copy(half_times, half_times, u_recv).wait()
    pair_index = lax.broadcasted_iota(jnp.int32, (1, 1024), 1)
    which_i = 32 * core + 8 * ((col_ref[2:3, :] + x) % 4) + pair_index // 8 % 8
    which_a = NOCC + 32 * z + 8 * ((col_ref[3:4, :] + y) % 4) + pair_index % 8
    orbital = lax.broadcasted_iota(jnp.int32, (320, 1024), 0)
    hot_i = jnp.where(orbital == which_i, 1.0, 0.0).astype(F32)
    hot_a = jnp.where(orbital == which_a, 1.0, 0.0).astype(F32)
    gaps = jnp.broadcast_to(gaps_ref[...].reshape(1, 320), (8, 320))
    high = lax.Precision.HIGHEST
    gap_i = jnp.dot(gaps, hot_i, precision=high, preferred_element_type=F32)
    gap_a = jnp.dot(gaps, hot_a, precision=high, preferred_element_type=F32)
    sub = lax.broadcasted_iota(jnp.int32, (8, 128), 0)
    tcol = jnp.zeros((8, 128), F32)
    for n in range(8):
        tcol = jnp.where(sub == n, t_all[n % 2 * 4 + n // 2], tcol)
    tcol = tcol[:, 0:1]
    decay = jnp.exp(-gap_i * tcol) * jnp.exp(-gap_a * tcol) * (NOCC**-0.5 * NEMP**-0.5)
    dmat[...] = jnp.dot(cw_ref[...], decay, precision=high, preferred_element_type=F32)

    def got(dx, dy, half):
        pltpu.make_async_copy(g_all.at[0], g_all.at[0], b_recv.at[SLOT[dx, dy], half]).wait()

    def relay(d, half):
        up_g, up_h = (y + d) % 4 < 2, (x + d) % 4 < 2
        got(3, d, half)
        pl.when(up_g)(lambda: send_g(g_all.at[SLOT[3, d]], SLOT[2, d], 1, 0, half))
        pl.when(up_h)(lambda: send_h(h_all.at[SLOT[d, 3]], SLOT[d, 2], 0, 1, half))
        got(1, d, half)
        pl.when(jnp.logical_not(up_g))(lambda: send_g(g_all.at[SLOT[1, d]], SLOT[2, d], 3, 0, half))
        pl.when(jnp.logical_not(up_h))(lambda: send_h(h_all.at[SLOT[d, 1]], SLOT[d, 2], 0, 3, half))

    for d, half in ((1, 0), (3, 0), (2, 0), (1, 1), (3, 1), (2, 1)):
        got(0, d, half)
        send_g(g_all.at[SLOT[0, d]], SLOT[3, d], 1, 0, half)
        send_g(g_all.at[SLOT[0, d]], SLOT[1, d], 3, 0, half)
        send_h(h_all.at[SLOT[d, 0]], SLOT[d, 3], 0, 1, half)
        send_h(h_all.at[SLOT[d, 0]], SLOT[d, 1], 0, 3, half)
    for d in (1, 3, 2):
        for half in range(2):
            relay(d, half)
    for d in (0, 1, 3):
        for half in range(2):
            got(d, 0, half)

    def turn_g(start):
        for n in range(start, start + 4):
            block = g_all[2 * n : 2 * n + 2].reshape(128, 256).astype(F32)
            g_t[:, n * 128 : (n + 1) * 128] = block.T

    turn_g(0)
    h_early = h_all[0:8].reshape(512, 256)

    def early(w, carry):
        left = (g_t[:, 0:512] * dmat[pl.ds(w, 1), 0:512]).astype(BF16)
        keep[w] = jnp.dot(left, h_early, preferred_element_type=F32)
        return carry

    lax.fori_loop(0, 8, early, 0)
    for d in range(4):
        for half in range(2):
            got(2, d, half)
    turn_g(4)
    sibling = device(x, y, z, 1 - core)
    mine = pl.ds(pl.multiple_of(core * 128, 128), 128)
    other = pl.ds(pl.multiple_of((1 - core) * 128, 128), 128)

    side = 2 * ((z + core) % 2) - 1
    partner = device(x, y, (z - side + 8) % 8, core)

    h_late = h_all[8:16].reshape(512, 256)

    def late(w, rows):
        left = [g_t[rows, 512:1024] * dmat[pl.ds(w + n, 1), 512:1024] for n in range(2)]
        left = jnp.concatenate(left, axis=0).astype(BF16)
        return jnp.dot(left, h_late, preferred_element_type=F32)

    def pair_of(n):
        return (x + jnp.where(n == 0, 1, jnp.where(n == 1, 3, jnp.where(n == 2, 2, 0)))) % 4

    def for_sibling(n, carry):
        first = 2 * pair_of(n)
        total = late(first, other)
        for m in range(2):
            w = first + m
            c_send[w] = (keep[w, other, :] + total[m * 128 : (m + 1) * 128, :]).astype(BF16)
            remote(c_send.at[w], c_recv.at[w], x_send, x_recv.at[n], sibling).start()
        return carry

    def either(action):
        pl.when(x < 3)(lambda: action(slice(0, 256)))
        pl.when(x == 3)(lambda: action(slice(0, 128)))

    def both_cores(n, carry):
        first = 2 * pair_of(n)
        rest = late(first, mine)
        for m in range(2):
            w = first + m
            if m == 0:
                two = c_recv.at[pl.ds(0, 2)]
                pltpu.make_async_copy(two, two, x_recv.at[n]).wait()
            total = keep[w, mine, :] + rest[m * 128 : (m + 1) * 128, :] + c_recv[w].astype(F32)
            both[w] = total
            for low in range(4):
                q_buf[w * 4 + low] = total[low * 32 : (low + 1) * 32, :].astype(BF16)
            for step in range(4, 8):
                owner = (z + side * step + 8) % 8
                there = w // 2 * 4 + 7 - step
                src, dst = q_buf.at[w * 4 + owner % 4], s_buf.at[there]

                def exchange():
                    either(lambda lanes: remote(
                        src.at[:, lanes], dst.at[:, lanes], s_send, s_recv.at[there], partner
                    ).start())

                pl.when(owner // 4 == m)(exchange)
        return carry

    lax.fori_loop(0, 4, for_sibling, 0)
    lax.fori_loop(0, 4, both_cores, 0)
    slot = (z + core) // 2 % 4 * 4 + x

    def deliver(n, carry):
        w = 2 * pair_of(n // 2) + n % 2
        for step in (3, 2, 1, 0):
            owner = (z + side * step + 8) % 8
            low, here = owner % 4, w // 2 * 4 + step

            def send():
                held = s_buf.at[here]
                either(lambda lanes: pltpu.make_async_copy(held.at[:, lanes], held.at[:, lanes], s_recv.at[here]).wait())
                rows = pl.ds(pl.multiple_of(low * 32, 32), 32)
                f_buf[here] = (both[w, rows, :] + s_buf[here].astype(F32)).astype(BF16)
                own_block = jnp.logical_and(w == tm, step == 0)
                src, dst = f_buf.at[here], r_buf.at[slot]

                def pass_on():
                    either(lambda lanes: remote(
                        src.at[:, lanes], dst.at[:, lanes], r_send, r_recv, (w, low * 8 + y * 2 + core)
                    ).start())

                def take():
                    either(lambda lanes: pltpu.make_async_copy(src.at[:, lanes], dst.at[:, lanes], r_recv).start())

                pl.when(own_block)(take)
                pl.when(jnp.logical_not(own_block))(pass_on)

            pl.when(owner // 4 == n % 2)(send)
        return carry

    lax.fori_loop(0, 8, deliver, 0)
    pltpu.make_async_copy(r_buf.at[pl.ds(0, 14)], r_buf.at[pl.ds(0, 14)], r_recv).wait()
    for n in range(4):
        total = r_buf[n].astype(F32)
        for m in range(1, 4):
            total += r_buf[m * 4 + n].astype(F32)
        width = 256 if n < 3 else 96
        out_ref[:, 0, n * 256 : n * 256 + width] = total[:27, :width]

    pltpu.make_async_copy(recv.at[pl.ds(0, 23)], recv.at[pl.ds(0, 23)], a_send).wait()
    pltpu.make_async_copy(recv.at[pl.ds(0, 8)], recv.at[pl.ds(0, 8)], e_send).wait()
    pltpu.make_async_copy(t_all.at[pl.ds(0, 3)], t_all.at[pl.ds(0, 3)], t_send).wait()
    pltpu.make_async_copy(half_times, half_times, u_send).wait()
    pltpu.make_async_copy(g_all.at[pl.ds(0, 15)], g_all.at[pl.ds(0, 15)], g_send).wait()
    pltpu.make_async_copy(h_all.at[pl.ds(0, 15)], h_all.at[pl.ds(0, 15)], h_send).wait()
    pltpu.make_async_copy(c_send, c_send, x_send).wait()
    either(lambda lanes: pltpu.make_async_copy(s_buf.at[:, :, lanes], s_buf.at[:, :, lanes], s_send).wait())
    sent = f_buf.at[pl.ds(0, 15)]
    either(lambda lanes: pltpu.make_async_copy(sent.at[:, :, lanes], sent.at[:, :, lanes], r_send).wait())


def local(orbitals, gaps, times, cos_weights):
    factors, columns, points = wave_tables()
    stay = lambda value: pltpu.with_memory_space_constraint(value, pltpu.HBM)
    dma = pltpu.SemaphoreType.DMA
    out = pl.pallas_call(
        kernel,
        out_shape=jax.ShapeDtypeStruct((27, 1, NG), F32),
        in_specs=[pl.BlockSpec(memory_space=pltpu.HBM)] * 7,
        out_specs=pl.BlockSpec(memory_space=pltpu.VMEM),
        scratch_shapes=[
            pltpu.VMEM((NOCC + NEMP,), F32),
            pltpu.SMEM((1,), F32),
            pltpu.VMEM((8, 8), F32),
            pltpu.VMEM((4, 1024), jnp.int32),
            pltpu.VMEM((1, 512), jnp.int32),
            pltpu.VMEM((320, 432), BF16),
            pltpu.VMEM((104, 1024), F32),
            pltpu.VMEM((40, 8, 512), BF16),
            pltpu.VMEM((32, 2, 8, 512), BF16),
            pltpu.VMEM((8, 128), F32),
            pltpu.VMEM((8, 8, 128), F32),
            pltpu.VMEM((144, 1024), F32),
            pltpu.VMEM((144, 1024), F32),
            pltpu.VMEM((8, 256, 1024), BF16),
            pltpu.VMEM((2, 1024, 1024), BF16),
            pltpu.VMEM((64, 512), F32),
            pltpu.VMEM((128, 512), F32),
            pltpu.VMEM((4, 2, 32, 256), BF16),
            pltpu.VMEM((4, 2, 32, 256), BF16),
            pltpu.VMEM((16, 2, 32, 256), BF16),
            pltpu.VMEM((16, 2, 32, 256), BF16),
            pltpu.VMEM((256, 1024), F32),
            pltpu.VMEM((8, 1024), F32),
            pltpu.VMEM((8, 128, 256), F32),
            pltpu.VMEM((8, 256, 256), F32),
            pltpu.VMEM((8, 128, 256), BF16),
            pltpu.VMEM((8, 128, 256), BF16),
            pltpu.VMEM((32, 32, 256), BF16),
            pltpu.VMEM((16, 32, 256), BF16),
            pltpu.VMEM((16, 32, 256), BF16),
            pltpu.VMEM((16, 32, 256), BF16),
            dma((8,)), dma, dma, dma, dma, dma, dma,
            dma((16, 2)), dma, dma,
            dma((3,)),
            dma((4,)), dma,
            dma((16,)), dma,
            dma, dma,
        ],
        compiler_params=pltpu.CompilerParams(has_side_effects=True, collective_id=0, vmem_limit_bytes=34 * 2**20),
    )(
        stay(orbitals.T), stay(gaps), times, stay(cos_weights),
        stay(jnp.asarray(factors)), stay(jnp.asarray(columns)), stay(jnp.asarray(points)),
    )
    return out.transpose(1, 0, 2)


def solution(mesh):
    return jax.shard_map(
        local,
        mesh=mesh,
        in_specs=(P("space", None), P(), P("tm"), P()),
        out_specs=P("tm", "space", None),
        check_vma=False,
    )
```
